512 devices in a mesh: lat: 16 (over x, y_lo, core), lon: 32 (over y_hi, z).
Axes of the slice: x: 4, y: 4 (y_hi: 2, y_lo: 2; y = y_hi * 2 + y_lo), z: 16, core: 2. Of those that a mesh axis runs over, the one named last changes fastest.
Arguments:
- features: bfloat16 [64, 1024, 256], P('lat', 'lon'), may hold values from -6 to 6
- cotangent: bfloat16 [64, 1024, 256], P('lat', 'lon'), may hold values from -6 to 6
- weight: bfloat16 [4, 256, 256], replicated, may hold values from -0.1875 to 0.1875
- filter_taps: bfloat16 [64, 4, 5, 64], P('lat'), may hold values from -6 to 6
- lat_ext: int32 [64], P('lat'), may hold values from 1 to 3, as said below
- lon_count: int32 [64], P('lat'), may hold values from 1 to 32, as said below
Outputs:
- output: bfloat16 [64, 1024, 256], P('lat', 'lon')
- field_grad: bfloat16 [64, 1024, 256], P('lat', 'lon')
- weight_grad: float32 [4, 256, 256], replicated
The draws below stay inside these ranges and needn't reach their ends.
Inputs may be any that keep to these rules, and one draw needn't show every extreme that they name: `lat_ext`: a row uses the latitude offsets whose magnitude is below its entry. `lon_count`: a row uses the longitude offsets whose magnitude is below its entry.
All inputs are finite; a program needn't handle non-finite values.
Results may differ from the reference program's by a relative error of at most 0.006.
Values may be sent and summed in bfloat16 or wider, within the bound.
A program may use at most 64 MiB of HBM per device.

```python
import math
import jax
import jax.numpy as jnp
from jax import lax

C = 256
K = 4
HLAT = 2
LON_DEV = 32
NDL = 5
NLAT = 64
NLON = 1024


def draw_lat_ext(key, part):
    base_ext = jax.random.randint(key, (NLAT,), 1, HLAT + 2)
    full_row = jax.random.randint(jax.random.fold_in(key, 7), (), 0, NLAT)
    return jnp.where(jnp.arange(NLAT) == full_row, HLAT + 1, base_ext).astype(jnp.int32)


def draw_lon_count(key, part):
    row_ids = jnp.arange(NLAT, dtype=jnp.int32)
    distance = jnp.abs(2 * row_ids - (NLAT - 1))
    base_count = 1 + (LON_DEV - 1) * distance * distance // ((NLAT - 1) * (NLAT - 1))
    jitter = jax.random.randint(key, (NLAT,), 0, max(LON_DEV // 4, 2))
    return jnp.minimum(base_count + jitter, LON_DEV).astype(jnp.int32)


def levels(own_key, shape, split, least, largest):
    loudness = 1.0
    for dim, parts in split:
        steps = jax.random.uniform(jax.random.fold_in(jax.random.fold_in(own_key, 6), dim), (parts,), jnp.float32, least / len(split), largest / len(split))
        loudness = loudness * jnp.repeat(jnp.exp(steps), shape[dim] // parts).reshape((-1,) + (1,) * (len(shape) - 1 - dim))
    return loudness


def gaussian(stream_key, extent, deviation, limit, shards=(), kind=jnp.bfloat16):
    entries = deviation * jax.random.normal(stream_key, extent, jnp.float32)
    if shards:
        entries = entries * levels(stream_key, extent, shards, -0.22, 0.18)
    return jnp.clip(entries, -limit, limit).astype(kind)


def setup_inputs(seed: int = 0) -> dict:
    key_list = jax.random.split(jax.random.key(seed), 7)
    features = gaussian(key_list[0], (NLAT, NLON, C), 1.0, 6.0, ((0, 16), (1, 32)))
    cotangent = gaussian(key_list[1], (NLAT, NLON, C), 1.0, 6.0, ((0, 16), (1, 32)))
    weight = gaussian(key_list[2], (K, C, C), (K * C) ** -0.5, 0.1875)
    filter_taps = gaussian(key_list[3], (NLAT, K, NDL, 2 * LON_DEV), 1.0, 6.0, ((0, 16),))
    lat_ext = draw_lat_ext(jax.random.fold_in(key_list[6], 71), 0)
    lon_count = draw_lon_count(jax.random.fold_in(key_list[6], 71), 0)
    return dict(features=features, cotangent=cotangent, weight=weight, filter_taps=filter_taps, lat_ext=lat_ext, lon_count=lon_count)


def make_filters(filter_taps, lat_ext, lon_count):
    lat_reach = filter_taps.shape[2] // 2
    half_width = filter_taps.shape[3] // 2
    lat_dist = jnp.abs(jnp.arange(filter_taps.shape[2], dtype=jnp.int32) - lat_reach)
    lon_dist = jnp.abs(jnp.arange(filter_taps.shape[3], dtype=jnp.int32) - half_width)
    support = (lat_dist[None, :, None] < lat_ext[:, None, None]) & (lon_dist[None, None, :] < lon_count[:, None, None])
    support_size = ((2 * lat_ext - 1) * (2 * lon_count - 1)).astype(jnp.float32)
    row_scale = lax.rsqrt(support_size)
    masked = filter_taps.astype(jnp.float32) * support[:, None].astype(jnp.float32) * row_scale[:, None, None, None]
    return masked.astype(jnp.bfloat16)

def reference(features, cotangent, weight, filter_taps, lat_ext, lon_count):
    filters = make_filters(filter_taps, lat_ext, lon_count)
    spread = jnp.concatenate([filters[..., LON_DEV:].astype(jnp.float32), jnp.zeros((NLAT, K, NDL, NLON - 2 * LON_DEV), jnp.float32), filters[..., :LON_DEV].astype(jnp.float32)], axis=-1)
    kernel_spec = jnp.fft.rfft(spread, axis=-1)
    feature_spec = jnp.pad(jnp.fft.rfft(features.astype(jnp.float32), axis=1), ((HLAT, HLAT), (0, 0), (0, 0)))
    flat_cot = cotangent.reshape(NLAT * NLON, C)
    output = jnp.zeros((NLAT * NLON, C), jnp.float32)
    grad_spec = jnp.zeros((NLAT + 2 * HLAT, NLON // 2 + 1, C), kernel_spec.dtype)
    norm_scale = 1.0 / math.sqrt(NLAT * NLON)
    basis_grads = []
    for basis_index in range(K):
        summed = jnp.conj(kernel_spec[:, basis_index, 0])[:, :, None] * feature_spec[0:NLAT]
        for offset in range(1, NDL):
            summed = summed + jnp.conj(kernel_spec[:, basis_index, offset])[:, :, None] * feature_spec[offset:offset + NLAT]
        basis_out = jnp.fft.irfft(summed, n=NLON, axis=1).astype(jnp.bfloat16).reshape(NLAT * NLON, C)
        output = output + jnp.dot(basis_out, weight[basis_index], preferred_element_type=jnp.float32)
        basis_grad = lax.dot_general(flat_cot, weight[basis_index], (((1,), (1,)), ((), ())), preferred_element_type=jnp.float32).astype(jnp.bfloat16)
        partial_grad = lax.dot_general(basis_out, flat_cot, (((0,), (0,)), ((), ())), preferred_element_type=jnp.float32)
        basis_grads.append(partial_grad * norm_scale)
        grad_rows = jnp.fft.rfft(basis_grad.astype(jnp.float32).reshape(NLAT, NLON, C), axis=1)
        for offset in range(NDL):
            grad_spec = grad_spec.at[offset:offset + NLAT].add(kernel_spec[:, basis_index, offset][:, :, None] * grad_rows)
    field_grad = jnp.fft.irfft(grad_spec[HLAT:HLAT + NLAT], n=NLON, axis=1).astype(jnp.bfloat16)
    return (output.astype(jnp.bfloat16).reshape(NLAT, NLON, C), field_grad, jnp.stack(basis_grads))
```

```python
import math

import jax
import jax.numpy as jnp
from jax import lax
from jax.experimental import pallas as pl
from jax.experimental.pallas import tpu as pltpu
from jax.sharding import PartitionSpec as P

MESH = pl.DeviceIdType.MESH
PLANE = 16
ZLEN = 16
CHUNK = 32


def extended(cells, sides, width, closed):
    for axis, dim in sides:
        count = lax.axis_size(axis)
        ends = count if closed else count - 1
        head = lax.slice_in_dim(cells, 0, width, axis=dim)
        tail = lax.slice_in_dim(cells, cells.shape[dim] - width, cells.shape[dim], axis=dim)
        cells = jnp.concatenate(
            [
                lax.ppermute(tail, axis, [(i, (i + 1) % count) for i in range(ends)]),
                cells,
                lax.ppermute(head, axis, [((i + 1) % count, i) for i in range(ends)]),
            ],
            axis=dim,
        )
    return cells


def make_filters(filter_taps, lat_ext, lon_count):
    lat_reach = filter_taps.shape[2] // 2
    half_width = filter_taps.shape[3] // 2
    lat_dist = jnp.abs(jnp.arange(filter_taps.shape[2], dtype=jnp.int32) - lat_reach)
    lon_dist = jnp.abs(jnp.arange(filter_taps.shape[3], dtype=jnp.int32) - half_width)
    support = (lat_dist[None, :, None] < lat_ext[:, None, None]) & (
        lon_dist[None, None, :] < lon_count[:, None, None]
    )
    support_size = ((2 * lat_ext - 1) * (2 * lon_count - 1)).astype(jnp.float32)
    row_scale = lax.rsqrt(support_size)
    masked = (
        filter_taps.astype(jnp.float32)
        * support[:, None].astype(jnp.float32)
        * row_scale[:, None, None, None]
    )
    return masked.astype(jnp.bfloat16)


def forward_taps(row_taps, lon_width):
    leading = row_taps.shape[:-1]
    return jnp.concatenate(
        [row_taps, jnp.zeros(leading + (lon_width + 1,), row_taps.dtype)], axis=-1
    )


def reverse_taps(row_taps, lon_width):
    leading = row_taps.shape[:-1]
    return jnp.concatenate(
        [
            jnp.zeros(leading + (1,), row_taps.dtype),
            row_taps[..., ::-1],
            jnp.zeros(leading + (lon_width,), row_taps.dtype),
        ],
        axis=-1,
    )


def band_matrix(padded, lon_width):
    leading = padded.shape[:-1]
    repeated = jnp.tile(padded, (1,) * len(leading) + (lon_width,))
    return repeated[..., : lon_width * 3 * lon_width].reshape(leading + (lon_width, 3 * lon_width))


def gather_adjoint(filter_rims, basis_rows, row_count, lon_width, channels, basis_count, lat_taps):
    last = lat_taps - 1
    diagonal = jnp.stack(
        [
            filter_rims[last - offset : last - offset + row_count, :, offset]
            for offset in range(lat_taps)
        ],
        axis=2,
    )
    banded = band_matrix(reverse_taps(diagonal, lon_width), lon_width)
    total_grad = jnp.zeros((row_count, lon_width, channels), jnp.float32)
    for basis_index in range(basis_count):
        grad_window = basis_rows(basis_index)
        patches = jnp.stack(
            [grad_window[last - offset : last - offset + row_count] for offset in range(lat_taps)],
            axis=1,
        )
        total_grad = total_grad + jnp.einsum(
            "oejn,oenc->ojc", banded[:, basis_index], patches, preferred_element_type=jnp.float32
        )
    return total_grad


def sum_kernel(
    part_ref, out_ref, pair_out, pair_in, half, plane_in, zbuf,
    pair_sem, plane_send, plane_recv, z_send, z_recv, all_send, all_recv, near_send, near_recv,
):
    lat = lax.axis_index("lat")
    lon = lax.axis_index("lon")
    core = lat % 2
    y_lo = (lat // 2) % 2
    x = lat // 4
    z = lon % ZLEN
    y_hi = lon // ZLEN
    spot = x * 4 + y_hi * 2 + y_lo
    partner = (lat + 1 - 2 * core, lon)
    rows = PLANE * CHUNK

    def plane_device(index):
        return ((index // 4) * 4 + (index % 2) * 2 + core, ((index // 2) % 2) * ZLEN + z)

    def z_device(index):
        return (lat, y_hi * ZLEN + index)

    barrier = pltpu.get_barrier_semaphore()
    pl.semaphore_signal(barrier, inc=1, device_id=partner, device_id_type=MESH)

    def greet(step, carry):
        pl.semaphore_signal(
            barrier, inc=1, device_id=z_device((z + step) % ZLEN), device_id_type=MESH
        )
        pl.semaphore_signal(
            barrier, inc=1, device_id=plane_device((spot + step) % PLANE), device_id_type=MESH
        )
        return carry

    lax.fori_loop(1, PLANE, greet, 0)
    theirs = pl.multiple_of((1 - core) * rows, rows)
    mine = pl.multiple_of(core * rows, rows)
    pair_out[...] = part_ref[pl.ds(theirs, rows), :].astype(jnp.bfloat16)
    pl.semaphore_wait(barrier, 1 + (PLANE - 1) + (ZLEN - 1))

    pair = pltpu.make_async_remote_copy(
        src_ref=pair_out, dst_ref=pair_in, send_sem=pair_sem.at[0], recv_sem=pair_sem.at[1],
        device_id=partner, device_id_type=MESH,
    )
    pair.start()
    pair.wait()
    total = part_ref[pl.ds(mine, rows), :] + pair_in[...].astype(jnp.float32)
    half[...] = total.astype(jnp.bfloat16).reshape(PLANE, CHUNK, total.shape[-1])

    def plane_copy(step):
        target = (spot + step) % PLANE
        return pltpu.make_async_remote_copy(
            src_ref=half.at[target], dst_ref=plane_in.at[step], send_sem=plane_send.at[step],
            recv_sem=plane_recv.at[step], device_id=plane_device(target), device_id_type=MESH,
        )

    def plane_start(step, carry):
        plane_copy(step).start()
        return carry

    def plane_add(step, carry):
        plane_copy(step).wait_recv()
        return carry + plane_in[step].astype(jnp.float32)

    lax.fori_loop(1, PLANE, plane_start, 0)
    acc = lax.fori_loop(1, PLANE, plane_add, half[spot].astype(jnp.float32))
    zbuf[z] = acc.astype(jnp.bfloat16)

    def z_copy(step):
        return pltpu.make_async_remote_copy(
            src_ref=zbuf.at[z], dst_ref=zbuf.at[z], send_sem=z_send.at[step],
            recv_sem=z_recv.at[z], device_id=z_device((z + step) % ZLEN), device_id_type=MESH,
        )

    def z_start(step, carry):
        z_copy(step).start()
        return carry

    def z_wait(step, carry):
        source = (z + step) % ZLEN
        pltpu.make_async_remote_copy(
            src_ref=zbuf.at[source], dst_ref=zbuf.at[source], send_sem=z_send.at[step],
            recv_sem=z_recv.at[source], device_id=z_device(source), device_id_type=MESH,
        ).wait_recv()
        return carry

    lax.fori_loop(1, ZLEN, z_start, 0)
    lax.fori_loop(1, ZLEN, z_wait, 0)
    acc = zbuf[0].astype(jnp.float32)
    for source in range(1, ZLEN):
        acc = acc + zbuf[source].astype(jnp.float32)
    out_ref[core, spot] = acc.astype(jnp.bfloat16)

    def all_copy(step):
        return pltpu.make_async_remote_copy(
            src_ref=out_ref.at[core, spot], dst_ref=out_ref.at[core, spot],
            send_sem=all_send.at[step], recv_sem=all_recv.at[spot],
            device_id=plane_device((spot + step) % PLANE), device_id_type=MESH,
        )

    def near_copy(index):
        return pltpu.make_async_remote_copy(
            src_ref=out_ref.at[core, index], dst_ref=out_ref.at[core, index],
            send_sem=near_send.at[index], recv_sem=near_recv.at[index],
            device_id=partner, device_id_type=MESH,
        )

    def all_start(step, carry):
        all_copy(step).start()
        return carry

    def all_forward(step, carry):
        source = (spot + step) % PLANE
        pltpu.make_async_remote_copy(
            src_ref=out_ref.at[core, source], dst_ref=out_ref.at[core, source],
            send_sem=all_send.at[step], recv_sem=all_recv.at[source],
            device_id=plane_device(source), device_id_type=MESH,
        ).wait_recv()
        near_copy(source).start()
        return carry

    lax.fori_loop(1, PLANE, all_start, 0)
    near_copy(spot).start()
    lax.fori_loop(1, PLANE, all_forward, 0)

    def finish(step, carry):
        plane_copy(step).wait_send()
        z_copy(step).wait_send()
        all_copy(step).wait_send()
        return carry

    lax.fori_loop(1, PLANE, finish, 0)

    def near_finish(index, carry):
        near_copy(index).wait_send()
        pltpu.make_async_remote_copy(
            src_ref=out_ref.at[1 - core, index], dst_ref=out_ref.at[1 - core, index],
            send_sem=near_send.at[index], recv_sem=near_recv.at[index],
            device_id=partner, device_id_type=MESH,
        ).wait_recv()
        return carry

    lax.fori_loop(0, PLANE, near_finish, 0)


def sum_all(partial_grad):
    width = partial_grad.shape[1]
    bf16 = jnp.bfloat16
    dma = pltpu.SemaphoreType.DMA
    return pl.pallas_call(
        sum_kernel,
        out_shape=jax.ShapeDtypeStruct((2, PLANE, CHUNK, width), bf16),
        in_specs=[pl.BlockSpec(memory_space=pltpu.VMEM)],
        out_specs=pl.BlockSpec(memory_space=pltpu.VMEM),
        scratch_shapes=[
            pltpu.VMEM((PLANE * CHUNK, width), bf16),
            pltpu.VMEM((PLANE * CHUNK, width), bf16),
            pltpu.VMEM((PLANE, CHUNK, width), bf16),
            pltpu.VMEM((PLANE, CHUNK, width), bf16),
            pltpu.VMEM((ZLEN, CHUNK, width), bf16),
            dma((2,)), dma((PLANE,)), dma((PLANE,)), dma((ZLEN,)), dma((ZLEN,)),
            dma((PLANE,)), dma((PLANE,)), dma((PLANE,)), dma((PLANE,)),
        ],
        compiler_params=pltpu.CompilerParams(collective_id=0, has_side_effects=True),
    )(partial_grad)


def per_device(features, cotangent, weight, filter_taps, lat_ext, lon_count):
    row_count, lon_width, channels = features.shape
    basis_count = weight.shape[0]
    lat_taps = filter_taps.shape[2]
    lat_reach = lat_taps // 2
    filters = make_filters(filter_taps, lat_ext, lon_count)
    both = jnp.concatenate([features, cotangent], axis=-1)
    band_rows = extended(both, (("lat", 0),), lat_reach, False)
    window = extended(band_rows, (("lon", 1),), lon_width, True)
    banded_all = band_matrix(forward_taps(filters, lon_width), lon_width)
    patches = jnp.stack(
        [window[offset : offset + row_count, :, :channels] for offset in range(lat_taps)], axis=1
    )
    basis_f32 = jnp.einsum(
        "okejm,oemc->ojkc", banded_all, patches, preferred_element_type=jnp.float32
    )
    basis_out = basis_f32.astype(jnp.bfloat16)
    flat_out = basis_out.reshape(row_count * lon_width, basis_count * channels)
    flat_weight = weight.reshape(basis_count * channels, channels)
    output = jnp.dot(flat_out, flat_weight, preferred_element_type=jnp.float32).astype(jnp.bfloat16)
    output = output.reshape(row_count, lon_width, channels)
    flat_cot = cotangent.reshape(row_count * lon_width, channels)
    partial_grad = lax.dot_general(
        flat_out, flat_cot, (((0,), (0,)), ((), ())), preferred_element_type=jnp.float32
    )
    total_cells = row_count * lax.axis_size("lat") * lon_width * lax.axis_size("lon")
    summed_grad = sum_all(partial_grad).astype(jnp.float32)
    weight_grad = (summed_grad * (1.0 / math.sqrt(total_cells))).reshape(
        basis_count, channels, channels
    )
    filter_rims = extended(filters, (("lat", 0),), lat_reach, False)
    flat_window = window[..., channels:].reshape(-1, channels)

    def received_rows(basis_index):
        grad = lax.dot_general(
            flat_window,
            weight[basis_index],
            (((1,), (1,)), ((), ())),
            preferred_element_type=jnp.float32,
        ).astype(jnp.bfloat16)
        return grad.reshape(row_count + 2 * lat_reach, 3 * lon_width, channels)

    field_grad = gather_adjoint(
        filter_rims, received_rows, row_count, lon_width, channels, basis_count, lat_taps
    ).astype(jnp.bfloat16)
    return (output, field_grad, weight_grad)


def solution(mesh):
    in_specs = (
        P("lat", "lon", None),
        P("lat", "lon", None),
        P(),
        P("lat", None, None, None),
        P("lat"),
        P("lat"),
    )
    out_specs = (P("lat", "lon", None), P("lat", "lon", None), P())
    return jax.shard_map(
        per_device, mesh=mesh, in_specs=in_specs, out_specs=out_specs, check_vma=False
    )
```

```python
import math

import jax
import jax.numpy as jnp
from jax import lax
from jax.experimental import pallas as pl
from jax.experimental.pallas import tpu as pltpu
from jax.sharding import PartitionSpec as P

MESH = pl.DeviceIdType.MESH
PLANE = 16
ZLEN = 16
CHUNK = 32
LATS = 16
LONS = 32
ROWS = 4
REACH = 2
TAPS = 5
WIDE = 32
HALF = 32
BASES = 4
CH = 256
SPAN = ROWS + 2 * REACH
LANES = 128
BF16 = jnp.bfloat16
F32 = jnp.float32


def fill_filters(taps_ref, lat_ref, lon_ref, ft):
    lat_dist = jnp.abs(lax.broadcasted_iota(jnp.int32, (TAPS, 2 * HALF), 0) - REACH)
    lon_dist = jnp.abs(lax.broadcasted_iota(jnp.int32, (TAPS, 2 * HALF), 1) - HALF)
    ft[REACH : REACH + ROWS] = jnp.zeros((ROWS, BASES, 8, LANES), F32)
    for row in range(ROWS):
        ext, count = lat_ref[row], lon_ref[row]
        size = jnp.full((TAPS, 2 * HALF), (2 * ext - 1) * (2 * count - 1), jnp.int32).astype(F32)
        guess = lax.rsqrt(size)
        scale = guess * (1.5 - 0.5 * size * guess * guess)
        scale = jnp.where((lat_dist < ext) & (lon_dist < count), scale, 0.0)
        for basis in range(BASES):
            taps = taps_ref[row, basis].astype(F32) * scale
            ft[REACH + row, basis, 0:TAPS, 0 : 2 * HALF] = taps.astype(BF16).astype(F32)


def slanted(base):
    return pltpu.roll(jnp.broadcast_to(base, (WIDE, LANES)), 0, 1, stride=1, stride_axis=0)


def fill_forward(ft, north, south, bands):
    def one(basis, carry):
        start = pl.multiple_of(basis * WIDE, WIDE)
        for row in range(ROWS):
            for tap in range(TAPS):
                line = row + tap
                base = ft[REACH + row, basis, tap : tap + 1, :]
                if line < REACH:
                    base = base * north
                if line >= REACH + ROWS:
                    base = base * south
                bands[row, pl.ds(start, WIDE), tap * LANES : (tap + 1) * LANES] = slanted(
                    base
                ).astype(BF16)
        return carry

    lax.fori_loop(0, BASES, one, 0)


def convolve(bands, fw, bo):
    for row in range(ROWS):
        patch = fw[row : row + TAPS].reshape(TAPS * LANES, CH)
        sums = jnp.dot(bands[row], patch, preferred_element_type=F32).astype(BF16)
        bo[:, row * WIDE : (row + 1) * WIDE, :] = sums.reshape(BASES, WIDE, CH)


def mix(bo, weight_ref, out_ref):
    total = jnp.dot(bo[0], weight_ref[0], preferred_element_type=F32)
    for basis in range(1, BASES):
        total = total + jnp.dot(bo[basis], weight_ref[basis], preferred_element_type=F32)
    out_ref[...] = total.astype(BF16).reshape(ROWS, WIDE, CH)


def fill_basis_grad(cw, weight_ref, bg):
    cells = cw[...].reshape(SPAN * LANES, CH)

    def one(basis, carry):
        grad = lax.dot_general(
            cells, weight_ref[basis], (((1,), (1,)), ((), ())), preferred_element_type=F32
        )
        start = pl.multiple_of(basis * LANES, LANES)
        bg[:, pl.ds(start, LANES), :] = grad.astype(BF16).reshape(SPAN, LANES, CH)
        return carry

    lax.fori_loop(0, BASES, one, 0)


def fill_reversed(ft, north, south, rt):
    first = lax.broadcasted_iota(jnp.int32, (LANES, LANES), 0)
    second = lax.broadcasted_iota(jnp.int32, (LANES, LANES), 1)
    flip = jnp.where(first + second == 2 * HALF, 1.0, 0.0).astype(BF16)
    flat = ft[...].reshape(SPAN * BASES * 8, LANES).astype(BF16)
    turned = jnp.dot(flat, flip, preferred_element_type=F32)
    rt[...] = turned.reshape(SPAN, BASES, 8, LANES)
    rt[0:REACH] = rt[0:REACH] * north
    rt[REACH + ROWS :] = rt[REACH + ROWS :] * south


def adjoint(rt, bg, wedge, acc, grad_ref):
    acc[...] = jnp.zeros((ROWS * WIDE, CH), F32)
    for line in range(SPAN):
        low, high = max(0, line - TAPS + 1), min(ROWS - 1, line)

        def one(basis, carry):
            start = pl.multiple_of(basis * LANES, LANES)
            for row in range(low, high + 1):
                tap = row + TAPS - 1 - line
                base = rt[line, basis, tap : tap + 1, :]
                wedge[row * WIDE : (row + 1) * WIDE, pl.ds(start, LANES)] = slanted(base).astype(BF16)
            return carry

        lax.fori_loop(0, BASES, one, 0)
        span = slice(low * WIDE, (high + 1) * WIDE)
        acc[span, :] = acc[span, :] + jnp.dot(wedge[span, :], bg[line], preferred_element_type=F32)
    grad_ref[...] = acc[...].astype(BF16).reshape(ROWS, WIDE, CH)


def layer_kernel(
    feat_ref, cot_ref, weight_ref, taps_ref, lat_ref, lon_ref,
    out_ref, grad_ref, sum_ref,
    fw, cw, ft, rt, bands, bo, bg, wedge, acc, part, pair_out, pair_in, half, plane_in, zbuf,
    feat_send, feat_recv, cot_send, cot_recv, ft_send, ft_recv, pair_send, pair_recv,
    plane_send, plane_recv, z_send, z_recv, all_send, all_recv, near_send, near_recv,
):
    lat = lax.axis_index("lat")
    lon = lax.axis_index("lon")
    core = lat % 2
    y_lo = (lat // 2) % 2
    x = lat // 4
    z = lon % ZLEN
    y_hi = lon // ZLEN
    spot = x * 4 + y_hi * 2 + y_lo
    partner = (lat + 1 - 2 * core, lon)

    def plane_device(index):
        return ((index // 4) * 4 + (index % 2) * 2 + core, ((index // 2) % 2) * ZLEN + z)

    def z_device(index):
        return (lat, y_hi * ZLEN + index)

    def beside(up, right):
        return ((lat + LATS + up) % LATS, (lon + LONS + right) % LONS)

    ways = [(0, 1), (0, -1), (1, 1), (1, -1), (-1, 1), (-1, -1), (1, 0), (-1, 0)]

    def remote(src, dst, send, recv, device):
        return pltpu.make_async_remote_copy(
            src_ref=src, dst_ref=dst, send_sem=send, recv_sem=recv,
            device_id=device, device_id_type=MESH,
        )

    barrier = pltpu.get_barrier_semaphore()
    for way in ways:
        pl.semaphore_signal(barrier, inc=1, device_id=beside(*way), device_id_type=MESH)

    def greet(step, carry):
        pl.semaphore_signal(
            barrier, inc=1, device_id=z_device((z + step) % ZLEN), device_id_type=MESH
        )
        pl.semaphore_signal(
            barrier, inc=1, device_id=plane_device((spot + step) % PLANE), device_id_type=MESH
        )
        return carry

    lax.fori_loop(1, PLANE, greet, 0)

    north = jnp.where(lat > 0, 1.0, 0.0)
    south = jnp.where(lat < LATS - 1, 1.0, 0.0)
    inner = slice(REACH, REACH + ROWS)
    blank = jnp.zeros((SPAN, LANES - 3 * WIDE, CH), BF16)
    fw[:, 3 * WIDE :, :] = blank
    cw[:, 3 * WIDE :, :] = blank
    fw[inner, WIDE : 2 * WIDE, :] = feat_ref[...]
    cw[inner, WIDE : 2 * WIDE, :] = cot_ref[...]
    fill_filters(taps_ref, lat_ref, lon_ref, ft)
    fill_forward(ft, north, south, bands)
    pl.semaphore_wait(barrier, len(ways) + (PLANE - 1) + (ZLEN - 1))

    def halo(source, window, send, recv):
        copies = []
        for index, (up, right) in enumerate(ways):
            own = slice(0, ROWS) if up == 0 else slice(ROWS - REACH, ROWS) if up > 0 else slice(0, REACH)
            line = inner if up == 0 else slice(0, REACH) if up > 0 else slice(REACH + ROWS, SPAN)
            left = WIDE * (1 - right)
            copies.append(
                remote(
                    source.at[own], window.at[line, left : left + WIDE],
                    send.at[index], recv.at[index], beside(up, right),
                )
            )
        return copies

    feat_copies = halo(feat_ref, fw, feat_send, feat_recv)
    cot_copies = halo(cot_ref, cw, cot_send, cot_recv)
    ft_copies = [
        remote(ft.at[ROWS : ROWS + REACH], ft.at[0:REACH], ft_send.at[0], ft_recv.at[0], beside(1, 0)),
        remote(ft.at[REACH : 2 * REACH], ft.at[REACH + ROWS :], ft_send.at[1], ft_recv.at[1], beside(-1, 0)),
    ]
    for copy in feat_copies + ft_copies + cot_copies:
        copy.start()
    for copy in feat_copies:
        copy.wait_recv()
    convolve(bands, fw, bo)

    cells = cot_ref[...].reshape(ROWS * WIDE, CH)

    def share(basis):
        return lax.dot_general(bo[basis], cells, (((0,), (0,)), ((), ())), preferred_element_type=F32)

    def pair_copy(index):
        span = pl.ds(pl.multiple_of(index * CH, CH), CH)
        return remote(pair_out.at[span], pair_in.at[span], pair_send.at[index], pair_recv.at[index], partner)

    for index in range(2):
        pair_out[index * CH : (index + 1) * CH, :] = share((1 - core) * 2 + index).astype(BF16)
        pair_copy(index).start()
    for index in range(2):
        part[index * CH : (index + 1) * CH, :] = share(core * 2 + index)
    per = PLANE // 2
    for index in range(2):
        pair_copy(index).wait_recv()
        span = slice(index * CH, (index + 1) * CH)
        total = part[span, :] + pair_in[span, :].astype(F32)
        half[index * per : (index + 1) * per] = total.astype(BF16).reshape(per, CHUNK, CH)

    def plane_copy(step):
        target = (spot + step) % PLANE
        return remote(
            half.at[target], plane_in.at[step], plane_send.at[step], plane_recv.at[step],
            plane_device(target),
        )

    def plane_start(step, carry):
        plane_copy(step).start()
        return carry

    def plane_add(step, carry):
        plane_copy(step).wait_recv()
        return carry + plane_in[step].astype(F32)

    lax.fori_loop(1, PLANE, plane_start, 0)
    mix(bo, weight_ref, out_ref)
    for copy in cot_copies + ft_copies:
        copy.wait_recv()
    fill_basis_grad(cw, weight_ref, bg)
    chunk = lax.fori_loop(1, PLANE, plane_add, half[spot].astype(F32))
    zbuf[z] = chunk.astype(BF16)

    def z_copy(step):
        return remote(
            zbuf.at[z], zbuf.at[z], z_send.at[step], z_recv.at[z], z_device((z + step) % ZLEN)
        )

    def z_start(step, carry):
        z_copy(step).start()
        return carry

    def z_wait(step, carry):
        source = (z + step) % ZLEN
        remote(
            zbuf.at[source], zbuf.at[source], z_send.at[step], z_recv.at[source], z_device(source)
        ).wait_recv()
        return carry

    lax.fori_loop(1, ZLEN, z_start, 0)
    fill_reversed(ft, north, south, rt)
    adjoint(rt, bg, wedge, acc, grad_ref)
    lax.fori_loop(1, ZLEN, z_wait, 0)
    chunk = zbuf[0].astype(F32)
    for source in range(1, ZLEN):
        chunk = chunk + zbuf[source].astype(F32)
    sum_ref[core, spot] = chunk.astype(BF16)

    def all_copy(step):
        return remote(
            sum_ref.at[core, spot], sum_ref.at[core, spot], all_send.at[step], all_recv.at[spot],
            plane_device((spot + step) % PLANE),
        )

    def near_copy(index):
        return remote(
            sum_ref.at[core, index], sum_ref.at[core, index], near_send.at[index],
            near_recv.at[index], partner,
        )

    def all_start(step, carry):
        all_copy(step).start()
        return carry

    def all_forward(step, carry):
        source = (spot + step) % PLANE
        remote(
            sum_ref.at[core, source], sum_ref.at[core, source], all_send.at[step],
            all_recv.at[source], plane_device(source),
        ).wait_recv()
        near_copy(source).start()
        return carry

    lax.fori_loop(1, PLANE, all_start, 0)
    near_copy(spot).start()
    for copy in feat_copies + cot_copies + ft_copies:
        copy.wait_send()
    for index in range(2):
        pair_copy(index).wait_send()
    lax.fori_loop(1, PLANE, all_forward, 0)

    def finish(step, carry):
        plane_copy(step).wait_send()
        z_copy(step).wait_send()
        all_copy(step).wait_send()
        return carry

    lax.fori_loop(1, PLANE, finish, 0)

    def near_finish(index, carry):
        near_copy(index).wait_send()
        remote(
            sum_ref.at[1 - core, index], sum_ref.at[1 - core, index], near_send.at[index],
            near_recv.at[index], partner,
        ).wait_recv()
        return carry

    lax.fori_loop(0, PLANE, near_finish, 0)


def layer(features, cotangent, weight, filter_taps, lat_ext, lon_count):
    dma = pltpu.SemaphoreType.DMA
    vmem = pl.BlockSpec(memory_space=pltpu.VMEM)
    smem = pl.BlockSpec(memory_space=pltpu.SMEM)
    return pl.pallas_call(
        layer_kernel,
        out_shape=[
            jax.ShapeDtypeStruct((ROWS, WIDE, CH), BF16),
            jax.ShapeDtypeStruct((ROWS, WIDE, CH), BF16),
            jax.ShapeDtypeStruct((2, PLANE, CHUNK, CH), BF16),
        ],
        in_specs=[vmem, vmem, vmem, vmem, smem, smem],
        out_specs=[vmem, vmem, vmem],
        scratch_shapes=[
            pltpu.VMEM((SPAN, LANES, CH), BF16),
            pltpu.VMEM((SPAN, LANES, CH), BF16),
            pltpu.VMEM((SPAN, BASES, 8, LANES), F32),
            pltpu.VMEM((SPAN, BASES, 8, LANES), F32),
            pltpu.VMEM((ROWS, BASES * WIDE, TAPS * LANES), BF16),
            pltpu.VMEM((BASES, ROWS * WIDE, CH), BF16),
            pltpu.VMEM((SPAN, BASES * LANES, CH), BF16),
            pltpu.VMEM((ROWS * WIDE, BASES * LANES), BF16),
            pltpu.VMEM((ROWS * WIDE, CH), F32),
            pltpu.VMEM((2 * CH, CH), F32),
            pltpu.VMEM((2 * CH, CH), BF16),
            pltpu.VMEM((2 * CH, CH), BF16),
            pltpu.VMEM((PLANE, CHUNK, CH), BF16),
            pltpu.VMEM((PLANE, CHUNK, CH), BF16),
            pltpu.VMEM((ZLEN, CHUNK, CH), BF16),
            dma((8,)), dma((8,)), dma((8,)), dma((8,)), dma((2,)), dma((2,)), dma((2,)), dma((2,)),
            dma((PLANE,)), dma((PLANE,)), dma((ZLEN,)), dma((ZLEN,)),
            dma((PLANE,)), dma((PLANE,)), dma((PLANE,)), dma((PLANE,)),
        ],
        compiler_params=pltpu.CompilerParams(collective_id=0, has_side_effects=True),
    )(features, cotangent, weight, filter_taps, lat_ext, lon_count)


def per_device(features, cotangent, weight, filter_taps, lat_ext, lon_count):
    output, field_grad, total = layer(features, cotangent, weight, filter_taps, lat_ext, lon_count)
    cells = LATS * ROWS * LONS * WIDE
    weight_grad = (total.astype(F32) * (1.0 / math.sqrt(cells))).reshape(BASES, CH, CH)
    return (output, field_grad, weight_grad)


def solution(mesh):
    in_specs = (
        P("lat", "lon", None),
        P("lat", "lon", None),
        P(),
        P("lat", None, None, None),
        P("lat"),
        P("lat"),
    )
    out_specs = (P("lat", "lon", None), P("lat", "lon", None), P())
    return jax.shard_map(
        per_device, mesh=mesh, in_specs=in_specs, out_specs=out_specs, check_vma=False
    )
```

```python
import math

import jax
import jax.numpy as jnp
from jax import lax
from jax.experimental import pallas as pl
from jax.experimental.pallas import tpu as pltpu
from jax.sharding import PartitionSpec as P

MESH = pl.DeviceIdType.MESH
GROUP = 32
ZLEN = 16
ZFAR = 8
CHUNK = 16
LATS = 16
LONS = 32
ROWS = 4
REACH = 2
TAPS = 5
WIDE = 32
HALF = 32
BASES = 4
CH = 256
SPAN = ROWS + 2 * REACH
LANES = 128
BF16 = jnp.bfloat16
F32 = jnp.float32


def fill_filters(taps_ref, lat_ref, lon_ref, ft):
    lon_dist = jnp.abs(lax.broadcasted_iota(jnp.int32, (BASES, 2 * HALF), 1) - HALF)
    ft[REACH : REACH + ROWS] = jnp.zeros((ROWS, TAPS, 8, LANES), F32)
    for row in range(ROWS):
        ext, count = lat_ref[row], lon_ref[row]
        size = jnp.full((BASES, 2 * HALF), (2 * ext - 1) * (2 * count - 1), jnp.int32).astype(F32)
        guess = lax.rsqrt(size)
        scale = guess * (1.5 - 0.5 * size * guess * guess)
        scale = jnp.where(lon_dist < count, scale, 0.0)
        for tap in range(TAPS):
            held = jnp.where(abs(tap - REACH) < ext, scale, 0.0)
            taps = taps_ref[row, tap].astype(F32) * held
            ft[REACH + row, tap, 0:BASES, 0 : 2 * HALF] = taps.astype(BF16).astype(F32)


def slanted(base):
    return pltpu.roll(jnp.broadcast_to(base, (WIDE, LANES)), 0, 1, stride=1, stride_axis=0)


def fill_forward(ft, north, south, bands):
    def one(basis, carry):
        start = pl.multiple_of(basis * WIDE, WIDE)
        for row in range(ROWS):
            for tap in range(TAPS):
                line = row + tap
                base = ft[REACH + row, tap, pl.ds(basis, 1), :]
                if line < REACH:
                    base = base * north
                if line >= REACH + ROWS:
                    base = base * south
                bands[row, pl.ds(start, WIDE), tap * LANES : (tap + 1) * LANES] = slanted(
                    base
                ).astype(BF16)
        return carry

    lax.fori_loop(0, BASES, one, 0)


def convolve(bands, fw, bo):
    for row in range(ROWS):
        patch = fw[row : row + TAPS].reshape(TAPS * LANES, CH)
        sums = jnp.dot(bands[row], patch, preferred_element_type=F32).astype(BF16)
        bo[:, row * WIDE : (row + 1) * WIDE, :] = sums.reshape(BASES, WIDE, CH)


def mix(bo, weight_ref, out_ref):
    total = jnp.dot(bo[0], weight_ref[0], preferred_element_type=F32)
    for basis in range(1, BASES):
        total = total + jnp.dot(bo[basis], weight_ref[basis], preferred_element_type=F32)
    out_ref[...] = total.astype(BF16).reshape(ROWS, WIDE, CH)


def fill_basis_grad(cw, weight_ref, bg):
    cells = cw[...].reshape(SPAN * LANES, CH)

    def one(basis, carry):
        grad = lax.dot_general(
            cells, weight_ref[basis], (((1,), (1,)), ((), ())), preferred_element_type=F32
        )
        start = pl.multiple_of(basis * LANES, LANES)
        bg[:, pl.ds(start, LANES), :] = grad.astype(BF16).reshape(SPAN, LANES, CH)
        return carry

    lax.fori_loop(0, BASES, one, 0)


def fill_reversed(ft, north, south, rt):
    first = lax.broadcasted_iota(jnp.int32, (LANES, LANES), 0)
    second = lax.broadcasted_iota(jnp.int32, (LANES, LANES), 1)
    flip = jnp.where(first + second == 2 * HALF, 1.0, 0.0).astype(BF16)
    flat = ft[...].reshape(SPAN * TAPS * 8, LANES).astype(BF16)
    turned = jnp.dot(flat, flip, preferred_element_type=F32)
    rt[...] = turned.reshape(SPAN, TAPS, 8, LANES)
    rt[0:REACH] = rt[0:REACH] * north
    rt[REACH + ROWS :] = rt[REACH + ROWS :] * south


def adjoint(rt, bg, wedge, acc, grad_ref):
    acc[...] = jnp.zeros((ROWS * WIDE, CH), F32)
    for line in range(SPAN):
        low, high = max(0, line - TAPS + 1), min(ROWS - 1, line)

        def one(basis, carry):
            start = pl.multiple_of(basis * LANES, LANES)
            for row in range(low, high + 1):
                tap = row + TAPS - 1 - line
                base = rt[line, tap, pl.ds(basis, 1), :]
                wedge[row * WIDE : (row + 1) * WIDE, pl.ds(start, LANES)] = slanted(base).astype(BF16)
            return carry

        lax.fori_loop(0, BASES, one, 0)
        span = slice(low * WIDE, (high + 1) * WIDE)
        acc[span, :] = acc[span, :] + jnp.dot(wedge[span, :], bg[line], preferred_element_type=F32)
    grad_ref[...] = acc[...].astype(BF16).reshape(ROWS, WIDE, CH)


def layer_kernel(
    feat_any, cot_any, weight_any, taps_ref, lat_ref, lon_ref,
    out_ref, grad_ref, sum_ref,
    fw, cw, weight_ref, ft, rt, bands, bo, bg, wedge, acc, part, pair_out, pair_in, half, group_in, zbuf,
    own_sem, feat_send, feat_recv, cot_send, cot_recv, ft_send, ft_recv, pair_send, pair_recv,
    group_send, group_recv, z_send, z_recv, all_send, all_recv, near_send, near_recv,
    hop_sem, leap_sem,
):
    lat = lax.axis_index("lat")
    lon = lax.axis_index("lon")
    core = lat % 2
    y_lo = (lat // 2) % 2
    x = lat // 4
    z = lon % ZLEN
    z_lo = z % 2
    z_hi = z // 2
    y_hi = lon // ZLEN
    spot = (x * 4 + y_hi * 2 + y_lo) * 2 + z_lo
    partner = (lat + 1 - 2 * core, lon)

    def group_device(index):
        place = index // 2
        return (
            (place // 4) * 4 + (place % 2) * 2 + core,
            ((place // 2) % 2) * ZLEN + z_hi * 2 + index % 2,
        )

    def z_device(index):
        return (lat, y_hi * ZLEN + index)

    def far_device(index):
        return z_device(index * 2 + z_lo)

    def beside(up, right):
        return ((lat + LATS + up) % LATS, (lon + LONS + right) % LONS)

    ways = [(0, 1), (0, -1), (1, 1), (1, -1), (-1, 1), (-1, -1), (1, 0), (-1, 0)]

    def remote(src, dst, send, recv, device):
        return pltpu.make_async_remote_copy(
            src_ref=src, dst_ref=dst, send_sem=send, recv_sem=recv,
            device_id=device, device_id_type=MESH,
        )

    barrier = pltpu.get_barrier_semaphore()
    for way in ways:
        pl.semaphore_signal(barrier, inc=1, device_id=beside(*way), device_id_type=MESH)
    pl.semaphore_signal(barrier, inc=1, device_id=z_device((z + 2) % ZLEN), device_id_type=MESH)
    pl.semaphore_signal(
        barrier, inc=1, device_id=z_device((z + ZLEN - 2) % ZLEN), device_id_type=MESH
    )

    def greet(step, carry):
        pl.semaphore_signal(
            barrier, inc=1, device_id=group_device((spot + step) % GROUP), device_id_type=MESH
        )
        return carry

    lax.fori_loop(1, GROUP, greet, 0)

    north = jnp.where(lat > 0, 1.0, 0.0)
    south = jnp.where(lat < LATS - 1, 1.0, 0.0)
    inner = slice(REACH, REACH + ROWS)
    middle = slice(WIDE, 2 * WIDE)
    own_copies = [
        pltpu.make_async_copy(feat_any, fw.at[inner, middle], own_sem.at[0]),
        pltpu.make_async_copy(cot_any, cw.at[inner, middle], own_sem.at[1]),
        pltpu.make_async_copy(weight_any, weight_ref, own_sem.at[2]),
    ]
    for copy in own_copies:
        copy.start()
    blank = jnp.zeros((SPAN, LANES - 3 * WIDE, CH), BF16)
    fw[:, 3 * WIDE :, :] = blank
    cw[:, 3 * WIDE :, :] = blank
    fill_filters(taps_ref, lat_ref, lon_ref, ft)
    fill_forward(ft, north, south, bands)
    own_copies[0].wait()
    own_copies[1].wait()
    pl.semaphore_wait(barrier, len(ways) + 2 + (GROUP - 1))

    def halo(window, send, recv):
        copies = []
        for index, (up, right) in enumerate(ways):
            own = inner if up == 0 else slice(ROWS, ROWS + REACH) if up > 0 else slice(REACH, 2 * REACH)
            line = inner if up == 0 else slice(0, REACH) if up > 0 else slice(REACH + ROWS, SPAN)
            left = WIDE * (1 - right)
            copies.append(
                remote(
                    window.at[own, middle], window.at[line, left : left + WIDE],
                    send.at[index], recv.at[index], beside(up, right),
                )
            )
        return copies

    feat_copies = halo(fw, feat_send, feat_recv)
    cot_copies = halo(cw, cot_send, cot_recv)
    ft_copies = [
        remote(ft.at[ROWS : ROWS + REACH], ft.at[0:REACH], ft_send.at[0], ft_recv.at[0], beside(1, 0)),
        remote(ft.at[REACH : 2 * REACH], ft.at[REACH + ROWS :], ft_send.at[1], ft_recv.at[1], beside(-1, 0)),
    ]
    for copy in feat_copies:
        copy.start()
    pl.semaphore_signal(hop_sem, inc=1, device_id=z_device((z + 2) % ZLEN), device_id_type=MESH)
    pl.semaphore_signal(hop_sem, inc=1, device_id=z_device((z + ZLEN - 2) % ZLEN), device_id_type=MESH)
    for copy in feat_copies:
        copy.wait_recv()
    for copy in cot_copies + ft_copies:
        copy.start()
    pl.semaphore_wait(hop_sem, 2)
    pl.semaphore_signal(leap_sem, inc=1, device_id=z_device((z + 4) % ZLEN), device_id_type=MESH)
    pl.semaphore_signal(leap_sem, inc=1, device_id=z_device((z + ZLEN - 4) % ZLEN), device_id_type=MESH)
    convolve(bands, fw, bo)

    cells = cw[inner, middle, :].reshape(ROWS * WIDE, CH)

    def share(basis):
        return lax.dot_general(bo[basis], cells, (((0,), (0,)), ((), ())), preferred_element_type=F32)

    def pair_copy(index):
        span = pl.ds(pl.multiple_of(index * CH, CH), CH)
        return remote(pair_out.at[span], pair_in.at[span], pair_send.at[index], pair_recv.at[index], partner)

    for index in range(2):
        pair_out[index * CH : (index + 1) * CH, :] = share((1 - core) * 2 + index).astype(BF16)
        pair_copy(index).start()
    for index in range(2):
        part[index * CH : (index + 1) * CH, :] = share(core * 2 + index)
    per = GROUP // 2
    for index in range(2):
        pair_copy(index).wait_recv()
        span = slice(index * CH, (index + 1) * CH)
        total = part[span, :] + pair_in[span, :].astype(F32)
        half[index * per : (index + 1) * per] = total.astype(BF16).reshape(per, CHUNK, CH)

    def group_copy(step):
        target = (spot + step) % GROUP
        return remote(
            half.at[target], group_in.at[step], group_send.at[step], group_recv.at[step],
            group_device(target),
        )

    def group_start(step, carry):
        group_copy(step).start()
        return carry

    def group_add(step, carry):
        group_copy(step).wait_recv()
        return carry + group_in[step].astype(F32)

    lax.fori_loop(1, GROUP, group_start, 0)
    own_copies[2].wait()
    mix(bo, weight_ref, out_ref)
    for copy in cot_copies + ft_copies:
        copy.wait_recv()
    fill_basis_grad(cw, weight_ref, bg)
    chunk = lax.fori_loop(1, GROUP, group_add, half[spot].astype(F32))
    zbuf[z_hi] = chunk.astype(BF16)
    pl.semaphore_wait(leap_sem, 2)

    def z_copy(step):
        return remote(
            zbuf.at[z_hi], zbuf.at[z_hi], z_send.at[step], z_recv.at[z_hi],
            far_device((z_hi + step) % ZFAR),
        )

    def z_start(step, carry):
        z_copy(step).start()
        return carry

    def z_wait(step, carry):
        source = (z_hi + step) % ZFAR
        remote(
            zbuf.at[source], zbuf.at[source], z_send.at[step], z_recv.at[source], far_device(source)
        ).wait_recv()
        return carry

    lax.fori_loop(1, ZFAR, z_start, 0)
    fill_reversed(ft, north, south, rt)
    adjoint(rt, bg, wedge, acc, grad_ref)
    lax.fori_loop(1, ZFAR, z_wait, 0)
    chunk = zbuf[0].astype(F32)
    for source in range(1, ZFAR):
        chunk = chunk + zbuf[source].astype(F32)
    sum_ref[core, spot] = chunk.astype(BF16)

    def all_copy(step):
        return remote(
            sum_ref.at[core, spot], sum_ref.at[core, spot], all_send.at[step], all_recv.at[spot],
            group_device((spot + step) % GROUP),
        )

    def near_copy(index):
        return remote(
            sum_ref.at[core, index], sum_ref.at[core, index], near_send.at[index],
            near_recv.at[index], partner,
        )

    def all_start(step, carry):
        all_copy(step).start()
        return carry

    def all_forward(step, carry):
        source = (spot + step) % GROUP
        remote(
            sum_ref.at[core, source], sum_ref.at[core, source], all_send.at[step],
            all_recv.at[source], group_device(source),
        ).wait_recv()
        near_copy(source).start()
        return carry

    lax.fori_loop(1, GROUP, all_start, 0)
    near_copy(spot).start()
    for copy in feat_copies + cot_copies + ft_copies:
        copy.wait_send()
    for index in range(2):
        pair_copy(index).wait_send()

    def z_finish(step, carry):
        z_copy(step).wait_send()
        return carry

    lax.fori_loop(1, ZFAR, z_finish, 0)
    lax.fori_loop(1, GROUP, all_forward, 0)

    def finish(step, carry):
        group_copy(step).wait_send()
        all_copy(step).wait_send()
        return carry

    lax.fori_loop(1, GROUP, finish, 0)

    def near_finish(index, carry):
        near_copy(index).wait_send()
        remote(
            sum_ref.at[1 - core, index], sum_ref.at[1 - core, index], near_send.at[index],
            near_recv.at[index], partner,
        ).wait_recv()
        return carry

    lax.fori_loop(0, GROUP, near_finish, 0)


def layer(features, cotangent, weight, filter_taps, lat_ext, lon_count):
    dma = pltpu.SemaphoreType.DMA
    vmem = pl.BlockSpec(memory_space=pltpu.VMEM)
    smem = pl.BlockSpec(memory_space=pltpu.SMEM)
    anywhere = pl.BlockSpec(memory_space=pl.ANY)
    return pl.pallas_call(
        layer_kernel,
        out_shape=[
            pltpu.VMEM((ROWS, WIDE, CH), BF16),
            pltpu.VMEM((ROWS, WIDE, CH), BF16),
            pltpu.VMEM((2, GROUP, CHUNK, CH), BF16),
        ],
        in_specs=[anywhere, anywhere, anywhere, vmem, smem, smem],
        out_specs=[vmem, vmem, vmem],
        scratch_shapes=[
            pltpu.VMEM((SPAN, LANES, CH), BF16),
            pltpu.VMEM((SPAN, LANES, CH), BF16),
            pltpu.VMEM((BASES, CH, CH), BF16),
            pltpu.VMEM((SPAN, TAPS, 8, LANES), F32),
            pltpu.VMEM((SPAN, TAPS, 8, LANES), F32),
            pltpu.VMEM((ROWS, BASES * WIDE, TAPS * LANES), BF16),
            pltpu.VMEM((BASES, ROWS * WIDE, CH), BF16),
            pltpu.VMEM((SPAN, BASES * LANES, CH), BF16),
            pltpu.VMEM((ROWS * WIDE, BASES * LANES), BF16),
            pltpu.VMEM((ROWS * WIDE, CH), F32),
            pltpu.VMEM((2 * CH, CH), F32),
            pltpu.VMEM((2 * CH, CH), BF16),
            pltpu.VMEM((2 * CH, CH), BF16),
            pltpu.VMEM((GROUP, CHUNK, CH), BF16),
            pltpu.VMEM((GROUP, CHUNK, CH), BF16),
            pltpu.VMEM((ZFAR, CHUNK, CH), BF16),
            dma((3,)),
            dma((8,)), dma((8,)), dma((8,)), dma((8,)), dma((2,)), dma((2,)), dma((2,)), dma((2,)),
            dma((GROUP,)), dma((GROUP,)), dma((ZFAR,)), dma((ZFAR,)),
            dma((GROUP,)), dma((GROUP,)), dma((GROUP,)), dma((GROUP,)),
            pltpu.SemaphoreType.REGULAR, pltpu.SemaphoreType.REGULAR,
        ],
        compiler_params=pltpu.CompilerParams(collective_id=0, has_side_effects=True),
    )(features, cotangent, weight, filter_taps, lat_ext, lon_count)


PIECES = 8


def write_kernel(scale, out_ref, grad_ref, sum_ref, out_any, grad_any, total_any, wide, sem):
    copies = [
        pltpu.make_async_copy(out_ref, out_any, sem.at[PIECES]),
        pltpu.make_async_copy(grad_ref, grad_any, sem.at[PIECES + 1]),
    ]
    for copy in copies:
        copy.start()
    per = 2 * GROUP // PIECES
    for index in range(PIECES):
        side, first = (index * per) // GROUP, (index * per) % GROUP
        wide[side, first : first + per] = sum_ref[side, first : first + per].astype(F32) * scale
        copy = pltpu.make_async_copy(
            wide.at[side, first : first + per], total_any.at[side, first : first + per], sem.at[index]
        )
        copy.start()
        copies.append(copy)
    for copy in copies:
        copy.wait()


def write(scale, output, grad, total):
    vmem = pl.BlockSpec(memory_space=pltpu.VMEM)
    anywhere = pl.BlockSpec(memory_space=pl.ANY)
    return pl.pallas_call(
        lambda *refs: write_kernel(scale, *refs),
        out_shape=[
            jax.ShapeDtypeStruct(output.shape, BF16),
            jax.ShapeDtypeStruct(grad.shape, BF16),
            jax.ShapeDtypeStruct(total.shape, F32),
        ],
        in_specs=[vmem, vmem, vmem],
        out_specs=[anywhere, anywhere, anywhere],
        scratch_shapes=[pltpu.VMEM(total.shape, F32), pltpu.SemaphoreType.DMA((PIECES + 2,))],
        name="write",
    )(*(pltpu.with_memory_space_constraint(held, pltpu.VMEM) for held in (output, grad, total)))


def per_device(features, cotangent, weight, filter_taps, lat_ext, lon_count):
    taps = jnp.transpose(filter_taps, (0, 2, 1, 3))
    output, field_grad, total = layer(features, cotangent, weight, taps, lat_ext, lon_count)
    cells = LATS * ROWS * LONS * WIDE
    output, field_grad, total = write(1.0 / math.sqrt(cells), output, field_grad, total)
    return (output, field_grad, total.reshape(BASES, CH, CH))


def solution(mesh):
    in_specs = (
        P("lat", "lon", None),
        P("lat", "lon", None),
        P(),
        P("lat", None, None, None),
        P("lat"),
        P("lat"),
    )
    out_specs = (P("lat", "lon", None), P("lat", "lon", None), P())
    return jax.shard_map(
        per_device, mesh=mesh, in_specs=in_specs, out_specs=out_specs, check_vma=False
    )
```

```python
import math

import jax
import jax.numpy as jnp
from jax import lax
from jax.experimental import pallas as pl
from jax.experimental.pallas import tpu as pltpu
from jax.sharding import PartitionSpec as P

MESH = pl.DeviceIdType.MESH
GROUP = 32
ZLEN = 16
ZFAR = 8
CHUNK = 16
LATS = 16
LONS = 32
ROWS = 4
REACH = 2
TAPS = 5
WIDE = 32
HALF = 32
BASES = 4
CH = 256
SPAN = ROWS + 2 * REACH
LANES = 128
BF16 = jnp.bfloat16
F32 = jnp.float32


def fill_filters(taps_ref, lat_ref, lon_ref, ft):
    lon_dist = jnp.abs(lax.broadcasted_iota(jnp.int32, (BASES, 2 * HALF), 1) - HALF)
    ft[REACH : REACH + ROWS] = jnp.zeros((ROWS, TAPS, 8, LANES), F32)
    for row in range(ROWS):
        ext, count = lat_ref[row], lon_ref[row]
        size = jnp.full((BASES, 2 * HALF), (2 * ext - 1) * (2 * count - 1), jnp.int32).astype(F32)
        guess = lax.rsqrt(size)
        scale = guess * (1.5 - 0.5 * size * guess * guess)
        scale = jnp.where(lon_dist < count, scale, 0.0)
        for tap in range(TAPS):
            held = jnp.where(abs(tap - REACH) < ext, scale, 0.0)
            taps = taps_ref[row, tap].astype(F32) * held
            ft[REACH + row, tap, 0:BASES, 0 : 2 * HALF] = taps.astype(BF16).astype(F32)


def slanted(base):
    return pltpu.roll(jnp.broadcast_to(base, (WIDE, LANES)), 0, 1, stride=1, stride_axis=0)


def fill_forward(ft, north, south, bands):
    def one(basis, carry):
        start = pl.multiple_of(basis * WIDE, WIDE)
        for row in range(ROWS):
            for tap in range(TAPS):
                line = row + tap
                base = ft[REACH + row, tap, pl.ds(basis, 1), :]
                if line < REACH:
                    base = base * north
                if line >= REACH + ROWS:
                    base = base * south
                bands[row, pl.ds(start, WIDE), tap * LANES : (tap + 1) * LANES] = slanted(
                    base
                ).astype(BF16)
        return carry

    lax.fori_loop(0, BASES, one, 0)


def convolve(bands, fw, bo):
    for row in range(ROWS):
        patch = fw[row : row + TAPS].reshape(TAPS * LANES, CH)
        sums = jnp.dot(bands[row], patch, preferred_element_type=F32).astype(BF16)
        bo[:, row * WIDE : (row + 1) * WIDE, :] = sums.reshape(BASES, WIDE, CH)


def mix(bo, weight_ref, out_ref):
    total = jnp.dot(bo[0], weight_ref[0], preferred_element_type=F32)
    for basis in range(1, BASES):
        total = total + jnp.dot(bo[basis], weight_ref[basis], preferred_element_type=F32)
    out_ref[...] = total.astype(BF16).reshape(ROWS, WIDE, CH)


def fill_basis_grad(cw, weight_ref, bg):
    cells = cw[...].reshape(SPAN * LANES, CH)

    def one(basis, carry):
        grad = lax.dot_general(
            cells, weight_ref[basis], (((1,), (1,)), ((), ())), preferred_element_type=F32
        )
        start = pl.multiple_of(basis * LANES, LANES)
        bg[:, pl.ds(start, LANES), :] = grad.astype(BF16).reshape(SPAN, LANES, CH)
        return carry

    lax.fori_loop(0, BASES, one, 0)


def fill_reversed(ft, north, south, rt):
    first = lax.broadcasted_iota(jnp.int32, (LANES, LANES), 0)
    second = lax.broadcasted_iota(jnp.int32, (LANES, LANES), 1)
    flip = jnp.where(first + second == 2 * HALF, 1.0, 0.0).astype(BF16)
    flat = ft[...].reshape(SPAN * TAPS * 8, LANES).astype(BF16)
    turned = jnp.dot(flat, flip, preferred_element_type=F32)
    rt[...] = turned.reshape(SPAN, TAPS, 8, LANES)
    rt[0:REACH] = rt[0:REACH] * north
    rt[REACH + ROWS :] = rt[REACH + ROWS :] * south


def adjoint(rt, bg, wedge, acc, grad_ref):
    acc[...] = jnp.zeros((ROWS * WIDE, CH), F32)
    for line in range(SPAN):
        low, high = max(0, line - TAPS + 1), min(ROWS - 1, line)

        def one(basis, carry):
            start = pl.multiple_of(basis * LANES, LANES)
            for row in range(low, high + 1):
                tap = row + TAPS - 1 - line
                base = rt[line, tap, pl.ds(basis, 1), :]
                wedge[row * WIDE : (row + 1) * WIDE, pl.ds(start, LANES)] = slanted(base).astype(BF16)
            return carry

        lax.fori_loop(0, BASES, one, 0)
        span = slice(low * WIDE, (high + 1) * WIDE)
        acc[span, :] = acc[span, :] + jnp.dot(wedge[span, :], bg[line], preferred_element_type=F32)
    grad_ref[...] = acc[...].astype(BF16).reshape(ROWS, WIDE, CH)


def layer_kernel(
    feat_any, cot_any, weight_any, taps_ref, lat_ref, lon_ref,
    out_ref, grad_ref, sum_ref,
    fw, cw, weight_ref, ft, rt, bands, bo, bg, wedge, acc, part, pair_out, pair_in, half, group_in, zbuf,
    own_sem, feat_send, feat_recv, cot_send, cot_recv, ft_send, ft_recv, pair_send, pair_recv,
    group_send, group_recv, z_send, z_recv, all_send, all_recv, near_send, near_recv,
    hop_sem, leap_sem, step_sem, cross_sem, twin_sem,
):
    lat = lax.axis_index("lat")
    lon = lax.axis_index("lon")
    core = lat % 2
    y_lo = (lat // 2) % 2
    x = lat // 4
    z = lon % ZLEN
    z_lo = z % 2
    z_hi = z // 2
    y_hi = lon // ZLEN
    spot = (x * 4 + y_hi * 2 + y_lo) * 2 + z_lo
    partner = (lat + 1 - 2 * core, lon)

    def across(dx, dy, dz):
        far_x, far_y, far_z = (x + dx) % 4, (y_hi * 2 + y_lo + dy) % 4, (z_lo + dz) % 2
        device = (far_x * 4 + (far_y % 2) * 2 + core, (far_y // 2) * ZLEN + z_hi * 2 + far_z)
        return device, (far_x * 4 + far_y) * 2 + far_z

    def z_device(index):
        return (lat, y_hi * ZLEN + index)

    def far_device(index):
        return z_device(index * 2 + z_lo)

    def beside(up, right):
        return ((lat + LATS + up) % LATS, (lon + LONS + right) % LONS)

    ways = [(1, 1), (1, -1), (-1, 1), (-1, -1), (0, 1), (0, -1), (1, 0), (-1, 0)]

    def remote(src, dst, send, recv, device):
        return pltpu.make_async_remote_copy(
            src_ref=src, dst_ref=dst, send_sem=send, recv_sem=recv,
            device_id=device, device_id_type=MESH,
        )

    def signal(sem, device):
        pl.semaphore_signal(sem, inc=1, device_id=device, device_id_type=MESH)

    steps = [(1, 0), (3, 0), (0, 1), (0, 3)]
    barrier = pltpu.get_barrier_semaphore()
    for way in ways:
        signal(barrier, beside(*way))
    for dx, dy in steps:
        signal(barrier, across(dx, dy, 0)[0])
    signal(barrier, z_device((z + 2) % ZLEN))
    signal(barrier, z_device((z + ZLEN - 2) % ZLEN))

    north = jnp.where(lat > 0, 1.0, 0.0)
    south = jnp.where(lat < LATS - 1, 1.0, 0.0)
    inner = slice(REACH, REACH + ROWS)
    middle = slice(WIDE, 2 * WIDE)
    own_copies = [
        pltpu.make_async_copy(feat_any, fw.at[inner, middle], own_sem.at[0]),
        pltpu.make_async_copy(cot_any, cw.at[inner, middle], own_sem.at[1]),
        pltpu.make_async_copy(weight_any, weight_ref, own_sem.at[2]),
    ]
    for copy in own_copies:
        copy.start()
    own_copies[0].wait()
    pl.semaphore_wait(barrier, len(ways) + len(steps) + 2)

    def halo(window, send, recv):
        copies = []
        for index, (up, right) in enumerate(ways):
            own = inner if up == 0 else slice(ROWS, ROWS + REACH) if up > 0 else slice(REACH, 2 * REACH)
            line = inner if up == 0 else slice(0, REACH) if up > 0 else slice(REACH + ROWS, SPAN)
            left = WIDE * (1 - right)
            copies.append(
                remote(
                    window.at[own, middle], window.at[line, left : left + WIDE],
                    send.at[index], recv.at[index], beside(up, right),
                )
            )
        return copies

    feat_copies = halo(fw, feat_send, feat_recv)
    cot_copies = halo(cw, cot_send, cot_recv)
    ft_copies = [
        remote(ft.at[ROWS : ROWS + REACH], ft.at[0:REACH], ft_send.at[0], ft_recv.at[0], beside(1, 0)),
        remote(ft.at[REACH : 2 * REACH], ft.at[REACH + ROWS :], ft_send.at[1], ft_recv.at[1], beside(-1, 0)),
    ]
    for copy in feat_copies:
        copy.start()
    for dx, dy in steps:
        signal(step_sem, across(dx, dy, 0)[0])
    signal(hop_sem, z_device((z + 2) % ZLEN))
    signal(hop_sem, z_device((z + ZLEN - 2) % ZLEN))
    blank = jnp.zeros((SPAN, LANES - 3 * WIDE, CH), BF16)
    fw[:, 3 * WIDE :, :] = blank
    cw[:, 3 * WIDE :, :] = blank
    fill_filters(taps_ref, lat_ref, lon_ref, ft)
    fill_forward(ft, north, south, bands)
    pl.semaphore_wait(step_sem, len(steps))
    signal(cross_sem, across(2, 0, 0)[0])
    signal(cross_sem, across(0, 2, 0)[0])
    pl.semaphore_wait(hop_sem, 2)
    signal(leap_sem, z_device((z + 4) % ZLEN))
    signal(leap_sem, z_device((z + ZLEN - 4) % ZLEN))
    pl.semaphore_wait(cross_sem, 2)
    signal(twin_sem, across(0, 0, 1)[0])
    for copy in feat_copies:
        copy.wait_recv()
    own_copies[1].wait()
    for copy in cot_copies + ft_copies:
        copy.start()
    convolve(bands, fw, bo)

    cells = cw[inner, middle, :].reshape(ROWS * WIDE, CH)

    def share(basis):
        return lax.dot_general(bo[basis], cells, (((0,), (0,)), ((), ())), preferred_element_type=F32)

    def pair_copy(index):
        span = pl.ds(pl.multiple_of(index * CH, CH), CH)
        return remote(pair_out.at[span], pair_in.at[span], pair_send.at[index], pair_recv.at[index], partner)

    for index in range(2):
        pair_out[index * CH : (index + 1) * CH, :] = share((1 - core) * 2 + index).astype(BF16)
        pair_copy(index).start()
    for index in range(2):
        part[index * CH : (index + 1) * CH, :] = share(core * 2 + index)
    per = GROUP // 2
    for index in range(2):
        pair_copy(index).wait_recv()
        span = slice(index * CH, (index + 1) * CH)
        total = part[span, :] + pair_in[span, :].astype(F32)
        half[index * per : (index + 1) * per] = total.astype(BF16).reshape(per, CHUNK, CH)

    offsets = [(dx, dy, dz) for dx in (0, 1, 2, 3) for dy in (0, 1, 2, 3) for dz in (0, 1)][1:]
    offsets.sort(key=lambda o: -(min(o[0], 4 - o[0]) + min(o[1], 4 - o[1]) + o[2]))

    def group_copy(step):
        device, piece = across(*offsets[step])
        return remote(
            half.at[piece], group_in.at[step], group_send.at[step], group_recv.at[step], device
        )

    def group_slot(step):
        return remote(
            half.at[step], group_in.at[step], group_send.at[step], group_recv.at[step], partner
        )

    def group_add(step, carry):
        group_slot(step).wait_recv()
        return carry + group_in[step].astype(F32)

    pl.semaphore_wait(twin_sem, 1)
    for step in range(GROUP - 1):
        group_copy(step).start()
    own_copies[2].wait()
    mix(bo, weight_ref, out_ref)
    for copy in cot_copies + ft_copies:
        copy.wait_recv()
    fill_basis_grad(cw, weight_ref, bg)
    chunk = lax.fori_loop(0, GROUP - 1, group_add, half[spot].astype(F32))
    zbuf[z_hi] = chunk.astype(BF16)
    pl.semaphore_wait(leap_sem, 2)

    def z_copy(step):
        return remote(
            zbuf.at[z_hi], zbuf.at[z_hi], z_send.at[step], z_recv.at[z_hi],
            far_device((z_hi + step) % ZFAR),
        )

    def z_wait(step, carry):
        source = (z_hi + step) % ZFAR
        remote(
            zbuf.at[source], zbuf.at[source], z_send.at[step], z_recv.at[source], far_device(source)
        ).wait_recv()
        return carry

    for step in (4, 3, 5, 2, 6, 1, 7):
        z_copy(step).start()
    fill_reversed(ft, north, south, rt)
    adjoint(rt, bg, wedge, acc, grad_ref)
    lax.fori_loop(1, ZFAR, z_wait, 0)
    chunk = zbuf[0].astype(F32)
    for source in range(1, ZFAR):
        chunk = chunk + zbuf[source].astype(F32)
    sum_ref[core, spot] = chunk.astype(BF16)

    def all_copy(step):
        return remote(
            sum_ref.at[core, spot], sum_ref.at[core, spot], all_send.at[step], all_recv.at[spot],
            across(*offsets[step])[0],
        )

    def near_copy(index):
        return remote(
            sum_ref.at[core, index], sum_ref.at[core, index], near_send.at[index],
            near_recv.at[index], partner,
        )

    def all_forward(step, carry):
        source = (spot + step) % GROUP
        remote(
            sum_ref.at[core, source], sum_ref.at[core, source], all_send.at[step],
            all_recv.at[source], partner,
        ).wait_recv()
        near_copy(source).start()
        return carry

    for step in range(GROUP - 1):
        all_copy(step).start()
    near_copy(spot).start()
    for copy in feat_copies + cot_copies + ft_copies:
        copy.wait_send()
    for index in range(2):
        pair_copy(index).wait_send()

    def z_finish(step, carry):
        z_copy(step).wait_send()
        return carry

    lax.fori_loop(1, ZFAR, z_finish, 0)
    lax.fori_loop(1, GROUP, all_forward, 0)

    def finish(step, carry):
        group_slot(step).wait_send()
        remote(
            sum_ref.at[core, spot], sum_ref.at[core, spot], all_send.at[step], all_recv.at[spot],
            partner,
        ).wait_send()
        return carry

    lax.fori_loop(0, GROUP - 1, finish, 0)

    def near_finish(index, carry):
        near_copy(index).wait_send()
        remote(
            sum_ref.at[1 - core, index], sum_ref.at[1 - core, index], near_send.at[index],
            near_recv.at[index], partner,
        ).wait_recv()
        return carry

    lax.fori_loop(0, GROUP, near_finish, 0)


def layer(features, cotangent, weight, filter_taps, lat_ext, lon_count):
    dma = pltpu.SemaphoreType.DMA
    vmem = pl.BlockSpec(memory_space=pltpu.VMEM)
    smem = pl.BlockSpec(memory_space=pltpu.SMEM)
    anywhere = pl.BlockSpec(memory_space=pl.ANY)
    return pl.pallas_call(
        layer_kernel,
        out_shape=[
            pltpu.VMEM((ROWS, WIDE, CH), BF16),
            pltpu.VMEM((ROWS, WIDE, CH), BF16),
            pltpu.VMEM((2, GROUP, CHUNK, CH), BF16),
        ],
        in_specs=[anywhere, anywhere, anywhere, vmem, smem, smem],
        out_specs=[vmem, vmem, vmem],
        scratch_shapes=[
            pltpu.VMEM((SPAN, LANES, CH), BF16),
            pltpu.VMEM((SPAN, LANES, CH), BF16),
            pltpu.VMEM((BASES, CH, CH), BF16),
            pltpu.VMEM((SPAN, TAPS, 8, LANES), F32),
            pltpu.VMEM((SPAN, TAPS, 8, LANES), F32),
            pltpu.VMEM((ROWS, BASES * WIDE, TAPS * LANES), BF16),
            pltpu.VMEM((BASES, ROWS * WIDE, CH), BF16),
            pltpu.VMEM((SPAN, BASES * LANES, CH), BF16),
            pltpu.VMEM((ROWS * WIDE, BASES * LANES), BF16),
            pltpu.VMEM((ROWS * WIDE, CH), F32),
            pltpu.VMEM((2 * CH, CH), F32),
            pltpu.VMEM((2 * CH, CH), BF16),
            pltpu.VMEM((2 * CH, CH), BF16),
            pltpu.VMEM((GROUP, CHUNK, CH), BF16),
            pltpu.VMEM((GROUP, CHUNK, CH), BF16),
            pltpu.VMEM((ZFAR, CHUNK, CH), BF16),
            dma((3,)),
            dma((8,)), dma((8,)), dma((8,)), dma((8,)), dma((2,)), dma((2,)), dma((2,)), dma((2,)),
            dma((GROUP,)), dma((GROUP,)), dma((ZFAR,)), dma((ZFAR,)),
            dma((GROUP,)), dma((GROUP,)), dma((GROUP,)), dma((GROUP,)),
            *[pltpu.SemaphoreType.REGULAR] * 5,
        ],
        compiler_params=pltpu.CompilerParams(collective_id=0, has_side_effects=True),
    )(features, cotangent, weight, filter_taps, lat_ext, lon_count)


PIECES = 8


def write_kernel(scale, out_ref, grad_ref, sum_ref, out_any, grad_any, total_any, wide, sem):
    copies = [
        pltpu.make_async_copy(out_ref, out_any, sem.at[PIECES]),
        pltpu.make_async_copy(grad_ref, grad_any, sem.at[PIECES + 1]),
    ]
    for copy in copies:
        copy.start()
    per = 2 * GROUP // PIECES
    for index in range(PIECES):
        side, first = (index * per) // GROUP, (index * per) % GROUP
        wide[side, first : first + per] = sum_ref[side, first : first + per].astype(F32) * scale
        copy = pltpu.make_async_copy(
            wide.at[side, first : first + per], total_any.at[side, first : first + per], sem.at[index]
        )
        copy.start()
        copies.append(copy)
    for copy in copies:
        copy.wait()


def write(scale, output, grad, total):
    vmem = pl.BlockSpec(memory_space=pltpu.VMEM)
    anywhere = pl.BlockSpec(memory_space=pl.ANY)
    return pl.pallas_call(
        lambda *refs: write_kernel(scale, *refs),
        out_shape=[
            jax.ShapeDtypeStruct(output.shape, BF16),
            jax.ShapeDtypeStruct(grad.shape, BF16),
            jax.ShapeDtypeStruct(total.shape, F32),
        ],
        in_specs=[vmem, vmem, vmem],
        out_specs=[anywhere, anywhere, anywhere],
        scratch_shapes=[pltpu.VMEM(total.shape, F32), pltpu.SemaphoreType.DMA((PIECES + 2,))],
        name="write",
    )(*(pltpu.with_memory_space_constraint(held, pltpu.VMEM) for held in (output, grad, total)))


def per_device(features, cotangent, weight, filter_taps, lat_ext, lon_count):
    taps = jnp.transpose(filter_taps, (0, 2, 1, 3))
    output, field_grad, total = layer(features, cotangent, weight, taps, lat_ext, lon_count)
    cells = LATS * ROWS * LONS * WIDE
    output, field_grad, total = write(1.0 / math.sqrt(cells), output, field_grad, total)
    return (output, field_grad, total.reshape(BASES, CH, CH))


def solution(mesh):
    in_specs = (
        P("lat", "lon", None),
        P("lat", "lon", None),
        P(),
        P("lat", None, None, None),
        P("lat"),
        P("lat"),
    )
    out_specs = (P("lat", "lon", None), P("lat", "lon", None), P())
    return jax.shard_map(
        per_device, mesh=mesh, in_specs=in_specs, out_specs=out_specs, check_vma=False
    )
```

```python
import math

import jax
import jax.numpy as jnp
from jax import lax
from jax.experimental import pallas as pl
from jax.experimental.pallas import tpu as pltpu
from jax.sharding import PartitionSpec as P

MESH = pl.DeviceIdType.MESH
GROUP = 32
ZLEN = 16
ZFAR = 8
CHUNK = 16
LATS = 16
LONS = 32
ROWS = 4
REACH = 2
TAPS = 5
WIDE = 32
HALF = 32
BASES = 4
CH = 256
SPAN = ROWS + 2 * REACH
LANES = 128
BF16 = jnp.bfloat16
F32 = jnp.float32


def fill_filters(taps_ref, lat_ref, lon_ref, ft):
    lon_dist = jnp.abs(lax.broadcasted_iota(jnp.int32, (BASES, 2 * HALF), 1) - HALF)
    ft[REACH : REACH + ROWS] = jnp.zeros((ROWS, TAPS, 8, LANES), F32)
    for row in range(ROWS):
        ext, count = lat_ref[row], lon_ref[row]
        size = jnp.full((BASES, 2 * HALF), (2 * ext - 1) * (2 * count - 1), jnp.int32).astype(F32)
        guess = lax.rsqrt(size)
        scale = guess * (1.5 - 0.5 * size * guess * guess)
        scale = jnp.where(lon_dist < count, scale, 0.0)
        for tap in range(TAPS):
            held = jnp.where(abs(tap - REACH) < ext, scale, 0.0)
            taps = taps_ref[row, tap].astype(F32) * held
            ft[REACH + row, tap, 0:BASES, 0 : 2 * HALF] = taps.astype(BF16).astype(F32)


def slanted(base):
    return pltpu.roll(jnp.broadcast_to(base, (WIDE, LANES)), 0, 1, stride=1, stride_axis=0)


def fill_forward(ft, north, south, bands):
    def one(basis, carry):
        start = pl.multiple_of(basis * WIDE, WIDE)
        for row in range(ROWS):
            for tap in range(TAPS):
                line = row + tap
                base = ft[REACH + row, tap, pl.ds(basis, 1), :]
                if line < REACH:
                    base = base * north
                if line >= REACH + ROWS:
                    base = base * south
                bands[row, pl.ds(start, WIDE), tap * LANES : (tap + 1) * LANES] = slanted(
                    base
                ).astype(BF16)
        return carry

    lax.fori_loop(0, BASES, one, 0)


def convolve(bands, fw, bo):
    for row in range(ROWS):
        patch = fw[row : row + TAPS].reshape(TAPS * LANES, CH)
        sums = jnp.dot(bands[row], patch, preferred_element_type=F32).astype(BF16)
        bo[:, row * WIDE : (row + 1) * WIDE, :] = sums.reshape(BASES, WIDE, CH)


def mix(bo, weight_ref, out_ref):
    total = jnp.dot(bo[0], weight_ref[0], preferred_element_type=F32)
    for basis in range(1, BASES):
        total = total + jnp.dot(bo[basis], weight_ref[basis], preferred_element_type=F32)
    out_ref[...] = total.astype(BF16).reshape(ROWS, WIDE, CH)


def fill_basis_grad(cw, weight_ref, bg):
    cells = cw[...].reshape(SPAN * LANES, CH)

    def one(basis, carry):
        grad = lax.dot_general(
            cells, weight_ref[basis], (((1,), (1,)), ((), ())), preferred_element_type=F32
        )
        start = pl.multiple_of(basis * LANES, LANES)
        bg[:, pl.ds(start, LANES), :] = grad.astype(BF16).reshape(SPAN, LANES, CH)
        return carry

    lax.fori_loop(0, BASES, one, 0)


def fill_reversed(ft, north, south, rt):
    first = lax.broadcasted_iota(jnp.int32, (LANES, LANES), 0)
    second = lax.broadcasted_iota(jnp.int32, (LANES, LANES), 1)
    flip = jnp.where(first + second == 2 * HALF, 1.0, 0.0).astype(BF16)
    flat = ft[...].reshape(SPAN * TAPS * 8, LANES).astype(BF16)
    turned = jnp.dot(flat, flip, preferred_element_type=F32)
    rt[...] = turned.reshape(SPAN, TAPS, 8, LANES)
    rt[0:REACH] = rt[0:REACH] * north
    rt[REACH + ROWS :] = rt[REACH + ROWS :] * south


def adjoint(rt, bg, wedge, acc, grad_ref):
    acc[...] = jnp.zeros((ROWS * WIDE, CH), F32)
    for line in range(SPAN):
        low, high = max(0, line - TAPS + 1), min(ROWS - 1, line)

        def one(basis, carry):
            start = pl.multiple_of(basis * LANES, LANES)
            for row in range(low, high + 1):
                tap = row + TAPS - 1 - line
                base = rt[line, tap, pl.ds(basis, 1), :]
                wedge[row * WIDE : (row + 1) * WIDE, pl.ds(start, LANES)] = slanted(base).astype(BF16)
            return carry

        lax.fori_loop(0, BASES, one, 0)
        span = slice(low * WIDE, (high + 1) * WIDE)
        acc[span, :] = acc[span, :] + jnp.dot(wedge[span, :], bg[line], preferred_element_type=F32)
    grad_ref[...] = acc[...].astype(BF16).reshape(ROWS, WIDE, CH)


def layer_kernel(
    feat_any, cot_any, weight_any, taps_any, lat_any, lon_any,
    out_ref, grad_ref, sum_ref,
    fw, cw, weight_ref, taps_ref, lat_ref, lon_ref, ft, rt, bands, bo, bg, wedge, acc, part, pair_out, pair_in, half, group_in, zbuf,
    own_sem, feat_send, feat_recv, cot_send, cot_recv, ft_send, ft_recv, pair_send, pair_recv,
    group_recv, z_recv, all_recv, many_sem,
    hop_sem, leap_sem, step_sem, cross_sem, twin_sem,
):
    lat = lax.axis_index("lat")
    lon = lax.axis_index("lon")
    core = lat % 2
    y_lo = (lat // 2) % 2
    x = lat // 4
    z = lon % ZLEN
    z_lo = z % 2
    z_hi = z // 2
    y_hi = lon // ZLEN
    spot = (x * 4 + y_hi * 2 + y_lo) * 2 + z_lo
    partner = (lat + 1 - 2 * core, lon)

    def across(dx, dy, dz):
        far_x, far_y, far_z = (x + dx) % 4, (y_hi * 2 + y_lo + dy) % 4, (z_lo + dz) % 2
        device = (far_x * 4 + (far_y % 2) * 2 + core, (far_y // 2) * ZLEN + z_hi * 2 + far_z)
        return device, (far_x * 4 + far_y) * 2 + far_z

    def z_device(index):
        return (lat, y_hi * ZLEN + index)

    def far_device(index):
        return z_device(index * 2 + z_lo)

    def beside(up, right):
        return ((lat + LATS + up) % LATS, (lon + LONS + right) % LONS)

    ways = [(1, 1), (1, -1), (-1, 1), (-1, -1), (0, 1), (0, -1), (1, 0), (-1, 0)]

    def remote(src, dst, send, recv, device):
        return pltpu.make_async_remote_copy(
            src_ref=src, dst_ref=dst, send_sem=send, recv_sem=recv,
            device_id=device, device_id_type=MESH,
        )

    def signal(sem, device):
        pl.semaphore_signal(sem, inc=1, device_id=device, device_id_type=MESH)

    steps = [(1, 0), (3, 0), (0, 1), (0, 3)]
    barrier = pltpu.get_barrier_semaphore()
    for way in ways:
        signal(barrier, beside(*way))
    for dx, dy in steps:
        signal(barrier, across(dx, dy, 0)[0])
    signal(barrier, z_device((z + 2) % ZLEN))
    signal(barrier, z_device((z + ZLEN - 2) % ZLEN))

    north = jnp.where(lat > 0, 1.0, 0.0)
    south = jnp.where(lat < LATS - 1, 1.0, 0.0)
    inner = slice(REACH, REACH + ROWS)
    middle = slice(WIDE, 2 * WIDE)
    own_copies = [
        pltpu.make_async_copy(feat_any, fw.at[inner, middle], own_sem.at[0]),
        pltpu.make_async_copy(cot_any, cw.at[inner, middle], own_sem.at[1]),
        pltpu.make_async_copy(weight_any, weight_ref, own_sem.at[2]),
        pltpu.make_async_copy(taps_any, taps_ref, own_sem.at[3]),
        pltpu.make_async_copy(lat_any, lat_ref, own_sem.at[4]),
        pltpu.make_async_copy(lon_any, lon_ref, own_sem.at[5]),
    ]
    for copy in own_copies:
        copy.start()
    pl.semaphore_wait(barrier, len(ways) + len(steps) + 2)

    def halo(source, window, send, recv):
        copies = []
        for index, (up, right) in enumerate(ways):
            own = slice(0, ROWS) if up == 0 else slice(ROWS - REACH, ROWS) if up > 0 else slice(0, REACH)
            line = inner if up == 0 else slice(0, REACH) if up > 0 else slice(REACH + ROWS, SPAN)
            left = WIDE * (1 - right)
            copies.append(
                remote(
                    source.at[own], window.at[line, left : left + WIDE],
                    send.at[index], recv.at[index], beside(up, right),
                )
            )
        return copies

    feat_copies = halo(feat_any, fw, feat_send, feat_recv)
    cot_copies = halo(cot_any, cw, cot_send, cot_recv)
    ft_copies = [
        remote(ft.at[ROWS : ROWS + REACH], ft.at[0:REACH], ft_send.at[0], ft_recv.at[0], beside(1, 0)),
        remote(ft.at[REACH : 2 * REACH], ft.at[REACH + ROWS :], ft_send.at[1], ft_recv.at[1], beside(-1, 0)),
    ]
    for copy in feat_copies:
        copy.start()
    for dx, dy in steps:
        signal(step_sem, across(dx, dy, 0)[0])
    signal(hop_sem, z_device((z + 2) % ZLEN))
    signal(hop_sem, z_device((z + ZLEN - 2) % ZLEN))
    blank = jnp.zeros((SPAN, LANES - 3 * WIDE, CH), BF16)
    fw[:, 3 * WIDE :, :] = blank
    cw[:, 3 * WIDE :, :] = blank
    for copy in own_copies[3:]:
        copy.wait()
    fill_filters(taps_ref, lat_ref, lon_ref, ft)
    fill_forward(ft, north, south, bands)
    pl.semaphore_wait(step_sem, len(steps))
    signal(cross_sem, across(2, 0, 0)[0])
    signal(cross_sem, across(0, 2, 0)[0])
    pl.semaphore_wait(hop_sem, 2)
    signal(leap_sem, z_device((z + 4) % ZLEN))
    signal(leap_sem, z_device((z + ZLEN - 4) % ZLEN))
    for copy in feat_copies:
        copy.wait_recv()
    own_copies[0].wait()
    own_copies[1].wait()
    for copy in cot_copies + ft_copies:
        copy.start()
    convolve(bands, fw, bo)

    cells = cw[inner, middle, :].reshape(ROWS * WIDE, CH)

    def share(basis):
        return lax.dot_general(bo[basis], cells, (((0,), (0,)), ((), ())), preferred_element_type=F32)

    def pair_copy(index):
        span = pl.ds(pl.multiple_of(index * CH, CH), CH)
        return remote(pair_out.at[span], pair_in.at[span], pair_send.at[index], pair_recv.at[index], partner)

    for index in range(2):
        pair_out[index * CH : (index + 1) * CH, :] = share((1 - core) * 2 + index).astype(BF16)
        pair_copy(index).start()
    pl.semaphore_wait(cross_sem, 2)
    signal(twin_sem, across(0, 0, 1)[0])
    for index in range(2):
        part[index * CH : (index + 1) * CH, :] = share(core * 2 + index)
    per = GROUP // 2
    for index in range(2):
        pair_copy(index).wait_recv()
        span = slice(index * CH, (index + 1) * CH)
        total = part[span, :] + pair_in[span, :].astype(F32)
        half[index * per : (index + 1) * per] = total.astype(BF16).reshape(per, CHUNK, CH)

    offsets = [(dx, dy, dz) for dx in (0, 1, 2, 3) for dy in (0, 1, 2, 3) for dz in (0, 1)][1:]
    offsets.sort(key=lambda o: -(min(o[0], 4 - o[0]) + min(o[1], 4 - o[1]) + o[2]))

    def group_copy(step):
        device, piece = across(*offsets[step])
        return remote(
            half.at[piece], group_in.at[step], many_sem.at[0], group_recv.at[step], device
        )

    def group_slot(step):
        return remote(
            half.at[step], group_in.at[step], many_sem.at[0], group_recv.at[step], partner
        )

    def group_add(step, carry):
        group_slot(step).wait_recv()
        return carry + group_in[step].astype(F32)

    pl.semaphore_wait(twin_sem, 1)
    for step in range(GROUP - 1):
        group_copy(step).start()
    own_copies[2].wait()
    mix(bo, weight_ref, out_ref)
    chunk = lax.fori_loop(0, GROUP - 1, group_add, half[spot].astype(F32))
    zbuf[z_hi] = chunk.astype(BF16)
    pl.semaphore_wait(leap_sem, 2)

    def z_copy(step):
        return remote(
            zbuf.at[z_hi], zbuf.at[z_hi], many_sem.at[1], z_recv.at[z_hi],
            far_device((z_hi + step) % ZFAR),
        )

    def z_wait(step, carry):
        source = (z_hi + step) % ZFAR
        remote(
            zbuf.at[source], zbuf.at[source], many_sem.at[1], z_recv.at[source], far_device(source)
        ).wait_recv()
        return carry

    for step in (4, 3, 5, 2, 6, 1, 7):
        z_copy(step).start()
    for copy in cot_copies + ft_copies:
        copy.wait_recv()
    fill_basis_grad(cw, weight_ref, bg)
    fill_reversed(ft, north, south, rt)
    adjoint(rt, bg, wedge, acc, grad_ref)
    lax.fori_loop(1, ZFAR, z_wait, 0)
    chunk = zbuf[0].astype(F32)
    for source in range(1, ZFAR):
        chunk = chunk + zbuf[source].astype(F32)
    sum_ref[core, spot] = chunk.astype(BF16)

    def all_copy(step):
        return remote(
            sum_ref.at[core, spot], sum_ref.at[core, spot], many_sem.at[2], all_recv.at[step],
            across(*offsets[step])[0],
        )

    def near_copy(index):
        return remote(
            sum_ref.at[core, index], sum_ref.at[core, index], many_sem.at[3], many_sem.at[4], partner
        )

    for step in range(GROUP - 1):
        all_copy(step).start()
    near_copy(spot).start()
    for copy in feat_copies + cot_copies + ft_copies:
        copy.wait_send()
    for index in range(2):
        pair_copy(index).wait_send()
    remote(
        half.at[0 : GROUP - 1], group_in.at[0 : GROUP - 1], many_sem.at[0], group_recv.at[0], partner
    ).wait_send()
    remote(
        zbuf.at[0 : ZFAR - 1], zbuf.at[0 : ZFAR - 1], many_sem.at[1], z_recv.at[0], partner
    ).wait_send()
    for step in range(GROUP - 1):
        dx, dy, dz = offsets[step]
        source = across(4 - dx, 4 - dy, dz)[1]
        remote(
            sum_ref.at[core, source], sum_ref.at[core, source], many_sem.at[2], all_recv.at[step],
            partner,
        ).wait_recv()
        near_copy(source).start()
    remote(
        sum_ref.at[core, 0 : GROUP - 1], sum_ref.at[core, 0 : GROUP - 1], many_sem.at[2],
        all_recv.at[0], partner,
    ).wait_send()
    near_all = remote(
        sum_ref.at[core], sum_ref.at[1 - core], many_sem.at[3], many_sem.at[4], partner
    )
    near_all.wait_send()
    near_all.wait_recv()


def layer(features, cotangent, weight, filter_taps, lat_ext, lon_count):
    dma = pltpu.SemaphoreType.DMA
    vmem = pl.BlockSpec(memory_space=pltpu.VMEM)
    anywhere = pl.BlockSpec(memory_space=pl.ANY)
    return pl.pallas_call(
        layer_kernel,
        out_shape=[
            pltpu.VMEM((ROWS, WIDE, CH), BF16),
            pltpu.VMEM((ROWS, WIDE, CH), BF16),
            pltpu.VMEM((2, GROUP, CHUNK, CH), BF16),
        ],
        in_specs=[anywhere] * 6,
        out_specs=[vmem, vmem, vmem],
        scratch_shapes=[
            pltpu.VMEM((SPAN, LANES, CH), BF16),
            pltpu.VMEM((SPAN, LANES, CH), BF16),
            pltpu.VMEM((BASES, CH, CH), BF16),
            pltpu.VMEM((ROWS, TAPS, BASES, 2 * HALF), BF16),
            pltpu.SMEM((ROWS,), jnp.int32),
            pltpu.SMEM((ROWS,), jnp.int32),
            pltpu.VMEM((SPAN, TAPS, 8, LANES), F32),
            pltpu.VMEM((SPAN, TAPS, 8, LANES), F32),
            pltpu.VMEM((ROWS, BASES * WIDE, TAPS * LANES), BF16),
            pltpu.VMEM((BASES, ROWS * WIDE, CH), BF16),
            pltpu.VMEM((SPAN, BASES * LANES, CH), BF16),
            pltpu.VMEM((ROWS * WIDE, BASES * LANES), BF16),
            pltpu.VMEM((ROWS * WIDE, CH), F32),
            pltpu.VMEM((2 * CH, CH), F32),
            pltpu.VMEM((2 * CH, CH), BF16),
            pltpu.VMEM((2 * CH, CH), BF16),
            pltpu.VMEM((GROUP, CHUNK, CH), BF16),
            pltpu.VMEM((GROUP, CHUNK, CH), BF16),
            pltpu.VMEM((ZFAR, CHUNK, CH), BF16),
            dma((6,)),
            dma((8,)), dma((8,)), dma((8,)), dma((8,)), dma((2,)), dma((2,)), dma((2,)), dma((2,)),
            dma((GROUP,)), dma((ZFAR,)), dma((GROUP,)), dma((5,)),
            *[pltpu.SemaphoreType.REGULAR] * 5,
        ],
        compiler_params=pltpu.CompilerParams(collective_id=0, has_side_effects=True),
    )(features, cotangent, weight, filter_taps, lat_ext, lon_count)


PIECES = 8


def write_kernel(scale, out_ref, grad_ref, sum_ref, out_any, grad_any, total_any, wide, sem):
    copies = [
        pltpu.make_async_copy(out_ref, out_any, sem.at[PIECES]),
        pltpu.make_async_copy(grad_ref, grad_any, sem.at[PIECES + 1]),
    ]
    for copy in copies:
        copy.start()
    per = 2 * GROUP // PIECES
    for index in range(PIECES):
        side, first = (index * per) // GROUP, (index * per) % GROUP
        wide[side, first : first + per] = sum_ref[side, first : first + per].astype(F32) * scale
        copy = pltpu.make_async_copy(
            wide.at[side, first : first + per], total_any.at[side, first : first + per], sem.at[index]
        )
        copy.start()
        copies.append(copy)
    for copy in copies:
        copy.wait()


def write(scale, output, grad, total):
    vmem = pl.BlockSpec(memory_space=pltpu.VMEM)
    anywhere = pl.BlockSpec(memory_space=pl.ANY)
    return pl.pallas_call(
        lambda *refs: write_kernel(scale, *refs),
        out_shape=[
            jax.ShapeDtypeStruct(output.shape, BF16),
            jax.ShapeDtypeStruct(grad.shape, BF16),
            jax.ShapeDtypeStruct(total.shape, F32),
        ],
        in_specs=[vmem, vmem, vmem],
        out_specs=[anywhere, anywhere, anywhere],
        scratch_shapes=[pltpu.VMEM(total.shape, F32), pltpu.SemaphoreType.DMA((PIECES + 2,))],
        name="write",
    )(*(pltpu.with_memory_space_constraint(held, pltpu.VMEM) for held in (output, grad, total)))


def per_device(features, cotangent, weight, filter_taps, lat_ext, lon_count):
    taps = jnp.transpose(filter_taps, (0, 2, 1, 3))
    output, field_grad, total = layer(features, cotangent, weight, taps, lat_ext, lon_count)
    cells = LATS * ROWS * LONS * WIDE
    output, field_grad, total = write(1.0 / math.sqrt(cells), output, field_grad, total)
    return (output, field_grad, total.reshape(BASES, CH, CH))


def solution(mesh):
    in_specs = (
        P("lat", "lon", None),
        P("lat", "lon", None),
        P(),
        P("lat", None, None, None),
        P("lat"),
        P("lat"),
    )
    out_specs = (P("lat", "lon", None), P("lat", "lon", None), P())
    return jax.shard_map(
        per_device, mesh=mesh, in_specs=in_specs, out_specs=out_specs, check_vma=False
    )
```

```python
import math

import jax
import jax.numpy as jnp
from jax import lax
from jax.experimental import pallas as pl
from jax.experimental.pallas import tpu as pltpu
from jax.sharding import PartitionSpec as P

MESH = pl.DeviceIdType.MESH
GROUP = 32
ZLEN = 16
ZFAR = 8
CHUNK = 16
LATS = 16
LONS = 32
ROWS = 4
REACH = 2
TAPS = 5
WIDE = 32
HALF = 32
BASES = 4
CH = 256
SPAN = ROWS + 2 * REACH
LANES = 128
BF16 = jnp.bfloat16
F32 = jnp.float32


def fill_filters(taps_ref, lat_ref, lon_ref, ft):
    lon_dist = jnp.abs(lax.broadcasted_iota(jnp.int32, (BASES, 2 * HALF), 1) - HALF)
    ft[REACH : REACH + ROWS] = jnp.zeros((ROWS, TAPS, 8, LANES), F32)
    for row in range(ROWS):
        ext, count = lat_ref[row], lon_ref[row]
        size = jnp.full((BASES, 2 * HALF), (2 * ext - 1) * (2 * count - 1), jnp.int32).astype(F32)
        guess = lax.rsqrt(size)
        scale = guess * (1.5 - 0.5 * size * guess * guess)
        scale = jnp.where(lon_dist < count, scale, 0.0)
        for tap in range(TAPS):
            held = jnp.where(abs(tap - REACH) < ext, scale, 0.0)
            taps = taps_ref[row, tap].astype(F32) * held
            ft[REACH + row, tap, 0:BASES, 0 : 2 * HALF] = taps.astype(BF16).astype(F32)


def slanted(base):
    return pltpu.roll(jnp.broadcast_to(base, (WIDE, LANES)), 0, 1, stride=1, stride_axis=0)


def fill_forward(ft, north, south, bands):
    def one(basis, carry):
        start = pl.multiple_of(basis * WIDE, WIDE)
        for row in range(ROWS):
            for tap in range(TAPS):
                line = row + tap
                base = ft[REACH + row, tap, pl.ds(basis, 1), :]
                if line < REACH:
                    base = base * north
                if line >= REACH + ROWS:
                    base = base * south
                bands[row, pl.ds(start, WIDE), tap * LANES : (tap + 1) * LANES] = slanted(
                    base
                ).astype(BF16)
        return carry

    lax.fori_loop(0, BASES, one, 0)


def convolve(bands, fw, bo, first):
    span = pl.ds(pl.multiple_of(first * WIDE, 2 * WIDE), 2 * WIDE)
    for row in range(ROWS):
        patch = fw[row : row + TAPS].reshape(TAPS * LANES, CH)
        sums = jnp.dot(bands[row, span, :], patch, preferred_element_type=F32).astype(BF16)
        bo[pl.ds(first, 2), row * WIDE : (row + 1) * WIDE, :] = sums.reshape(2, WIDE, CH)


def mix(bo, weight_ref, out_ref):
    total = jnp.dot(bo[0], weight_ref[0], preferred_element_type=F32)
    for basis in range(1, BASES):
        total = total + jnp.dot(bo[basis], weight_ref[basis], preferred_element_type=F32)
    out_ref[...] = total.astype(BF16).reshape(ROWS, WIDE, CH)


def fill_basis_grad(cw, weight_ref, bg):
    cells = cw[...].reshape(SPAN * LANES, CH)

    def one(basis, carry):
        grad = lax.dot_general(
            cells, weight_ref[basis], (((1,), (1,)), ((), ())), preferred_element_type=F32
        )
        start = pl.multiple_of(basis * LANES, LANES)
        bg[:, pl.ds(start, LANES), :] = grad.astype(BF16).reshape(SPAN, LANES, CH)
        return carry

    lax.fori_loop(0, BASES, one, 0)


def fill_reversed(ft, north, south, rt):
    first = lax.broadcasted_iota(jnp.int32, (LANES, LANES), 0)
    second = lax.broadcasted_iota(jnp.int32, (LANES, LANES), 1)
    flip = jnp.where(first + second == 2 * HALF, 1.0, 0.0).astype(BF16)
    flat = ft[...].reshape(SPAN * TAPS * 8, LANES).astype(BF16)
    turned = jnp.dot(flat, flip, preferred_element_type=F32)
    rt[...] = turned.reshape(SPAN, TAPS, 8, LANES)
    rt[0:REACH] = rt[0:REACH] * north
    rt[REACH + ROWS :] = rt[REACH + ROWS :] * south


def adjoint(rt, bg, wedge, acc, grad_ref):
    acc[...] = jnp.zeros((ROWS * WIDE, CH), F32)
    for line in range(SPAN):
        low, high = max(0, line - TAPS + 1), min(ROWS - 1, line)

        def one(basis, carry):
            start = pl.multiple_of(basis * LANES, LANES)
            for row in range(low, high + 1):
                tap = row + TAPS - 1 - line
                base = rt[line, tap, pl.ds(basis, 1), :]
                wedge[row * WIDE : (row + 1) * WIDE, pl.ds(start, LANES)] = slanted(base).astype(BF16)
            return carry

        lax.fori_loop(0, BASES, one, 0)
        span = slice(low * WIDE, (high + 1) * WIDE)
        acc[span, :] = acc[span, :] + jnp.dot(wedge[span, :], bg[line], preferred_element_type=F32)
    grad_ref[...] = acc[...].astype(BF16).reshape(ROWS, WIDE, CH)


def layer_kernel(
    feat_any, cot_any, weight_any, taps_any, lat_any, lon_any,
    out_ref, grad_ref, sum_ref,
    fw, cw, weight_ref, taps_ref, lat_ref, lon_ref, ft, rt, bands, bo, bg, wedge, acc, part, pair_out, pair_in, half, group_in, zbuf,
    own_sem, feat_send, feat_recv, cot_send, cot_recv, ft_send, ft_recv, pair_send, pair_recv,
    group_recv, z_recv, all_recv, many_sem,
    hop_sem, leap_sem, step_sem, cross_sem, twin_sem,
):
    lat = lax.axis_index("lat")
    lon = lax.axis_index("lon")
    core = lat % 2
    y_lo = (lat // 2) % 2
    x = lat // 4
    z = lon % ZLEN
    z_lo = z % 2
    z_hi = z // 2
    y_hi = lon // ZLEN
    spot = z_lo * 16 + x * 4 + y_hi * 2 + y_lo
    partner = (lat + 1 - 2 * core, lon)

    def across(dx, dy, dz):
        far_x, far_y, far_z = (x + dx) % 4, (y_hi * 2 + y_lo + dy) % 4, (z_lo + dz) % 2
        device = (far_x * 4 + (far_y % 2) * 2 + core, (far_y // 2) * ZLEN + z_hi * 2 + far_z)
        return device, far_z * 16 + far_x * 4 + far_y

    def z_device(index):
        return (lat, y_hi * ZLEN + index)

    def far_device(index):
        return z_device(index * 2 + z_lo)

    def beside(up, right):
        return ((lat + LATS + up) % LATS, (lon + LONS + right) % LONS)

    away = 2 * core - 1
    ways = [(away, 1), (away, -1), (0, 1), (0, -1), (1, 0), (-1, 0)]

    def remote(src, dst, send, recv, device):
        return pltpu.make_async_remote_copy(
            src_ref=src, dst_ref=dst, send_sem=send, recv_sem=recv,
            device_id=device, device_id_type=MESH,
        )

    def signal(sem, device):
        pl.semaphore_signal(sem, inc=1, device_id=device, device_id_type=MESH)

    steps = [(1, 0), (3, 0), (0, 1), (0, 3)]
    barrier = pltpu.get_barrier_semaphore()
    for way in ways:
        signal(barrier, beside(*way))
    for dx, dy in steps:
        signal(barrier, across(dx, dy, 0)[0])
    signal(barrier, z_device((z + 2) % ZLEN))
    signal(barrier, z_device((z + ZLEN - 2) % ZLEN))

    north = jnp.where(lat > 0, 1.0, 0.0)
    south = jnp.where(lat < LATS - 1, 1.0, 0.0)
    inner = slice(REACH, REACH + ROWS)
    middle = slice(WIDE, 2 * WIDE)
    own_copies = [
        pltpu.make_async_copy(feat_any, fw.at[inner, middle], own_sem.at[0]),
        pltpu.make_async_copy(cot_any, cw.at[inner, middle], own_sem.at[1]),
        pltpu.make_async_copy(weight_any, weight_ref, own_sem.at[2]),
        pltpu.make_async_copy(taps_any, taps_ref, own_sem.at[3]),
        pltpu.make_async_copy(lat_any, lat_ref, own_sem.at[4]),
        pltpu.make_async_copy(lon_any, lon_ref, own_sem.at[5]),
    ]
    for copy in own_copies:
        copy.start()
    pl.semaphore_wait(barrier, len(ways) + len(steps) + 2)

    def rows(window, start, left):
        return window.at[pl.ds(start, REACH), left : left + WIDE]

    common, single = REACH * (1 - core), REACH * core
    far = REACH + ROWS

    def halo(source, window, send, recv):
        out, arrive = [], []

        def add(src, start, landing, left, device):
            index = len(out)
            out.append(remote(src, rows(window, start, left), send.at[index], recv.at[index], device))
            place = rows(window, landing, left)
            arrive.append(remote(place, place, send.at[index], recv.at[index], partner))

        for right in (1, -1):
            start = REACH + common
            add(source.at[pl.ds(common, REACH)], start, start, WIDE * (1 - right), beside(0, right))
        for right in (1, -1):
            add(
                source.at[pl.ds(single, REACH)], far * (1 - core), far * core, WIDE * (1 - right),
                beside(away, right),
            )
        for right in (1, -1):
            start = REACH + single
            add(source.at[pl.ds(single, REACH)], start, start, WIDE * (1 - right), beside(0, right))
        add(source.at[ROWS - REACH :], 0, 0, WIDE, beside(1, 0))
        add(source.at[0:REACH], far, far, WIDE, beside(-1, 0))
        for right in (1, -1):
            left = WIDE * (1 - right)
            add(rows(window, REACH + common, left), far * core, far * (1 - core), left, partner)
        return out, arrive

    feat_copies, feat_arrive = halo(feat_any, fw, feat_send, feat_recv)
    cot_copies, cot_arrive = halo(cot_any, cw, cot_send, cot_recv)
    ft_copies = [
        remote(ft.at[ROWS : ROWS + REACH], ft.at[0:REACH], ft_send.at[0], ft_recv.at[0], beside(1, 0)),
        remote(ft.at[REACH : 2 * REACH], ft.at[REACH + ROWS :], ft_send.at[1], ft_recv.at[1], beside(-1, 0)),
    ]
    for copy in feat_copies[:8]:
        copy.start()
    for dx, dy in steps:
        signal(step_sem, across(dx, dy, 0)[0])
    signal(hop_sem, z_device((z + 2) % ZLEN))
    signal(hop_sem, z_device((z + ZLEN - 2) % ZLEN))
    blank = jnp.zeros((SPAN, LANES - 3 * WIDE, CH), BF16)
    fw[:, 3 * WIDE :, :] = blank
    cw[:, 3 * WIDE :, :] = blank
    for copy in own_copies[3:]:
        copy.wait()
    fill_filters(taps_ref, lat_ref, lon_ref, ft)
    fill_forward(ft, north, south, bands)
    pl.semaphore_wait(step_sem, len(steps))
    signal(cross_sem, across(2, 0, 0)[0])
    signal(cross_sem, across(0, 2, 0)[0])
    pl.semaphore_wait(hop_sem, 2)
    signal(leap_sem, z_device((z + 4) % ZLEN))
    signal(leap_sem, z_device((z + ZLEN - 4) % ZLEN))
    for index in range(2):
        feat_arrive[index].wait_recv()
        feat_copies[8 + index].start()
    for copy in feat_arrive[2:]:
        copy.wait_recv()
    own_copies[0].wait()
    own_copies[1].wait()
    convolve(bands, fw, bo, (1 - core) * 2)

    cells = cw[inner, middle, :].reshape(ROWS * WIDE, CH)

    def share(basis):
        return lax.dot_general(bo[basis], cells, (((0,), (0,)), ((), ())), preferred_element_type=F32)

    def pair_copy(index):
        span = pl.ds(pl.multiple_of(index * CH, CH), CH)
        return remote(pair_out.at[span], pair_in.at[span], pair_send.at[index], pair_recv.at[index], partner)

    for index in range(2):
        pair_out[index * CH : (index + 1) * CH, :] = share((1 - core) * 2 + index).astype(BF16)
        pair_copy(index).start()
    pl.semaphore_wait(cross_sem, 2)
    signal(twin_sem, across(0, 0, 1)[0])
    convolve(bands, fw, bo, core * 2)
    for index in range(2):
        part[index * CH : (index + 1) * CH, :] = share(core * 2 + index)
    per = GROUP // 2
    places = [(dx, dy) for dx in (0, 1, 2, 3) for dy in (0, 1, 2, 3)]
    places.sort(key=lambda p: -(min(p[0], 4 - p[0]) + min(p[1], 4 - p[1])))
    offsets = [(dx, dy, dz) for dx, dy in places for dz in (0, 1)]
    offsets.sort(key=lambda o: -(min(o[0], 4 - o[0]) + min(o[1], 4 - o[1]) + o[2]))

    def group_copy(index, dz):
        device, piece = across(*places[index], dz)
        slot = dz * per + index
        return remote(half.at[piece], group_in.at[slot], many_sem.at[0], group_recv.at[slot], device)

    def group_arrive(slot):
        return remote(
            group_in.at[slot], group_in.at[slot], many_sem.at[0], group_recv.at[slot], partner
        )

    def group_add(slot, carry):
        group_arrive(slot).wait_recv()
        return carry + group_in[slot].astype(F32)

    for index in range(2):
        pair_copy(index).wait_recv()
        span = slice(index * CH, (index + 1) * CH)
        total = part[span, :] + pair_in[span, :].astype(F32)
        half[index * per : (index + 1) * per] = total.astype(BF16).reshape(per, CHUNK, CH)
        if index == 0:
            pl.semaphore_wait(twin_sem, 1)
        turn = (z_lo + index) % 2
        for place in range(per - 1):
            group_copy(place, turn).start()

        @pl.when(turn == 1)
        def _():
            group_copy(per - 1, 1).start()

    for copy in cot_copies[:8] + ft_copies:
        copy.start()
    own_copies[2].wait()
    mix(bo, weight_ref, out_ref)
    chunk = lax.fori_loop(0, per - 1, group_add, half[spot].astype(F32))
    chunk = lax.fori_loop(per, GROUP, group_add, chunk)
    zbuf[z_hi] = chunk.astype(BF16)
    pl.semaphore_wait(leap_sem, 2)

    def z_copy(step):
        return remote(
            zbuf.at[z_hi], zbuf.at[z_hi], many_sem.at[1], z_recv.at[z_hi],
            far_device((z_hi + step) % ZFAR),
        )

    def z_wait(step, carry):
        source = (z_hi + step) % ZFAR
        remote(
            zbuf.at[source], zbuf.at[source], many_sem.at[1], z_recv.at[source], far_device(source)
        ).wait_recv()
        return carry

    for step in (4, 3, 5, 2, 6, 1, 7):
        z_copy(step).start()
    for index in range(2):
        cot_arrive[index].wait_recv()
        cot_copies[8 + index].start()
    for copy in cot_arrive[2:] + ft_copies:
        copy.wait_recv()
    fill_basis_grad(cw, weight_ref, bg)
    fill_reversed(ft, north, south, rt)
    adjoint(rt, bg, wedge, acc, grad_ref)
    lax.fori_loop(1, ZFAR, z_wait, 0)
    chunk = zbuf[0].astype(F32)
    for source in range(1, ZFAR):
        chunk = chunk + zbuf[source].astype(F32)
    sum_ref[core, spot] = chunk.astype(BF16)

    def all_copy(step):
        return remote(
            sum_ref.at[core, spot], sum_ref.at[core, spot], many_sem.at[2], all_recv.at[step],
            across(*offsets[step])[0],
        )

    def near_copy(index):
        return remote(
            sum_ref.at[core, index], sum_ref.at[core, index], many_sem.at[3], many_sem.at[4], partner
        )

    for step in range(GROUP - 1):
        all_copy(step).start()
    near_copy(spot).start()
    for copy in feat_copies + cot_copies + ft_copies:
        copy.wait_send()
    for index in range(2):
        pair_copy(index).wait_send()
    remote(
        half.at[0 : GROUP - 1], group_in.at[0 : GROUP - 1], many_sem.at[0], group_recv.at[0], partner
    ).wait_send()
    remote(
        zbuf.at[0 : ZFAR - 1], zbuf.at[0 : ZFAR - 1], many_sem.at[1], z_recv.at[0], partner
    ).wait_send()
    for step in range(GROUP - 1):
        dx, dy, dz = offsets[step]
        source = across(4 - dx, 4 - dy, dz)[1]
        remote(
            sum_ref.at[core, source], sum_ref.at[core, source], many_sem.at[2], all_recv.at[step],
            partner,
        ).wait_recv()
        near_copy(source).start()
    remote(
        sum_ref.at[core, 0 : GROUP - 1], sum_ref.at[core, 0 : GROUP - 1], many_sem.at[2],
        all_recv.at[0], partner,
    ).wait_send()
    near_all = remote(
        sum_ref.at[core], sum_ref.at[1 - core], many_sem.at[3], many_sem.at[4], partner
    )
    near_all.wait_send()
    near_all.wait_recv()


def layer(features, cotangent, weight, filter_taps, lat_ext, lon_count):
    dma = pltpu.SemaphoreType.DMA
    vmem = pl.BlockSpec(memory_space=pltpu.VMEM)
    anywhere = pl.BlockSpec(memory_space=pl.ANY)
    return pl.pallas_call(
        layer_kernel,
        out_shape=[
            pltpu.VMEM((ROWS, WIDE, CH), BF16),
            pltpu.VMEM((ROWS, WIDE, CH), BF16),
            pltpu.VMEM((2, GROUP, CHUNK, CH), BF16),
        ],
        in_specs=[anywhere] * 6,
        out_specs=[vmem, vmem, vmem],
        scratch_shapes=[
            pltpu.VMEM((SPAN, LANES, CH), BF16),
            pltpu.VMEM((SPAN, LANES, CH), BF16),
            pltpu.VMEM((BASES, CH, CH), BF16),
            pltpu.VMEM((ROWS, TAPS, BASES, 2 * HALF), BF16),
            pltpu.SMEM((ROWS,), jnp.int32),
            pltpu.SMEM((ROWS,), jnp.int32),
            pltpu.VMEM((SPAN, TAPS, 8, LANES), F32),
            pltpu.VMEM((SPAN, TAPS, 8, LANES), F32),
            pltpu.VMEM((ROWS, BASES * WIDE, TAPS * LANES), BF16),
            pltpu.VMEM((BASES, ROWS * WIDE, CH), BF16),
            pltpu.VMEM((SPAN, BASES * LANES, CH), BF16),
            pltpu.VMEM((ROWS * WIDE, BASES * LANES), BF16),
            pltpu.VMEM((ROWS * WIDE, CH), F32),
            pltpu.VMEM((2 * CH, CH), F32),
            pltpu.VMEM((2 * CH, CH), BF16),
            pltpu.VMEM((2 * CH, CH), BF16),
            pltpu.VMEM((GROUP, CHUNK, CH), BF16),
            pltpu.VMEM((GROUP, CHUNK, CH), BF16),
            pltpu.VMEM((ZFAR, CHUNK, CH), BF16),
            dma((6,)),
            dma((10,)), dma((10,)), dma((10,)), dma((10,)), dma((2,)), dma((2,)), dma((2,)), dma((2,)),
            dma((GROUP,)), dma((ZFAR,)), dma((GROUP,)), dma((5,)),
            *[pltpu.SemaphoreType.REGULAR] * 5,
        ],
        compiler_params=pltpu.CompilerParams(collective_id=0, has_side_effects=True),
    )(features, cotangent, weight, filter_taps, lat_ext, lon_count)


PIECES = 8


def write_kernel(scale, out_ref, grad_ref, sum_ref, out_any, grad_any, total_any, wide, sem):
    copies = [
        pltpu.make_async_copy(out_ref, out_any, sem.at[PIECES]),
        pltpu.make_async_copy(grad_ref, grad_any, sem.at[PIECES + 1]),
    ]
    for copy in copies:
        copy.start()
    per = 2 * GROUP // PIECES
    for index in range(PIECES):
        side, first = (index * per) // GROUP, (index * per) % GROUP
        wide[side, first : first + per] = sum_ref[side, first : first + per].astype(F32) * scale
        copy = pltpu.make_async_copy(
            wide.at[side, first : first + per], total_any.at[side, first : first + per], sem.at[index]
        )
        copy.start()
        copies.append(copy)
    for copy in copies:
        copy.wait()


def write(scale, output, grad, total):
    vmem = pl.BlockSpec(memory_space=pltpu.VMEM)
    anywhere = pl.BlockSpec(memory_space=pl.ANY)
    return pl.pallas_call(
        lambda *refs: write_kernel(scale, *refs),
        out_shape=[
            jax.ShapeDtypeStruct(output.shape, BF16),
            jax.ShapeDtypeStruct(grad.shape, BF16),
            jax.ShapeDtypeStruct(total.shape, F32),
        ],
        in_specs=[vmem, vmem, vmem],
        out_specs=[anywhere, anywhere, anywhere],
        scratch_shapes=[pltpu.VMEM(total.shape, F32), pltpu.SemaphoreType.DMA((PIECES + 2,))],
        name="write",
    )(*(pltpu.with_memory_space_constraint(held, pltpu.VMEM) for held in (output, grad, total)))


def per_device(features, cotangent, weight, filter_taps, lat_ext, lon_count):
    taps = jnp.transpose(filter_taps, (0, 2, 1, 3))
    output, field_grad, total = layer(features, cotangent, weight, taps, lat_ext, lon_count)
    cells = LATS * ROWS * LONS * WIDE
    output, field_grad, total = write(1.0 / math.sqrt(cells), output, field_grad, total)
    return (output, field_grad, total.reshape(BASES, CH, CH))


def solution(mesh):
    in_specs = (
        P("lat", "lon", None),
        P("lat", "lon", None),
        P(),
        P("lat", None, None, None),
        P("lat"),
        P("lat"),
    )
    out_specs = (P("lat", "lon", None), P("lat", "lon", None), P())
    return jax.shard_map(
        per_device, mesh=mesh, in_specs=in_specs, out_specs=out_specs, check_vma=False
    )
```

```python
import math

import jax
import jax.numpy as jnp
from jax import lax
from jax.experimental import pallas as pl
from jax.experimental.pallas import tpu as pltpu
from jax.sharding import PartitionSpec as P

MESH = pl.DeviceIdType.MESH
GROUP = 32
ZLEN = 16
ZFAR = 8
CHUNK = 16
LATS = 16
LONS = 32
ROWS = 4
REACH = 2
TAPS = 5
WIDE = 32
HALF = 32
BASES = 4
CH = 256
SPAN = ROWS + 2 * REACH
LANES = 128
BF16 = jnp.bfloat16
F32 = jnp.float32


def fill_filters(taps_ref, lat_ref, lon_ref, ft):
    lon_dist = jnp.abs(lax.broadcasted_iota(jnp.int32, (BASES, 2 * HALF), 1) - HALF)
    ft[REACH : REACH + ROWS] = jnp.zeros((ROWS, TAPS, 8, LANES), F32)
    for row in range(ROWS):
        ext, count = lat_ref[row], lon_ref[row]
        size = jnp.full((BASES, 2 * HALF), (2 * ext - 1) * (2 * count - 1), jnp.int32).astype(F32)
        guess = lax.rsqrt(size)
        scale = guess * (1.5 - 0.5 * size * guess * guess)
        scale = jnp.where(lon_dist < count, scale, 0.0)
        for tap in range(TAPS):
            held = jnp.where(abs(tap - REACH) < ext, scale, 0.0)
            taps = taps_ref[row, tap].astype(F32) * held
            ft[REACH + row, tap, 0:BASES, 0 : 2 * HALF] = taps.astype(BF16).astype(F32)


def slanted(base):
    return pltpu.roll(jnp.broadcast_to(base, (WIDE, LANES)), 0, 1, stride=1, stride_axis=0)


def fill_forward(ft, north, south, bands):
    def one(basis, carry):
        start = pl.multiple_of(basis * WIDE, WIDE)
        for row in range(ROWS):
            for tap in range(TAPS):
                line = row + tap
                base = ft[REACH + row, tap, pl.ds(basis, 1), :]
                if line < REACH:
                    base = base * north
                if line >= REACH + ROWS:
                    base = base * south
                bands[row, pl.ds(start, WIDE), tap * LANES : (tap + 1) * LANES] = slanted(
                    base
                ).astype(BF16)
        return carry

    lax.fori_loop(0, BASES, one, 0)


def convolve(bands, fw, bo, first):
    span = pl.ds(pl.multiple_of(first * WIDE, 2 * WIDE), 2 * WIDE)
    for row in range(ROWS):
        patch = fw[row : row + TAPS].reshape(TAPS * LANES, CH)
        sums = jnp.dot(bands[row, span, :], patch, preferred_element_type=F32).astype(BF16)
        bo[pl.ds(first, 2), row * WIDE : (row + 1) * WIDE, :] = sums.reshape(2, WIDE, CH)


def mix(bo, weight_ref, out_ref):
    total = jnp.dot(bo[0], weight_ref[0], preferred_element_type=F32)
    for basis in range(1, BASES):
        total = total + jnp.dot(bo[basis], weight_ref[basis], preferred_element_type=F32)
    out_ref[...] = total.astype(BF16).reshape(ROWS, WIDE, CH)


def fill_basis_grad(cw, weight_ref, bg):
    cells = cw[...].reshape(SPAN * LANES, CH)

    def one(basis, carry):
        grad = lax.dot_general(
            cells, weight_ref[basis], (((1,), (1,)), ((), ())), preferred_element_type=F32
        )
        start = pl.multiple_of(basis * LANES, LANES)
        bg[:, pl.ds(start, LANES), :] = grad.astype(BF16).reshape(SPAN, LANES, CH)
        return carry

    lax.fori_loop(0, BASES, one, 0)


def fill_reversed(ft, north, south, rt):
    first = lax.broadcasted_iota(jnp.int32, (LANES, LANES), 0)
    second = lax.broadcasted_iota(jnp.int32, (LANES, LANES), 1)
    flip = jnp.where(first + second == 2 * HALF, 1.0, 0.0).astype(BF16)
    flat = ft[...].reshape(SPAN * TAPS * 8, LANES).astype(BF16)
    turned = jnp.dot(flat, flip, preferred_element_type=F32)
    rt[...] = turned.reshape(SPAN, TAPS, 8, LANES)
    rt[0:REACH] = rt[0:REACH] * north
    rt[REACH + ROWS :] = rt[REACH + ROWS :] * south


def fill_adjoint(rt, wedge):
    def one(basis, carry):
        for row in range(ROWS):
            for tap in range(TAPS):
                line = row + TAPS - 1 - tap
                base = rt[line, tap, pl.ds(basis, 1), :]
                start = pl.multiple_of((line * BASES + basis) * LANES, LANES)
                wedge[row * WIDE : (row + 1) * WIDE, pl.ds(start, LANES)] = slanted(base).astype(BF16)
        return carry

    lax.fori_loop(0, BASES, one, 0)


def adjoint(wedge, bg, grad_ref):
    flat = bg[...].reshape(SPAN * BASES * LANES, CH)
    total = jnp.dot(wedge[...], flat, preferred_element_type=F32)
    grad_ref[...] = total.astype(BF16).reshape(ROWS, WIDE, CH)


def layer_kernel(
    feat_any, cot_any, weight_any, taps_any, lat_any, lon_any,
    out_ref, grad_ref, sum_ref,
    fw, cw, weight_ref, taps_ref, lat_ref, lon_ref, ft, rt, bands, bo, bg, wedge, part, pair_out, pair_in, half, group_in, zbuf,
    own_sem, feat_send, feat_recv, cot_send, cot_recv, ft_send, ft_recv, pair_send, pair_recv,
    group_recv, z_recv, all_recv, many_sem,
    hop_sem, leap_sem, step_sem, cross_sem, twin_sem,
):
    lat = lax.axis_index("lat")
    lon = lax.axis_index("lon")
    core = lat % 2
    y_lo = (lat // 2) % 2
    x = lat // 4
    z = lon % ZLEN
    z_lo = z % 2
    z_hi = z // 2
    y_hi = lon // ZLEN
    spot = z_lo * 16 + x * 4 + y_hi * 2 + y_lo
    partner = (lat + 1 - 2 * core, lon)

    def across(dx, dy, dz):
        far_x, far_y, far_z = (x + dx) % 4, (y_hi * 2 + y_lo + dy) % 4, (z_lo + dz) % 2
        device = (far_x * 4 + (far_y % 2) * 2 + core, (far_y // 2) * ZLEN + z_hi * 2 + far_z)
        return device, far_z * 16 + far_x * 4 + far_y

    def z_device(index):
        return (lat, y_hi * ZLEN + index)

    def far_device(index):
        return z_device(index * 2 + z_lo)

    def beside(up, right):
        return ((lat + LATS + up) % LATS, (lon + LONS + right) % LONS)

    away = 2 * core - 1
    ways = [(away, 1), (away, -1), (0, 1), (0, -1), (1, 0), (-1, 0)]

    def remote(src, dst, send, recv, device):
        return pltpu.make_async_remote_copy(
            src_ref=src, dst_ref=dst, send_sem=send, recv_sem=recv,
            device_id=device, device_id_type=MESH,
        )

    def signal(sem, device):
        pl.semaphore_signal(sem, inc=1, device_id=device, device_id_type=MESH)

    steps = [(1, 0), (3, 0), (0, 1), (0, 3)]
    barrier = pltpu.get_barrier_semaphore()
    for way in ways:
        signal(barrier, beside(*way))
    for dx, dy in steps:
        signal(barrier, across(dx, dy, 0)[0])
    signal(barrier, z_device((z + 2) % ZLEN))
    signal(barrier, z_device((z + ZLEN - 2) % ZLEN))

    north = jnp.where(lat > 0, 1.0, 0.0)
    south = jnp.where(lat < LATS - 1, 1.0, 0.0)
    inner = slice(REACH, REACH + ROWS)
    middle = slice(WIDE, 2 * WIDE)
    own_copies = [
        pltpu.make_async_copy(feat_any, fw.at[inner, middle], own_sem.at[0]),
        pltpu.make_async_copy(cot_any, cw.at[inner, middle], own_sem.at[1]),
        pltpu.make_async_copy(weight_any, weight_ref, own_sem.at[2]),
        pltpu.make_async_copy(taps_any, taps_ref, own_sem.at[3]),
        pltpu.make_async_copy(lat_any, lat_ref, own_sem.at[4]),
        pltpu.make_async_copy(lon_any, lon_ref, own_sem.at[5]),
    ]
    for copy in own_copies:
        copy.start()
    pl.semaphore_wait(barrier, len(ways) + len(steps) + 2)

    def rows(window, start, left):
        return window.at[pl.ds(start, REACH), left : left + WIDE]

    common, single = REACH * (1 - core), REACH * core
    far = REACH + ROWS

    def halo(source, window, send, recv):
        out, arrive = [], []

        def add(src, start, landing, left, device):
            index = len(out)
            out.append(remote(src, rows(window, start, left), send.at[index], recv.at[index], device))
            place = rows(window, landing, left)
            arrive.append(remote(place, place, send.at[index], recv.at[index], partner))

        for right in (1, -1):
            start = REACH + common
            add(source.at[pl.ds(common, REACH)], start, start, WIDE * (1 - right), beside(0, right))
        for right in (1, -1):
            add(
                source.at[pl.ds(single, REACH)], far * (1 - core), far * core, WIDE * (1 - right),
                beside(away, right),
            )
        for right in (1, -1):
            start = REACH + single
            add(source.at[pl.ds(single, REACH)], start, start, WIDE * (1 - right), beside(0, right))
        add(source.at[ROWS - REACH :], 0, 0, WIDE, beside(1, 0))
        add(source.at[0:REACH], far, far, WIDE, beside(-1, 0))
        for right in (1, -1):
            left = WIDE * (1 - right)
            add(rows(window, REACH + common, left), far * core, far * (1 - core), left, partner)
        return out, arrive

    feat_copies, feat_arrive = halo(feat_any, fw, feat_send, feat_recv)
    cot_copies, cot_arrive = halo(cot_any, cw, cot_send, cot_recv)
    ft_copies = [
        remote(ft.at[ROWS : ROWS + REACH], ft.at[0:REACH], ft_send.at[0], ft_recv.at[0], beside(1, 0)),
        remote(ft.at[REACH : 2 * REACH], ft.at[REACH + ROWS :], ft_send.at[1], ft_recv.at[1], beside(-1, 0)),
    ]
    for copy in feat_copies[:8]:
        copy.start()
    for dx, dy in steps:
        signal(step_sem, across(dx, dy, 0)[0])
    signal(hop_sem, z_device((z + 2) % ZLEN))
    signal(hop_sem, z_device((z + ZLEN - 2) % ZLEN))
    blank = jnp.zeros((SPAN, LANES - 3 * WIDE, CH), BF16)
    fw[:, 3 * WIDE :, :] = blank
    cw[:, 3 * WIDE :, :] = blank
    for copy in own_copies[3:]:
        copy.wait()
    fill_filters(taps_ref, lat_ref, lon_ref, ft)
    fill_forward(ft, north, south, bands)
    wedge[...] = jnp.zeros(wedge.shape, BF16)
    pl.semaphore_wait(step_sem, len(steps))
    signal(cross_sem, across(2, 0, 0)[0])
    signal(cross_sem, across(0, 2, 0)[0])
    pl.semaphore_wait(hop_sem, 2)
    signal(leap_sem, z_device((z + 4) % ZLEN))
    signal(leap_sem, z_device((z + ZLEN - 4) % ZLEN))
    for index in range(2):
        feat_arrive[index].wait_recv()
        feat_copies[8 + index].start()
    for copy in feat_arrive[2:]:
        copy.wait_recv()
    own_copies[0].wait()
    own_copies[1].wait()
    convolve(bands, fw, bo, (1 - core) * 2)

    cells = cw[inner, middle, :].reshape(ROWS * WIDE, CH)

    def share(basis):
        return lax.dot_general(bo[basis], cells, (((0,), (0,)), ((), ())), preferred_element_type=F32)

    def pair_copy(index):
        span = pl.ds(pl.multiple_of(index * CH, CH), CH)
        return remote(pair_out.at[span], pair_in.at[span], pair_send.at[index], pair_recv.at[index], partner)

    for index in range(2):
        pair_out[index * CH : (index + 1) * CH, :] = share((1 - core) * 2 + index).astype(BF16)
        pair_copy(index).start()
    pl.semaphore_wait(cross_sem, 2)
    signal(twin_sem, across(0, 0, 1)[0])
    convolve(bands, fw, bo, core * 2)
    for index in range(2):
        part[index * CH : (index + 1) * CH, :] = share(core * 2 + index)
    per = GROUP // 2
    places = [(dx, dy) for dx in (0, 1, 2, 3) for dy in (0, 1, 2, 3)]
    places.sort(key=lambda p: -(min(p[0], 4 - p[0]) + min(p[1], 4 - p[1])))
    offsets = [(dx, dy, dz) for dx, dy in places for dz in (0, 1)]
    offsets.sort(key=lambda o: -(min(o[0], 4 - o[0]) + min(o[1], 4 - o[1]) + o[2]))

    def group_copy(index, dz):
        device, piece = across(*places[index], dz)
        slot = dz * per + index
        return remote(half.at[piece], group_in.at[slot], many_sem.at[0], group_recv.at[slot], device)

    def group_arrive(slot):
        return remote(
            group_in.at[slot], group_in.at[slot], many_sem.at[0], group_recv.at[slot], partner
        )

    def group_add(slot, carry):
        group_arrive(slot).wait_recv()
        return carry + group_in[slot].astype(F32)

    for index in range(2):
        pair_copy(index).wait_recv()
        span = slice(index * CH, (index + 1) * CH)
        total = part[span, :] + pair_in[span, :].astype(F32)
        half[index * per : (index + 1) * per] = total.astype(BF16).reshape(per, CHUNK, CH)
        if index == 0:
            pl.semaphore_wait(twin_sem, 1)
        turn = (z_lo + index) % 2
        for place in range(per - 1):
            group_copy(place, turn).start()

        @pl.when(turn == 1)
        def _():
            group_copy(per - 1, 1).start()

    for copy in cot_copies[:8] + ft_copies:
        copy.start()
    own_copies[2].wait()
    mix(bo, weight_ref, out_ref)
    chunk = lax.fori_loop(0, per - 1, group_add, half[spot].astype(F32))
    chunk = lax.fori_loop(per, GROUP, group_add, chunk)
    zbuf[z_hi] = chunk.astype(BF16)
    pl.semaphore_wait(leap_sem, 2)

    def z_copy(step):
        return remote(
            zbuf.at[z_hi], zbuf.at[z_hi], many_sem.at[1], z_recv.at[z_hi],
            far_device((z_hi + step) % ZFAR),
        )

    def z_wait(step, carry):
        source = (z_hi + step) % ZFAR
        remote(
            zbuf.at[source], zbuf.at[source], many_sem.at[1], z_recv.at[source], far_device(source)
        ).wait_recv()
        return carry

    for step in (4, 3, 5, 2, 6, 1, 7):
        z_copy(step).start()
    for copy in ft_copies:
        copy.wait_recv()
    for index in range(2):
        cot_arrive[index].wait_recv()
        cot_copies[8 + index].start()
    fill_reversed(ft, north, south, rt)
    fill_adjoint(rt, wedge)
    for copy in cot_arrive[2:]:
        copy.wait_recv()
    fill_basis_grad(cw, weight_ref, bg)
    adjoint(wedge, bg, grad_ref)
    lax.fori_loop(1, ZFAR, z_wait, 0)
    chunk = zbuf[0].astype(F32)
    for source in range(1, ZFAR):
        chunk = chunk + zbuf[source].astype(F32)
    sum_ref[core, spot] = chunk.astype(BF16)

    def all_copy(step):
        return remote(
            sum_ref.at[core, spot], sum_ref.at[core, spot], many_sem.at[2], all_recv.at[step],
            across(*offsets[step])[0],
        )

    def near_copy(index):
        return remote(
            sum_ref.at[core, index], sum_ref.at[core, index], many_sem.at[3], many_sem.at[4], partner
        )

    for step in range(GROUP - 1):
        all_copy(step).start()
    near_copy(spot).start()
    for copy in feat_copies + cot_copies + ft_copies:
        copy.wait_send()
    for index in range(2):
        pair_copy(index).wait_send()
    remote(
        half.at[0 : GROUP - 1], group_in.at[0 : GROUP - 1], many_sem.at[0], group_recv.at[0], partner
    ).wait_send()
    remote(
        zbuf.at[0 : ZFAR - 1], zbuf.at[0 : ZFAR - 1], many_sem.at[1], z_recv.at[0], partner
    ).wait_send()
    for step in range(GROUP - 1):
        dx, dy, dz = offsets[step]
        source = across(4 - dx, 4 - dy, dz)[1]
        remote(
            sum_ref.at[core, source], sum_ref.at[core, source], many_sem.at[2], all_recv.at[step],
            partner,
        ).wait_recv()
        near_copy(source).start()
    remote(
        sum_ref.at[core, 0 : GROUP - 1], sum_ref.at[core, 0 : GROUP - 1], many_sem.at[2],
        all_recv.at[0], partner,
    ).wait_send()
    near_all = remote(
        sum_ref.at[core], sum_ref.at[1 - core], many_sem.at[3], many_sem.at[4], partner
    )
    near_all.wait_send()
    near_all.wait_recv()


def layer(features, cotangent, weight, filter_taps, lat_ext, lon_count):
    dma = pltpu.SemaphoreType.DMA
    vmem = pl.BlockSpec(memory_space=pltpu.VMEM)
    anywhere = pl.BlockSpec(memory_space=pl.ANY)
    return pl.pallas_call(
        layer_kernel,
        out_shape=[
            pltpu.VMEM((ROWS, WIDE, CH), BF16),
            pltpu.VMEM((ROWS, WIDE, CH), BF16),
            pltpu.VMEM((2, GROUP, CHUNK, CH), BF16),
        ],
        in_specs=[anywhere] * 6,
        out_specs=[vmem, vmem, vmem],
        scratch_shapes=[
            pltpu.VMEM((SPAN, LANES, CH), BF16),
            pltpu.VMEM((SPAN, LANES, CH), BF16),
            pltpu.VMEM((BASES, CH, CH), BF16),
            pltpu.VMEM((ROWS, TAPS, BASES, 2 * HALF), BF16),
            pltpu.SMEM((ROWS,), jnp.int32),
            pltpu.SMEM((ROWS,), jnp.int32),
            pltpu.VMEM((SPAN, TAPS, 8, LANES), F32),
            pltpu.VMEM((SPAN, TAPS, 8, LANES), F32),
            pltpu.VMEM((ROWS, BASES * WIDE, TAPS * LANES), BF16),
            pltpu.VMEM((BASES, ROWS * WIDE, CH), BF16),
            pltpu.VMEM((SPAN, BASES * LANES, CH), BF16),
            pltpu.VMEM((ROWS * WIDE, SPAN * BASES * LANES), BF16),
            pltpu.VMEM((2 * CH, CH), F32),
            pltpu.VMEM((2 * CH, CH), BF16),
            pltpu.VMEM((2 * CH, CH), BF16),
            pltpu.VMEM((GROUP, CHUNK, CH), BF16),
            pltpu.VMEM((GROUP, CHUNK, CH), BF16),
            pltpu.VMEM((ZFAR, CHUNK, CH), BF16),
            dma((6,)),
            dma((10,)), dma((10,)), dma((10,)), dma((10,)), dma((2,)), dma((2,)), dma((2,)), dma((2,)),
            dma((GROUP,)), dma((ZFAR,)), dma((GROUP,)), dma((5,)),
            *[pltpu.SemaphoreType.REGULAR] * 5,
        ],
        compiler_params=pltpu.CompilerParams(collective_id=0, has_side_effects=True),
    )(features, cotangent, weight, filter_taps, lat_ext, lon_count)


PIECES = 8


def write_kernel(scale, out_ref, grad_ref, sum_ref, out_any, grad_any, total_any, wide, sem):
    copies = [
        pltpu.make_async_copy(out_ref, out_any, sem.at[PIECES]),
        pltpu.make_async_copy(grad_ref, grad_any, sem.at[PIECES + 1]),
    ]
    for copy in copies:
        copy.start()
    per = 2 * GROUP // PIECES
    for index in range(PIECES):
        side, first = (index * per) // GROUP, (index * per) % GROUP
        wide[side, first : first + per] = sum_ref[side, first : first + per].astype(F32) * scale
        copy = pltpu.make_async_copy(
            wide.at[side, first : first + per], total_any.at[side, first : first + per], sem.at[index]
        )
        copy.start()
        copies.append(copy)
    for copy in copies:
        copy.wait()


def write(scale, output, grad, total):
    vmem = pl.BlockSpec(memory_space=pltpu.VMEM)
    anywhere = pl.BlockSpec(memory_space=pl.ANY)
    return pl.pallas_call(
        lambda *refs: write_kernel(scale, *refs),
        out_shape=[
            jax.ShapeDtypeStruct(output.shape, BF16),
            jax.ShapeDtypeStruct(grad.shape, BF16),
            jax.ShapeDtypeStruct(total.shape, F32),
        ],
        in_specs=[vmem, vmem, vmem],
        out_specs=[anywhere, anywhere, anywhere],
        scratch_shapes=[pltpu.VMEM(total.shape, F32), pltpu.SemaphoreType.DMA((PIECES + 2,))],
        name="write",
    )(*(pltpu.with_memory_space_constraint(held, pltpu.VMEM) for held in (output, grad, total)))


def per_device(features, cotangent, weight, filter_taps, lat_ext, lon_count):
    taps = jnp.transpose(filter_taps, (0, 2, 1, 3))
    output, field_grad, total = layer(features, cotangent, weight, taps, lat_ext, lon_count)
    cells = LATS * ROWS * LONS * WIDE
    output, field_grad, total = write(1.0 / math.sqrt(cells), output, field_grad, total)
    return (output, field_grad, total.reshape(BASES, CH, CH))


def solution(mesh):
    in_specs = (
        P("lat", "lon", None),
        P("lat", "lon", None),
        P(),
        P("lat", None, None, None),
        P("lat"),
        P("lat"),
    )
    out_specs = (P("lat", "lon", None), P("lat", "lon", None), P())
    return jax.shard_map(
        per_device, mesh=mesh, in_specs=in_specs, out_specs=out_specs, check_vma=False
    )
```

```python
import math

import jax
import jax.numpy as jnp
from jax import lax
from jax.experimental import pallas as pl
from jax.experimental.pallas import tpu as pltpu
from jax.sharding import PartitionSpec as P

MESH = pl.DeviceIdType.MESH
GROUP = 32
ZLEN = 16
ZFAR = 8
CHUNK = 16
LATS = 16
LONS = 32
ROWS = 4
REACH = 2
TAPS = 5
WIDE = 32
HALF = 32
BASES = 4
CH = 256
SPAN = ROWS + 2 * REACH
LANES = 128
BF16 = jnp.bfloat16
F32 = jnp.float32


def fill_filters(taps_ref, lat_ref, lon_ref, ft):
    lon_dist = jnp.abs(lax.broadcasted_iota(jnp.int32, (BASES, 2 * HALF), 1) - HALF)
    ft[REACH : REACH + ROWS] = jnp.zeros((ROWS, TAPS, 8, LANES), F32)
    for row in range(ROWS):
        ext, count = lat_ref[row], lon_ref[row]
        size = jnp.full((BASES, 2 * HALF), (2 * ext - 1) * (2 * count - 1), jnp.int32).astype(F32)
        guess = lax.rsqrt(size)
        scale = guess * (1.5 - 0.5 * size * guess * guess)
        scale = jnp.where(lon_dist < count, scale, 0.0)
        for tap in range(TAPS):
            held = jnp.where(abs(tap - REACH) < ext, scale, 0.0)
            taps = taps_ref[row, tap].astype(F32) * held
            ft[REACH + row, tap, 0:BASES, 0 : 2 * HALF] = taps.astype(BF16).astype(F32)


def slanted(base):
    return pltpu.roll(jnp.broadcast_to(base, (WIDE, LANES)), 0, 1, stride=1, stride_axis=0)


def fill_forward(ft, north, south, bands):
    def one(basis, carry):
        start = pl.multiple_of(basis * WIDE, WIDE)
        for row in range(ROWS):
            for tap in range(TAPS):
                line = row + tap
                base = ft[REACH + row, tap, pl.ds(basis, 1), :]
                if line < REACH:
                    base = base * north
                if line >= REACH + ROWS:
                    base = base * south
                bands[row, pl.ds(start, WIDE), tap * LANES : (tap + 1) * LANES] = slanted(
                    base
                ).astype(BF16)
        return carry

    lax.fori_loop(0, BASES, one, 0)


def convolve(bands, fw, bo, first):
    span = pl.ds(pl.multiple_of(first * WIDE, 2 * WIDE), 2 * WIDE)
    for row in range(ROWS):
        patch = fw[row : row + TAPS].reshape(TAPS * LANES, CH)
        sums = jnp.dot(bands[row, span, :], patch, preferred_element_type=F32).astype(BF16)
        bo[pl.ds(first, 2), row * WIDE : (row + 1) * WIDE, :] = sums.reshape(2, WIDE, CH)


def mix(bo, weight_ref, out_ref):
    total = jnp.dot(bo[0], weight_ref[0], preferred_element_type=F32)
    for basis in range(1, BASES):
        total = total + jnp.dot(bo[basis], weight_ref[basis], preferred_element_type=F32)
    out_ref[...] = total.astype(BF16).reshape(ROWS, WIDE, CH)


def fill_basis_grad(cw, weight_ref, bg):
    cells = cw[...].reshape(SPAN * LANES, CH)

    def one(basis, carry):
        grad = lax.dot_general(
            cells, weight_ref[basis], (((1,), (1,)), ((), ())), preferred_element_type=F32
        )
        start = pl.multiple_of(basis * LANES, LANES)
        bg[:, pl.ds(start, LANES), :] = grad.astype(BF16).reshape(SPAN, LANES, CH)
        return carry

    lax.fori_loop(0, BASES, one, 0)


def fill_reversed(ft, north, south, rt):
    first = lax.broadcasted_iota(jnp.int32, (LANES, LANES), 0)
    second = lax.broadcasted_iota(jnp.int32, (LANES, LANES), 1)
    flip = jnp.where(first + second == 2 * HALF, 1.0, 0.0).astype(BF16)
    flat = ft[...].reshape(SPAN * TAPS * 8, LANES).astype(BF16)
    turned = jnp.dot(flat, flip, preferred_element_type=F32)
    rt[...] = turned.reshape(SPAN, TAPS, 8, LANES)
    rt[0:REACH] = rt[0:REACH] * north
    rt[REACH + ROWS :] = rt[REACH + ROWS :] * south


def fill_adjoint(rt, wedge):
    def one(basis, carry):
        for row in range(ROWS):
            for tap in range(TAPS):
                line = row + TAPS - 1 - tap
                base = rt[line, tap, pl.ds(basis, 1), :]
                start = pl.multiple_of((line * BASES + basis) * LANES, LANES)
                wedge[row * WIDE : (row + 1) * WIDE, pl.ds(start, LANES)] = slanted(base).astype(BF16)
        return carry

    lax.fori_loop(0, BASES, one, 0)


def adjoint(wedge, bg, grad_ref):
    flat = bg[...].reshape(SPAN * BASES * LANES, CH)
    total = jnp.dot(wedge[...], flat, preferred_element_type=F32)
    grad_ref[...] = total.astype(BF16).reshape(ROWS, WIDE, CH)


def layer_kernel(
    feat_any, cot_any, weight_any, taps_any, lat_any, lon_any,
    out_ref, grad_ref, sum_ref,
    fw, cw, weight_ref, taps_ref, lat_ref, lon_ref, ft, rt, bands, bo, bg, wedge, part, pair_out, pair_in, half, group_in, zbuf,
    own_sem, feat_send, feat_recv, cot_send, cot_recv, ft_send, ft_recv, pair_send, pair_recv,
    group_recv, z_recv, all_recv, many_sem,
    hop_sem, leap_sem, step_sem, cross_sem, twin_sem,
):
    lat = lax.axis_index("lat")
    lon = lax.axis_index("lon")
    core = lat % 2
    y_lo = (lat // 2) % 2
    x = lat // 4
    z = lon % ZLEN
    z_lo = z % 2
    z_hi = z // 2
    y_hi = lon // ZLEN
    spot = z_lo * 16 + x * 4 + y_hi * 2 + y_lo
    partner = (lat + 1 - 2 * core, lon)

    def across(dx, dy, dz):
        far_x, far_y, far_z = (x + dx) % 4, (y_hi * 2 + y_lo + dy) % 4, (z_lo + dz) % 2
        device = (far_x * 4 + (far_y % 2) * 2 + core, (far_y // 2) * ZLEN + z_hi * 2 + far_z)
        return device, far_z * 16 + far_x * 4 + far_y

    def z_device(index):
        return (lat, y_hi * ZLEN + index)

    def far_device(index):
        return z_device(index * 2 + z_lo)

    def beside(up, right):
        return ((lat + LATS + up) % LATS, (lon + LONS + right) % LONS)

    away = 2 * core - 1
    ways = [(away, 1), (away, -1), (0, 1), (0, -1), (1, 0), (-1, 0)]

    def remote(src, dst, send, recv, device):
        return pltpu.make_async_remote_copy(
            src_ref=src, dst_ref=dst, send_sem=send, recv_sem=recv,
            device_id=device, device_id_type=MESH,
        )

    def signal(sem, device):
        pl.semaphore_signal(sem, inc=1, device_id=device, device_id_type=MESH)

    steps = [(1, 0), (3, 0), (0, 1), (0, 3)]
    barrier = pltpu.get_barrier_semaphore()
    for way in ways:
        signal(barrier, beside(*way))
    for dx, dy in steps:
        signal(barrier, across(dx, dy, 0)[0])
    signal(barrier, z_device((z + 2) % ZLEN))
    signal(barrier, z_device((z + ZLEN - 2) % ZLEN))

    north = jnp.where(lat > 0, 1.0, 0.0)
    south = jnp.where(lat < LATS - 1, 1.0, 0.0)
    inner = slice(REACH, REACH + ROWS)
    middle = slice(WIDE, 2 * WIDE)
    own_copies = [
        pltpu.make_async_copy(feat_any, fw.at[inner, middle], own_sem.at[0]),
        pltpu.make_async_copy(cot_any, cw.at[inner, middle], own_sem.at[1]),
        pltpu.make_async_copy(weight_any, weight_ref, own_sem.at[2]),
        pltpu.make_async_copy(taps_any, taps_ref, own_sem.at[3]),
        pltpu.make_async_copy(lat_any, lat_ref, own_sem.at[4]),
        pltpu.make_async_copy(lon_any, lon_ref, own_sem.at[5]),
    ]
    for copy in own_copies:
        copy.start()
    pl.semaphore_wait(barrier, len(ways) + len(steps) + 2)

    def rows(window, start, left):
        return window.at[pl.ds(start, REACH), left : left + WIDE]

    common, single = REACH * (1 - core), REACH * core
    far = REACH + ROWS

    def halo(source, window, send, recv):
        out, arrive = [], []

        def add(src, start, landing, left, device):
            index = len(out)
            out.append(remote(src, rows(window, start, left), send.at[index], recv.at[index], device))
            place = rows(window, landing, left)
            arrive.append(remote(place, place, send.at[index], recv.at[index], partner))

        for right in (1, -1):
            start = REACH + common
            add(source.at[pl.ds(common, REACH)], start, start, WIDE * (1 - right), beside(0, right))
        for right in (1, -1):
            add(
                source.at[pl.ds(single, REACH)], far * (1 - core), far * core, WIDE * (1 - right),
                beside(away, right),
            )
        for right in (1, -1):
            start = REACH + single
            add(source.at[pl.ds(single, REACH)], start, start, WIDE * (1 - right), beside(0, right))
        add(source.at[ROWS - REACH :], 0, 0, WIDE, beside(1, 0))
        add(source.at[0:REACH], far, far, WIDE, beside(-1, 0))
        for right in (1, -1):
            left = WIDE * (1 - right)
            add(rows(window, REACH + common, left), far * core, far * (1 - core), left, partner)
        return out, arrive

    feat_copies, feat_arrive = halo(feat_any, fw, feat_send, feat_recv)
    cot_copies, cot_arrive = halo(cot_any, cw, cot_send, cot_recv)
    ft_copies = [
        remote(ft.at[ROWS : ROWS + REACH], ft.at[0:REACH], ft_send.at[0], ft_recv.at[0], beside(1, 0)),
        remote(ft.at[REACH : 2 * REACH], ft.at[REACH + ROWS :], ft_send.at[1], ft_recv.at[1], beside(-1, 0)),
    ]
    for copy in feat_copies[:8]:
        copy.start()
    for dx, dy in steps:
        signal(step_sem, across(dx, dy, 0)[0])
    signal(hop_sem, z_device((z + 2) % ZLEN))
    signal(hop_sem, z_device((z + ZLEN - 2) % ZLEN))
    blank = jnp.zeros((SPAN, LANES - 3 * WIDE, CH), BF16)
    fw[:, 3 * WIDE :, :] = blank
    cw[:, 3 * WIDE :, :] = blank
    for copy in own_copies[3:]:
        copy.wait()
    fill_filters(taps_ref, lat_ref, lon_ref, ft)
    fill_forward(ft, north, south, bands)
    wedge[...] = jnp.zeros(wedge.shape, BF16)
    pl.semaphore_wait(step_sem, len(steps))
    signal(cross_sem, across(2, 0, 0)[0])
    signal(cross_sem, across(0, 2, 0)[0])
    pl.semaphore_wait(hop_sem, 2)
    signal(leap_sem, z_device((z + 4) % ZLEN))
    signal(leap_sem, z_device((z + ZLEN - 4) % ZLEN))
    for index in range(2):
        feat_arrive[index].wait_recv()
        feat_copies[8 + index].start()
    for copy in feat_arrive[2:]:
        copy.wait_recv()
    own_copies[0].wait()
    own_copies[1].wait()
    convolve(bands, fw, bo, (1 - core) * 2)

    cells = cw[inner, middle, :].reshape(ROWS * WIDE, CH)

    def share(basis):
        return lax.dot_general(bo[basis], cells, (((0,), (0,)), ((), ())), preferred_element_type=F32)

    def pair_copy(index):
        span = pl.ds(pl.multiple_of(index * CH, CH), CH)
        return remote(pair_out.at[span], pair_in.at[span], pair_send.at[index], pair_recv.at[index], partner)

    for index in range(2):
        pair_out[index * CH : (index + 1) * CH, :] = share((1 - core) * 2 + index).astype(BF16)
        pair_copy(index).start()
    for copy in cot_copies[:8] + ft_copies:
        copy.start()
    pl.semaphore_wait(cross_sem, 2)
    signal(twin_sem, across(0, 0, 1)[0])
    convolve(bands, fw, bo, core * 2)
    for index in range(2):
        part[index * CH : (index + 1) * CH, :] = share(core * 2 + index)
    per = GROUP // 2
    places = [(dx, dy) for dx in (0, 1, 2, 3) for dy in (0, 1, 2, 3)]
    places.sort(key=lambda p: -(min(p[0], 4 - p[0]) + min(p[1], 4 - p[1])))
    offsets = [(dx, dy, dz) for dx, dy in places for dz in (0, 1)]
    offsets.sort(key=lambda o: -(min(o[0], 4 - o[0]) + min(o[1], 4 - o[1]) + o[2]))

    def group_copy(index, dz):
        device, piece = across(*places[index], dz)
        slot = dz * per + index
        return remote(half.at[piece], group_in.at[slot], many_sem.at[0], group_recv.at[slot], device)

    def group_arrive(slot):
        return remote(
            group_in.at[slot], group_in.at[slot], many_sem.at[0], group_recv.at[slot], partner
        )

    def group_add(slot, carry):
        group_arrive(slot).wait_recv()
        return carry + group_in[slot].astype(F32)

    for index in range(2):
        pair_copy(index).wait_recv()
        span = slice(index * CH, (index + 1) * CH)
        total = part[span, :] + pair_in[span, :].astype(F32)
        half[index * per : (index + 1) * per] = total.astype(BF16).reshape(per, CHUNK, CH)
        if index == 0:
            pl.semaphore_wait(twin_sem, 1)
        turn = (z_lo + index) % 2
        for place in range(per - 1):
            group_copy(place, turn).start()

        @pl.when(turn == 1)
        def _():
            group_copy(per - 1, 1).start()

    own_copies[2].wait()
    mix(bo, weight_ref, out_ref)
    chunk = lax.fori_loop(0, per - 1, group_add, half[spot].astype(F32))
    chunk = lax.fori_loop(per, GROUP, group_add, chunk)
    zbuf[z_hi] = chunk.astype(BF16)
    pl.semaphore_wait(leap_sem, 2)

    def z_copy(step):
        return remote(
            zbuf.at[z_hi], zbuf.at[z_hi], many_sem.at[1], z_recv.at[z_hi],
            far_device((z_hi + step) % ZFAR),
        )

    def z_wait(step, carry):
        source = (z_hi + step) % ZFAR
        remote(
            zbuf.at[source], zbuf.at[source], many_sem.at[1], z_recv.at[source], far_device(source)
        ).wait_recv()
        return carry

    for step in (4, 3, 5, 2, 6, 1, 7):
        z_copy(step).start()
    for copy in ft_copies:
        copy.wait_recv()
    for index in range(2):
        cot_arrive[index].wait_recv()
        cot_copies[8 + index].start()
    fill_reversed(ft, north, south, rt)
    fill_adjoint(rt, wedge)
    for copy in cot_arrive[2:]:
        copy.wait_recv()
    fill_basis_grad(cw, weight_ref, bg)
    adjoint(wedge, bg, grad_ref)
    lax.fori_loop(1, ZFAR, z_wait, 0)
    chunk = zbuf[0].astype(F32)
    for source in range(1, ZFAR):
        chunk = chunk + zbuf[source].astype(F32)
    sum_ref[core, spot] = chunk.astype(BF16)

    def all_copy(step):
        return remote(
            sum_ref.at[core, spot], sum_ref.at[core, spot], many_sem.at[2], all_recv.at[step],
            across(*offsets[step])[0],
        )

    def near_copy(index):
        return remote(
            sum_ref.at[core, index], sum_ref.at[core, index], many_sem.at[3], many_sem.at[4], partner
        )

    for step in range(GROUP - 1):
        all_copy(step).start()
    near_copy(spot).start()
    for copy in feat_copies + cot_copies + ft_copies:
        copy.wait_send()
    for index in range(2):
        pair_copy(index).wait_send()
    remote(
        half.at[0 : GROUP - 1], group_in.at[0 : GROUP - 1], many_sem.at[0], group_recv.at[0], partner
    ).wait_send()
    remote(
        zbuf.at[0 : ZFAR - 1], zbuf.at[0 : ZFAR - 1], many_sem.at[1], z_recv.at[0], partner
    ).wait_send()
    for step in range(GROUP - 1):
        dx, dy, dz = offsets[step]
        source = across(4 - dx, 4 - dy, dz)[1]
        remote(
            sum_ref.at[core, source], sum_ref.at[core, source], many_sem.at[2], all_recv.at[step],
            partner,
        ).wait_recv()
        near_copy(source).start()
    remote(
        sum_ref.at[core, 0 : GROUP - 1], sum_ref.at[core, 0 : GROUP - 1], many_sem.at[2],
        all_recv.at[0], partner,
    ).wait_send()
    near_all = remote(
        sum_ref.at[core], sum_ref.at[1 - core], many_sem.at[3], many_sem.at[4], partner
    )
    near_all.wait_send()
    near_all.wait_recv()


def layer(features, cotangent, weight, filter_taps, lat_ext, lon_count):
    dma = pltpu.SemaphoreType.DMA
    vmem = pl.BlockSpec(memory_space=pltpu.VMEM)
    anywhere = pl.BlockSpec(memory_space=pl.ANY)
    return pl.pallas_call(
        layer_kernel,
        out_shape=[
            pltpu.VMEM((ROWS, WIDE, CH), BF16),
            pltpu.VMEM((ROWS, WIDE, CH), BF16),
            pltpu.VMEM((2, GROUP, CHUNK, CH), BF16),
        ],
        in_specs=[anywhere] * 6,
        out_specs=[vmem, vmem, vmem],
        scratch_shapes=[
            pltpu.VMEM((SPAN, LANES, CH), BF16),
            pltpu.VMEM((SPAN, LANES, CH), BF16),
            pltpu.VMEM((BASES, CH, CH), BF16),
            pltpu.VMEM((ROWS, TAPS, BASES, 2 * HALF), BF16),
            pltpu.SMEM((ROWS,), jnp.int32),
            pltpu.SMEM((ROWS,), jnp.int32),
            pltpu.VMEM((SPAN, TAPS, 8, LANES), F32),
            pltpu.VMEM((SPAN, TAPS, 8, LANES), F32),
            pltpu.VMEM((ROWS, BASES * WIDE, TAPS * LANES), BF16),
            pltpu.VMEM((BASES, ROWS * WIDE, CH), BF16),
            pltpu.VMEM((SPAN, BASES * LANES, CH), BF16),
            pltpu.VMEM((ROWS * WIDE, SPAN * BASES * LANES), BF16),
            pltpu.VMEM((2 * CH, CH), F32),
            pltpu.VMEM((2 * CH, CH), BF16),
            pltpu.VMEM((2 * CH, CH), BF16),
            pltpu.VMEM((GROUP, CHUNK, CH), BF16),
            pltpu.VMEM((GROUP, CHUNK, CH), BF16),
            pltpu.VMEM((ZFAR, CHUNK, CH), BF16),
            dma((6,)),
            dma((10,)), dma((10,)), dma((10,)), dma((10,)), dma((2,)), dma((2,)), dma((2,)), dma((2,)),
            dma((GROUP,)), dma((ZFAR,)), dma((GROUP,)), dma((5,)),
            *[pltpu.SemaphoreType.REGULAR] * 5,
        ],
        compiler_params=pltpu.CompilerParams(collective_id=0, has_side_effects=True),
    )(features, cotangent, weight, filter_taps, lat_ext, lon_count)


PIECES = 8


def write_kernel(scale, out_ref, grad_ref, sum_ref, out_any, grad_any, total_any, wide, sem):
    copies = [
        pltpu.make_async_copy(out_ref, out_any, sem.at[PIECES]),
        pltpu.make_async_copy(grad_ref, grad_any, sem.at[PIECES + 1]),
    ]
    for copy in copies:
        copy.start()
    per = 2 * GROUP // PIECES
    for index in range(PIECES):
        side, first = (index * per) // GROUP, (index * per) % GROUP
        wide[side, first : first + per] = sum_ref[side, first : first + per].astype(F32) * scale
        copy = pltpu.make_async_copy(
            wide.at[side, first : first + per], total_any.at[side, first : first + per], sem.at[index]
        )
        copy.start()
        copies.append(copy)
    for copy in copies:
        copy.wait()


def write(scale, output, grad, total):
    vmem = pl.BlockSpec(memory_space=pltpu.VMEM)
    anywhere = pl.BlockSpec(memory_space=pl.ANY)
    return pl.pallas_call(
        lambda *refs: write_kernel(scale, *refs),
        out_shape=[
            jax.ShapeDtypeStruct(output.shape, BF16),
            jax.ShapeDtypeStruct(grad.shape, BF16),
            jax.ShapeDtypeStruct(total.shape, F32),
        ],
        in_specs=[vmem, vmem, vmem],
        out_specs=[anywhere, anywhere, anywhere],
        scratch_shapes=[pltpu.VMEM(total.shape, F32), pltpu.SemaphoreType.DMA((PIECES + 2,))],
        name="write",
    )(*(pltpu.with_memory_space_constraint(held, pltpu.VMEM) for held in (output, grad, total)))


def per_device(features, cotangent, weight, filter_taps, lat_ext, lon_count):
    taps = jnp.transpose(filter_taps, (0, 2, 1, 3))
    output, field_grad, total = layer(features, cotangent, weight, taps, lat_ext, lon_count)
    cells = LATS * ROWS * LONS * WIDE
    output, field_grad, total = write(1.0 / math.sqrt(cells), output, field_grad, total)
    return (output, field_grad, total.reshape(BASES, CH, CH))


def solution(mesh):
    in_specs = (
        P("lat", "lon", None),
        P("lat", "lon", None),
        P(),
        P("lat", None, None, None),
        P("lat"),
        P("lat"),
    )
    out_specs = (P("lat", "lon", None), P("lat", "lon", None), P())
    return jax.shard_map(
        per_device, mesh=mesh, in_specs=in_specs, out_specs=out_specs, check_vma=False
    )
```

```python
import math

import jax
import jax.numpy as jnp
from jax import lax
from jax.experimental import pallas as pl
from jax.experimental.pallas import tpu as pltpu
from jax.sharding import PartitionSpec as P

MESH = pl.DeviceIdType.MESH
GROUP = 32
ZLEN = 16
ZFAR = 8
CHUNK = 16
LATS = 16
LONS = 32
ROWS = 4
REACH = 2
TAPS = 5
WIDE = 32
HALF = 32
BASES = 4
CH = 256
SPAN = ROWS + 2 * REACH
LANES = 128
BF16 = jnp.bfloat16
F32 = jnp.float32


def fill_filters(taps_ref, lat_ref, lon_ref, ft):
    lon_dist = jnp.abs(lax.broadcasted_iota(jnp.int32, (BASES, 2 * HALF), 1) - HALF)
    ft[REACH : REACH + ROWS] = jnp.zeros((ROWS, TAPS, 8, LANES), F32)
    for row in range(ROWS):
        ext, count = lat_ref[row], lon_ref[row]
        size = jnp.full((BASES, 2 * HALF), (2 * ext - 1) * (2 * count - 1), jnp.int32).astype(F32)
        guess = lax.rsqrt(size)
        scale = guess * (1.5 - 0.5 * size * guess * guess)
        scale = jnp.where(lon_dist < count, scale, 0.0)
        for tap in range(TAPS):
            held = jnp.where(abs(tap - REACH) < ext, scale, 0.0)
            taps = taps_ref[row, tap].astype(F32) * held
            ft[REACH + row, tap, 0:BASES, 0 : 2 * HALF] = taps.astype(BF16).astype(F32)


def slanted(base):
    return pltpu.roll(jnp.broadcast_to(base, (WIDE, LANES)), 0, 1, stride=1, stride_axis=0)


def fill_forward(ft, north, south, bands):
    def one(basis, carry):
        start = pl.multiple_of(basis * WIDE, WIDE)
        for row in range(ROWS):
            for tap in range(TAPS):
                line = row + tap
                base = ft[REACH + row, tap, pl.ds(basis, 1), :]
                if line < REACH:
                    base = base * north
                if line >= REACH + ROWS:
                    base = base * south
                bands[row, pl.ds(start, WIDE), tap * LANES : (tap + 1) * LANES] = slanted(
                    base
                ).astype(BF16)
        return carry

    lax.fori_loop(0, BASES, one, 0)


def convolve(bands, fw, bo, first):
    span = pl.ds(pl.multiple_of(first * WIDE, 2 * WIDE), 2 * WIDE)
    for row in range(ROWS):
        patch = fw[row : row + TAPS].reshape(TAPS * LANES, CH)
        sums = jnp.dot(bands[row, span, :], patch, preferred_element_type=F32).astype(BF16)
        bo[pl.ds(first, 2), row * WIDE : (row + 1) * WIDE, :] = sums.reshape(2, WIDE, CH)


def mix(bo, weight_ref, out_ref):
    total = jnp.dot(bo[0], weight_ref[0], preferred_element_type=F32)
    for basis in range(1, BASES):
        total = total + jnp.dot(bo[basis], weight_ref[basis], preferred_element_type=F32)
    out_ref[...] = total.astype(BF16).reshape(ROWS, WIDE, CH)


def fill_basis_grad(cw, weight_ref, bg):
    cells = cw[...].reshape(SPAN * LANES, CH)

    def one(basis, carry):
        grad = lax.dot_general(
            cells, weight_ref[basis], (((1,), (1,)), ((), ())), preferred_element_type=F32
        )
        start = pl.multiple_of(basis * LANES, LANES)
        bg[:, pl.ds(start, LANES), :] = grad.astype(BF16).reshape(SPAN, LANES, CH)
        return carry

    lax.fori_loop(0, BASES, one, 0)


def fill_reversed(ft, north, south, rt):
    first = lax.broadcasted_iota(jnp.int32, (LANES, LANES), 0)
    second = lax.broadcasted_iota(jnp.int32, (LANES, LANES), 1)
    flip = jnp.where(first + second == 2 * HALF, 1.0, 0.0).astype(BF16)
    flat = ft[...].reshape(SPAN * TAPS * 8, LANES).astype(BF16)
    turned = jnp.dot(flat, flip, preferred_element_type=F32)
    rt[...] = turned.reshape(SPAN, TAPS, 8, LANES)
    rt[0:REACH] = rt[0:REACH] * north
    rt[REACH + ROWS :] = rt[REACH + ROWS :] * south


def fill_adjoint(rt, wedge):
    def one(basis, carry):
        for row in range(ROWS):
            for tap in range(TAPS):
                line = row + TAPS - 1 - tap
                base = rt[line, tap, pl.ds(basis, 1), :]
                start = pl.multiple_of((line * BASES + basis) * LANES, LANES)
                wedge[row * WIDE : (row + 1) * WIDE, pl.ds(start, LANES)] = slanted(base).astype(BF16)
        return carry

    lax.fori_loop(0, BASES, one, 0)


def adjoint(wedge, bg, grad_ref):
    flat = bg[...].reshape(SPAN * BASES * LANES, CH)
    total = jnp.dot(wedge[...], flat, preferred_element_type=F32)
    grad_ref[...] = total.astype(BF16).reshape(ROWS, WIDE, CH)


def layer_kernel(
    feat_any, cot_any, weight_any, taps_any, lat_any, lon_any,
    out_ref, grad_ref, sum_ref,
    fw, cw, weight_ref, taps_ref, lat_ref, lon_ref, ft, rt, bands, bo, bg, wedge, part, pair_out, pair_in, half, group_in, zbuf,
    own_sem, feat_send, feat_recv, cot_send, cot_recv, ft_send, ft_recv, pair_send, pair_recv,
    group_recv, z_recv, all_recv, many_sem,
    hop_sem, leap_sem, step_sem, cross_sem, twin_sem,
):
    lat = lax.axis_index("lat")
    lon = lax.axis_index("lon")
    core = lat % 2
    y_lo = (lat // 2) % 2
    x = lat // 4
    z = lon % ZLEN
    z_lo = z % 2
    z_hi = z // 2
    y_hi = lon // ZLEN
    spot = z_lo * 16 + x * 4 + y_hi * 2 + y_lo
    partner = (lat + 1 - 2 * core, lon)

    def across(dx, dy, dz):
        far_x, far_y, far_z = (x + dx) % 4, (y_hi * 2 + y_lo + dy) % 4, (z_lo + dz) % 2
        device = (far_x * 4 + (far_y % 2) * 2 + core, (far_y // 2) * ZLEN + z_hi * 2 + far_z)
        return device, far_z * 16 + far_x * 4 + far_y

    def z_device(index):
        return (lat, y_hi * ZLEN + index)

    def far_device(index):
        return z_device(index * 2 + z_lo)

    def beside(up, right):
        return ((lat + LATS + up) % LATS, (lon + LONS + right) % LONS)

    away = 2 * core - 1
    ways = [(away, 1), (away, -1), (0, 1), (0, -1), (1, 0), (-1, 0)]

    def remote(src, dst, send, recv, device):
        return pltpu.make_async_remote_copy(
            src_ref=src, dst_ref=dst, send_sem=send, recv_sem=recv,
            device_id=device, device_id_type=MESH,
        )

    def signal(sem, device):
        pl.semaphore_signal(sem, inc=1, device_id=device, device_id_type=MESH)

    steps = [(1, 0), (3, 0), (0, 1), (0, 3)]
    barrier = pltpu.get_barrier_semaphore()
    for way in ways:
        signal(barrier, beside(*way))
    for dx, dy in steps:
        signal(barrier, across(dx, dy, 0)[0])
    signal(barrier, z_device((z + 2) % ZLEN))
    signal(barrier, z_device((z + ZLEN - 2) % ZLEN))

    north = jnp.where(lat > 0, 1.0, 0.0)
    south = jnp.where(lat < LATS - 1, 1.0, 0.0)
    inner = slice(REACH, REACH + ROWS)
    middle = slice(WIDE, 2 * WIDE)
    own_copies = [
        pltpu.make_async_copy(feat_any, fw.at[inner, middle], own_sem.at[0]),
        pltpu.make_async_copy(cot_any, cw.at[inner, middle], own_sem.at[1]),
        pltpu.make_async_copy(weight_any, weight_ref, own_sem.at[2]),
        pltpu.make_async_copy(taps_any, taps_ref, own_sem.at[3]),
        pltpu.make_async_copy(lat_any, lat_ref, own_sem.at[4]),
        pltpu.make_async_copy(lon_any, lon_ref, own_sem.at[5]),
    ]
    for copy in own_copies:
        copy.start()
    pl.semaphore_wait(barrier, len(ways) + len(steps) + 2)

    def rows(window, start, left):
        return window.at[pl.ds(start, REACH), left : left + WIDE]

    common, single = REACH * (1 - core), REACH * core
    far = REACH + ROWS

    def halo(source, window, send, recv):
        out, arrive = [], []

        def add(src, start, landing, left, device):
            index = len(out)
            out.append(remote(src, rows(window, start, left), send.at[index], recv.at[index], device))
            place = rows(window, landing, left)
            arrive.append(remote(place, place, send.at[index], recv.at[index], partner))

        for right in (1, -1):
            start = REACH + common
            add(source.at[pl.ds(common, REACH)], start, start, WIDE * (1 - right), beside(0, right))
        for right in (1, -1):
            add(
                source.at[pl.ds(single, REACH)], far * (1 - core), far * core, WIDE * (1 - right),
                beside(away, right),
            )
        for right in (1, -1):
            start = REACH + single
            add(source.at[pl.ds(single, REACH)], start, start, WIDE * (1 - right), beside(0, right))
        add(source.at[ROWS - REACH :], 0, 0, WIDE, beside(1, 0))
        add(source.at[0:REACH], far, far, WIDE, beside(-1, 0))
        for right in (1, -1):
            left = WIDE * (1 - right)
            add(rows(window, REACH + common, left), far * core, far * (1 - core), left, partner)
        return out, arrive

    feat_copies, feat_arrive = halo(feat_any, fw, feat_send, feat_recv)
    cot_copies, cot_arrive = halo(cot_any, cw, cot_send, cot_recv)
    ft_copies = [
        remote(ft.at[ROWS : ROWS + REACH], ft.at[0:REACH], ft_send.at[0], ft_recv.at[0], beside(1, 0)),
        remote(ft.at[REACH : 2 * REACH], ft.at[REACH + ROWS :], ft_send.at[1], ft_recv.at[1], beside(-1, 0)),
    ]
    for copy in feat_copies[:8]:
        copy.start()
    for dx, dy in steps:
        signal(step_sem, across(dx, dy, 0)[0])
    signal(hop_sem, z_device((z + 2) % ZLEN))
    signal(hop_sem, z_device((z + ZLEN - 2) % ZLEN))
    blank = jnp.zeros((SPAN, LANES - 3 * WIDE, CH), BF16)
    fw[:, 3 * WIDE :, :] = blank
    cw[:, 3 * WIDE :, :] = blank
    for copy in own_copies[3:]:
        copy.wait()
    fill_filters(taps_ref, lat_ref, lon_ref, ft)
    fill_forward(ft, north, south, bands)
    wedge[...] = jnp.zeros(wedge.shape, BF16)
    pl.semaphore_wait(step_sem, len(steps))
    signal(cross_sem, across(2, 0, 0)[0])
    signal(cross_sem, across(0, 2, 0)[0])
    pl.semaphore_wait(hop_sem, 2)
    signal(leap_sem, z_device((z + 4) % ZLEN))
    signal(leap_sem, z_device((z + ZLEN - 4) % ZLEN))
    for index in range(2):
        feat_arrive[index].wait_recv()
        feat_copies[8 + index].start()
    for copy in feat_arrive[2:]:
        copy.wait_recv()
    own_copies[0].wait()
    own_copies[1].wait()
    convolve(bands, fw, bo, (1 - core) * 2)

    cells = cw[inner, middle, :].reshape(ROWS * WIDE, CH)

    def share(basis):
        return lax.dot_general(bo[basis], cells, (((0,), (0,)), ((), ())), preferred_element_type=F32)

    def pair_copy(index):
        span = pl.ds(pl.multiple_of(index * CH, CH), CH)
        return remote(pair_out.at[span], pair_in.at[span], pair_send.at[index], pair_recv.at[index], partner)

    for index in range(2):
        pair_out[index * CH : (index + 1) * CH, :] = share((1 - core) * 2 + index).astype(BF16)
        pair_copy(index).start()
    pl.semaphore_wait(cross_sem, 2)
    signal(twin_sem, across(0, 0, 1)[0])
    convolve(bands, fw, bo, core * 2)
    for index in range(2):
        part[index * CH : (index + 1) * CH, :] = share(core * 2 + index)
    per = GROUP // 2
    places = [(dx, dy) for dx in (0, 1, 2, 3) for dy in (0, 1, 2, 3)]
    places.sort(key=lambda p: -(min(p[0], 4 - p[0]) + min(p[1], 4 - p[1])))
    offsets = [(dx, dy, dz) for dx, dy in places for dz in (0, 1)]
    offsets.sort(key=lambda o: -(min(o[0], 4 - o[0]) + min(o[1], 4 - o[1]) + o[2]))

    def group_copy(index, dz):
        device, piece = across(*places[index], dz)
        slot = dz * per + index
        return remote(half.at[piece], group_in.at[slot], many_sem.at[0], group_recv.at[slot], device)

    def group_arrive(slot):
        return remote(
            group_in.at[slot], group_in.at[slot], many_sem.at[0], group_recv.at[slot], partner
        )

    def group_add(slot, carry):
        group_arrive(slot).wait_recv()
        return carry + group_in[slot].astype(F32)

    for index in range(2):
        pair_copy(index).wait_recv()
        span = slice(index * CH, (index + 1) * CH)
        total = part[span, :] + pair_in[span, :].astype(F32)
        half[index * per : (index + 1) * per] = total.astype(BF16).reshape(per, CHUNK, CH)
        if index == 0:
            pl.semaphore_wait(twin_sem, 1)
        turn = (z_lo + index) % 2
        for place in range(per - 1):
            group_copy(place, turn).start()

        @pl.when(turn == 1)
        def _():
            group_copy(per - 1, 1).start()

    for copy in cot_copies[:8] + ft_copies:
        copy.start()
    own_copies[2].wait()
    mix(bo, weight_ref, out_ref)
    chunk = lax.fori_loop(0, per - 1, group_add, half[spot].astype(F32))
    chunk = lax.fori_loop(per, GROUP, group_add, chunk)
    zbuf[z_hi] = chunk.astype(BF16)
    pl.semaphore_wait(leap_sem, 2)

    def z_copy(step):
        return remote(
            zbuf.at[z_hi], zbuf.at[z_hi], many_sem.at[1], z_recv.at[z_hi],
            far_device((z_hi + step) % ZFAR),
        )

    def z_wait(step, carry):
        source = (z_hi + step) % ZFAR
        remote(
            zbuf.at[source], zbuf.at[source], many_sem.at[1], z_recv.at[source], far_device(source)
        ).wait_recv()
        return carry

    for step in (4, 3, 5, 2, 6, 1, 7):
        z_copy(step).start()
    for copy in ft_copies:
        copy.wait_recv()
    for index in range(2):
        cot_arrive[index].wait_recv()
        cot_copies[8 + index].start()
    fill_reversed(ft, north, south, rt)
    fill_adjoint(rt, wedge)
    lax.fori_loop(1, ZFAR, z_wait, 0)
    chunk = zbuf[0].astype(F32)
    for source in range(1, ZFAR):
        chunk = chunk + zbuf[source].astype(F32)
    sum_ref[core, spot] = chunk.astype(BF16)

    def all_copy(step):
        return remote(
            sum_ref.at[core, spot], sum_ref.at[core, spot], many_sem.at[2], all_recv.at[step],
            across(*offsets[step])[0],
        )

    def near_copy(index):
        return remote(
            sum_ref.at[core, index], sum_ref.at[core, index], many_sem.at[3], many_sem.at[4], partner
        )

    for step in range(GROUP - 1):
        all_copy(step).start()
    near_copy(spot).start()
    for copy in cot_arrive[2:]:
        copy.wait_recv()
    fill_basis_grad(cw, weight_ref, bg)
    adjoint(wedge, bg, grad_ref)
    for copy in feat_copies + cot_copies + ft_copies:
        copy.wait_send()
    for index in range(2):
        pair_copy(index).wait_send()
    remote(
        half.at[0 : GROUP - 1], group_in.at[0 : GROUP - 1], many_sem.at[0], group_recv.at[0], partner
    ).wait_send()
    remote(
        zbuf.at[0 : ZFAR - 1], zbuf.at[0 : ZFAR - 1], many_sem.at[1], z_recv.at[0], partner
    ).wait_send()
    for step in range(GROUP - 1):
        dx, dy, dz = offsets[step]
        source = across(4 - dx, 4 - dy, dz)[1]
        remote(
            sum_ref.at[core, source], sum_ref.at[core, source], many_sem.at[2], all_recv.at[step],
            partner,
        ).wait_recv()
        near_copy(source).start()
    remote(
        sum_ref.at[core, 0 : GROUP - 1], sum_ref.at[core, 0 : GROUP - 1], many_sem.at[2],
        all_recv.at[0], partner,
    ).wait_send()
    near_all = remote(
        sum_ref.at[core], sum_ref.at[1 - core], many_sem.at[3], many_sem.at[4], partner
    )
    near_all.wait_send()
    near_all.wait_recv()


def layer(features, cotangent, weight, filter_taps, lat_ext, lon_count):
    dma = pltpu.SemaphoreType.DMA
    vmem = pl.BlockSpec(memory_space=pltpu.VMEM)
    anywhere = pl.BlockSpec(memory_space=pl.ANY)
    return pl.pallas_call(
        layer_kernel,
        out_shape=[
            pltpu.VMEM((ROWS, WIDE, CH), BF16),
            pltpu.VMEM((ROWS, WIDE, CH), BF16),
            pltpu.VMEM((2, GROUP, CHUNK, CH), BF16),
        ],
        in_specs=[anywhere] * 6,
        out_specs=[vmem, vmem, vmem],
        scratch_shapes=[
            pltpu.VMEM((SPAN, LANES, CH), BF16),
            pltpu.VMEM((SPAN, LANES, CH), BF16),
            pltpu.VMEM((BASES, CH, CH), BF16),
            pltpu.VMEM((ROWS, TAPS, BASES, 2 * HALF), BF16),
            pltpu.SMEM((ROWS,), jnp.int32),
            pltpu.SMEM((ROWS,), jnp.int32),
            pltpu.VMEM((SPAN, TAPS, 8, LANES), F32),
            pltpu.VMEM((SPAN, TAPS, 8, LANES), F32),
            pltpu.VMEM((ROWS, BASES * WIDE, TAPS * LANES), BF16),
            pltpu.VMEM((BASES, ROWS * WIDE, CH), BF16),
            pltpu.VMEM((SPAN, BASES * LANES, CH), BF16),
            pltpu.VMEM((ROWS * WIDE, SPAN * BASES * LANES), BF16),
            pltpu.VMEM((2 * CH, CH), F32),
            pltpu.VMEM((2 * CH, CH), BF16),
            pltpu.VMEM((2 * CH, CH), BF16),
            pltpu.VMEM((GROUP, CHUNK, CH), BF16),
            pltpu.VMEM((GROUP, CHUNK, CH), BF16),
            pltpu.VMEM((ZFAR, CHUNK, CH), BF16),
            dma((6,)),
            dma((10,)), dma((10,)), dma((10,)), dma((10,)), dma((2,)), dma((2,)), dma((2,)), dma((2,)),
            dma((GROUP,)), dma((ZFAR,)), dma((GROUP,)), dma((5,)),
            *[pltpu.SemaphoreType.REGULAR] * 5,
        ],
        compiler_params=pltpu.CompilerParams(collective_id=0, has_side_effects=True),
    )(features, cotangent, weight, filter_taps, lat_ext, lon_count)


PIECES = 8


def write_kernel(scale, out_ref, grad_ref, sum_ref, out_any, grad_any, total_any, wide, sem):
    copies = [
        pltpu.make_async_copy(out_ref, out_any, sem.at[PIECES]),
        pltpu.make_async_copy(grad_ref, grad_any, sem.at[PIECES + 1]),
    ]
    for copy in copies:
        copy.start()
    per = 2 * GROUP // PIECES
    for index in range(PIECES):
        side, first = (index * per) // GROUP, (index * per) % GROUP
        wide[side, first : first + per] = sum_ref[side, first : first + per].astype(F32) * scale
        copy = pltpu.make_async_copy(
            wide.at[side, first : first + per], total_any.at[side, first : first + per], sem.at[index]
        )
        copy.start()
        copies.append(copy)
    for copy in copies:
        copy.wait()


def write(scale, output, grad, total):
    vmem = pl.BlockSpec(memory_space=pltpu.VMEM)
    anywhere = pl.BlockSpec(memory_space=pl.ANY)
    return pl.pallas_call(
        lambda *refs: write_kernel(scale, *refs),
        out_shape=[
            jax.ShapeDtypeStruct(output.shape, BF16),
            jax.ShapeDtypeStruct(grad.shape, BF16),
            jax.ShapeDtypeStruct(total.shape, F32),
        ],
        in_specs=[vmem, vmem, vmem],
        out_specs=[anywhere, anywhere, anywhere],
        scratch_shapes=[pltpu.VMEM(total.shape, F32), pltpu.SemaphoreType.DMA((PIECES + 2,))],
        name="write",
    )(*(pltpu.with_memory_space_constraint(held, pltpu.VMEM) for held in (output, grad, total)))


def per_device(features, cotangent, weight, filter_taps, lat_ext, lon_count):
    taps = jnp.transpose(filter_taps, (0, 2, 1, 3))
    output, field_grad, total = layer(features, cotangent, weight, taps, lat_ext, lon_count)
    cells = LATS * ROWS * LONS * WIDE
    output, field_grad, total = write(1.0 / math.sqrt(cells), output, field_grad, total)
    return (output, field_grad, total.reshape(BASES, CH, CH))


def solution(mesh):
    in_specs = (
        P("lat", "lon", None),
        P("lat", "lon", None),
        P(),
        P("lat", None, None, None),
        P("lat"),
        P("lat"),
    )
    out_specs = (P("lat", "lon", None), P("lat", "lon", None), P())
    return jax.shard_map(
        per_device, mesh=mesh, in_specs=in_specs, out_specs=out_specs, check_vma=False
    )
```

```python
import math

import jax
import jax.numpy as jnp
from jax import lax
from jax.experimental import pallas as pl
from jax.experimental.pallas import tpu as pltpu
from jax.sharding import PartitionSpec as P

MESH = pl.DeviceIdType.MESH
GROUP = 32
ZLEN = 16
ZFAR = 8
CHUNK = 16
LATS = 16
LONS = 32
ROWS = 4
REACH = 2
TAPS = 5
WIDE = 32
HALF = 32
BASES = 4
CH = 256
SPAN = ROWS + 2 * REACH
LANES = 128
BF16 = jnp.bfloat16
F32 = jnp.float32


def fill_filters(taps_ref, lat_ref, lon_ref, ft):
    lon_dist = jnp.abs(lax.broadcasted_iota(jnp.int32, (BASES, 2 * HALF), 1) - HALF)
    ft[REACH : REACH + ROWS] = jnp.zeros((ROWS, TAPS, 8, LANES), F32)
    for row in range(ROWS):
        ext, count = lat_ref[row], lon_ref[row]
        size = jnp.full((BASES, 2 * HALF), (2 * ext - 1) * (2 * count - 1), jnp.int32).astype(F32)
        guess = lax.rsqrt(size)
        scale = guess * (1.5 - 0.5 * size * guess * guess)
        scale = jnp.where(lon_dist < count, scale, 0.0)
        for tap in range(TAPS):
            held = jnp.where(abs(tap - REACH) < ext, scale, 0.0)
            taps = taps_ref[row, tap].astype(F32) * held
            ft[REACH + row, tap, 0:BASES, 0 : 2 * HALF] = taps.astype(BF16).astype(F32)


def slanted(base):
    return pltpu.roll(jnp.broadcast_to(base, (WIDE, LANES)), 0, 1, stride=1, stride_axis=0)


def fill_forward(ft, north, south, bands):
    def one(basis, carry):
        start = pl.multiple_of(basis * WIDE, WIDE)
        for row in range(ROWS):
            for tap in range(TAPS):
                line = row + tap
                base = ft[REACH + row, tap, pl.ds(basis, 1), :]
                if line < REACH:
                    base = base * north
                if line >= REACH + ROWS:
                    base = base * south
                bands[row, pl.ds(start, WIDE), tap * LANES : (tap + 1) * LANES] = slanted(
                    base
                ).astype(BF16)
        return carry

    lax.fori_loop(0, BASES, one, 0)


def convolve(bands, fw, bo, first):
    span = pl.ds(pl.multiple_of(first * WIDE, 2 * WIDE), 2 * WIDE)
    for row in range(ROWS):
        patch = fw[row : row + TAPS].reshape(TAPS * LANES, CH)
        sums = jnp.dot(bands[row, span, :], patch, preferred_element_type=F32).astype(BF16)
        bo[pl.ds(first, 2), row * WIDE : (row + 1) * WIDE, :] = sums.reshape(2, WIDE, CH)


def mix(bo, weight_ref, out_ref):
    total = jnp.dot(bo[0], weight_ref[0], preferred_element_type=F32)
    for basis in range(1, BASES):
        total = total + jnp.dot(bo[basis], weight_ref[basis], preferred_element_type=F32)
    out_ref[...] = total.astype(BF16).reshape(ROWS, WIDE, CH)


def fill_basis_grad(cw, weight_ref, bg):
    cells = cw[...].reshape(SPAN * LANES, CH)

    def one(basis, carry):
        grad = lax.dot_general(
            cells, weight_ref[basis], (((1,), (1,)), ((), ())), preferred_element_type=F32
        )
        start = pl.multiple_of(basis * LANES, LANES)
        bg[:, pl.ds(start, LANES), :] = grad.astype(BF16).reshape(SPAN, LANES, CH)
        return carry

    lax.fori_loop(0, BASES, one, 0)


def fill_reversed(ft, north, south, rt):
    first = lax.broadcasted_iota(jnp.int32, (LANES, LANES), 0)
    second = lax.broadcasted_iota(jnp.int32, (LANES, LANES), 1)
    flip = jnp.where(first + second == 2 * HALF, 1.0, 0.0).astype(BF16)
    flat = ft[...].reshape(SPAN * TAPS * 8, LANES).astype(BF16)
    turned = jnp.dot(flat, flip, preferred_element_type=F32)
    rt[...] = turned.reshape(SPAN, TAPS, 8, LANES)
    rt[0:REACH] = rt[0:REACH] * north
    rt[REACH + ROWS :] = rt[REACH + ROWS :] * south


def fill_adjoint(rt, wedge):
    def one(basis, carry):
        for row in range(ROWS):
            for tap in range(TAPS):
                line = row + TAPS - 1 - tap
                base = rt[line, tap, pl.ds(basis, 1), :]
                start = pl.multiple_of((line * BASES + basis) * LANES, LANES)
                wedge[row * WIDE : (row + 1) * WIDE, pl.ds(start, LANES)] = slanted(base).astype(BF16)
        return carry

    lax.fori_loop(0, BASES, one, 0)


def adjoint(wedge, bg, grad_ref):
    flat = bg[...].reshape(SPAN * BASES * LANES, CH)
    total = jnp.dot(wedge[...], flat, preferred_element_type=F32)
    grad_ref[...] = total.astype(BF16).reshape(ROWS, WIDE, CH)


def layer_kernel(
    feat_any, cot_any, weight_any, taps_any, lat_any, lon_any,
    out_ref, grad_ref, sum_ref,
    fw, cw, weight_ref, taps_ref, lat_ref, lon_ref, ft, rt, bands, bo, bg, wedge, part, pair_out, pair_in, half, group_in, zbuf,
    own_sem, feat_send, feat_recv, cot_send, cot_recv, ft_send, ft_recv, pair_send, pair_recv,
    group_recv, z_recv, all_recv, many_sem,
    hop_sem, leap_sem, step_sem, cross_sem, twin_sem,
):
    lat = lax.axis_index("lat")
    lon = lax.axis_index("lon")
    core = lat % 2
    y_lo = (lat // 2) % 2
    x = lat // 4
    z = lon % ZLEN
    z_lo = z % 2
    z_hi = z // 2
    y_hi = lon // ZLEN
    spot = z_lo * 16 + x * 4 + y_hi * 2 + y_lo
    partner = (lat + 1 - 2 * core, lon)

    def across(dx, dy, dz):
        far_x, far_y, far_z = (x + dx) % 4, (y_hi * 2 + y_lo + dy) % 4, (z_lo + dz) % 2
        device = (far_x * 4 + (far_y % 2) * 2 + core, (far_y // 2) * ZLEN + z_hi * 2 + far_z)
        return device, far_z * 16 + far_x * 4 + far_y

    def z_device(index):
        return (lat, y_hi * ZLEN + index)

    def far_device(index):
        return z_device(index * 2 + z_lo)

    def beside(up, right):
        return ((lat + LATS + up) % LATS, (lon + LONS + right) % LONS)

    away = 2 * core - 1
    ways = [(away, 1), (away, -1), (0, 1), (0, -1), (1, 0), (-1, 0)]

    def remote(src, dst, send, recv, device):
        return pltpu.make_async_remote_copy(
            src_ref=src, dst_ref=dst, send_sem=send, recv_sem=recv,
            device_id=device, device_id_type=MESH,
        )

    def signal(sem, device):
        pl.semaphore_signal(sem, inc=1, device_id=device, device_id_type=MESH)

    steps = [(1, 0), (3, 0), (0, 1), (0, 3)]
    barrier = pltpu.get_barrier_semaphore()
    for way in ways:
        signal(barrier, beside(*way))
    for dx, dy in steps:
        signal(barrier, across(dx, dy, 0)[0])
    signal(barrier, z_device((z + 2) % ZLEN))
    signal(barrier, z_device((z + ZLEN - 2) % ZLEN))

    north = jnp.where(lat > 0, 1.0, 0.0)
    south = jnp.where(lat < LATS - 1, 1.0, 0.0)
    inner = slice(REACH, REACH + ROWS)
    middle = slice(WIDE, 2 * WIDE)
    own_copies = [
        pltpu.make_async_copy(feat_any, fw.at[inner, middle], own_sem.at[0]),
        pltpu.make_async_copy(cot_any, cw.at[inner, middle], own_sem.at[1]),
        pltpu.make_async_copy(weight_any, weight_ref, own_sem.at[2]),
        pltpu.make_async_copy(taps_any, taps_ref, own_sem.at[3]),
        pltpu.make_async_copy(lat_any, lat_ref, own_sem.at[4]),
        pltpu.make_async_copy(lon_any, lon_ref, own_sem.at[5]),
    ]
    for copy in own_copies:
        copy.start()
    pl.semaphore_wait(barrier, len(ways) + len(steps) + 2)

    def rows(window, start, left):
        return window.at[pl.ds(start, REACH), left : left + WIDE]

    common, single = REACH * (1 - core), REACH * core
    far = REACH + ROWS

    def halo(source, window, send, recv):
        out, arrive = [], []

        def add(src, start, landing, left, device):
            index = len(out)
            out.append(remote(src, rows(window, start, left), send.at[index], recv.at[index], device))
            place = rows(window, landing, left)
            arrive.append(remote(place, place, send.at[index], recv.at[index], partner))

        for right in (1, -1):
            start = REACH + common
            add(source.at[pl.ds(common, REACH)], start, start, WIDE * (1 - right), beside(0, right))
        for right in (1, -1):
            add(
                source.at[pl.ds(single, REACH)], far * (1 - core), far * core, WIDE * (1 - right),
                beside(away, right),
            )
        for right in (1, -1):
            start = REACH + single
            add(source.at[pl.ds(single, REACH)], start, start, WIDE * (1 - right), beside(0, right))
        add(source.at[ROWS - REACH :], 0, 0, WIDE, beside(1, 0))
        add(source.at[0:REACH], far, far, WIDE, beside(-1, 0))
        for right in (1, -1):
            left = WIDE * (1 - right)
            add(rows(window, REACH + common, left), far * core, far * (1 - core), left, partner)
        return out, arrive

    feat_copies, feat_arrive = halo(feat_any, fw, feat_send, feat_recv)
    cot_copies, cot_arrive = halo(cot_any, cw, cot_send, cot_recv)
    ft_copies = [
        remote(ft.at[ROWS : ROWS + REACH], ft.at[0:REACH], ft_send.at[0], ft_recv.at[0], beside(1, 0)),
        remote(ft.at[REACH : 2 * REACH], ft.at[REACH + ROWS :], ft_send.at[1], ft_recv.at[1], beside(-1, 0)),
    ]
    for copy in feat_copies[:8]:
        copy.start()
    for dx, dy in steps:
        signal(step_sem, across(dx, dy, 0)[0])
    signal(hop_sem, z_device((z + 2) % ZLEN))
    signal(hop_sem, z_device((z + ZLEN - 2) % ZLEN))
    blank = jnp.zeros((SPAN, LANES - 3 * WIDE, CH), BF16)
    fw[:, 3 * WIDE :, :] = blank
    cw[:, 3 * WIDE :, :] = blank
    for copy in own_copies[3:]:
        copy.wait()
    fill_filters(taps_ref, lat_ref, lon_ref, ft)
    fill_forward(ft, north, south, bands)
    wedge[...] = jnp.zeros(wedge.shape, BF16)
    pl.semaphore_wait(step_sem, len(steps))
    signal(cross_sem, across(2, 0, 0)[0])
    signal(cross_sem, across(0, 2, 0)[0])
    pl.semaphore_wait(hop_sem, 2)
    signal(leap_sem, z_device((z + 4) % ZLEN))
    signal(leap_sem, z_device((z + ZLEN - 4) % ZLEN))
    for index in range(2):
        feat_arrive[index].wait_recv()
        feat_copies[8 + index].start()
    for copy in feat_arrive[2:]:
        copy.wait_recv()
    own_copies[0].wait()
    own_copies[1].wait()
    convolve(bands, fw, bo, (1 - core) * 2)

    cells = cw[inner, middle, :].reshape(ROWS * WIDE, CH)

    def share(basis):
        return lax.dot_general(bo[basis], cells, (((0,), (0,)), ((), ())), preferred_element_type=F32)

    def pair_copy(index):
        span = pl.ds(pl.multiple_of(index * CH, CH), CH)
        return remote(pair_out.at[span], pair_in.at[span], pair_send.at[index], pair_recv.at[index], partner)

    for index in range(2):
        pair_out[index * CH : (index + 1) * CH, :] = share((1 - core) * 2 + index).astype(BF16)
        pair_copy(index).start()
    pl.semaphore_wait(cross_sem, 2)
    signal(twin_sem, across(0, 0, 1)[0])
    convolve(bands, fw, bo, core * 2)
    for index in range(2):
        part[index * CH : (index + 1) * CH, :] = share(core * 2 + index)
    per = GROUP // 2
    places = [(dx, dy) for dx in (0, 1, 2, 3) for dy in (0, 1, 2, 3)]
    places.sort(key=lambda p: -(min(p[0], 4 - p[0]) + min(p[1], 4 - p[1])))
    offsets = [(dx, dy, dz) for dx, dy in places for dz in (0, 1)]
    offsets.sort(key=lambda o: -(min(o[0], 4 - o[0]) + min(o[1], 4 - o[1]) + o[2]))

    def group_copy(index, dz):
        device, piece = across(*places[index], dz)
        slot = dz * per + index
        return remote(half.at[piece], group_in.at[slot], many_sem.at[0], group_recv.at[slot], device)

    def group_arrive(slot):
        return remote(
            group_in.at[slot], group_in.at[slot], many_sem.at[0], group_recv.at[slot], partner
        )

    def group_add(slot, carry):
        group_arrive(slot).wait_recv()
        return carry + group_in[slot].astype(F32)

    for index in range(2):
        pair_copy(index).wait_recv()
        span = slice(index * CH, (index + 1) * CH)
        total = part[span, :] + pair_in[span, :].astype(F32)
        half[index * per : (index + 1) * per] = total.astype(BF16).reshape(per, CHUNK, CH)
        if index == 0:
            pl.semaphore_wait(twin_sem, 1)
        turn = (z_lo + index) % 2
        for place in range(per - 1):
            group_copy(place, turn).start()

        @pl.when(turn == 1)
        def _():
            group_copy(per - 1, 1).start()

    for copy in cot_copies[:8] + ft_copies:
        copy.start()
    own_copies[2].wait()
    mix(bo, weight_ref, out_ref)
    chunk = lax.fori_loop(0, per - 1, group_add, half[spot].astype(F32))
    chunk = lax.fori_loop(per, GROUP, group_add, chunk)
    zbuf[z_hi] = chunk.astype(BF16)
    pl.semaphore_wait(leap_sem, 2)

    def z_copy(step):
        return remote(
            zbuf.at[z_hi], zbuf.at[z_hi], many_sem.at[1], z_recv.at[z_hi],
            far_device((z_hi + step) % ZFAR),
        )

    def z_wait(step, carry):
        source = (z_hi + step) % ZFAR
        remote(
            zbuf.at[source], zbuf.at[source], many_sem.at[1], z_recv.at[source], far_device(source)
        ).wait_recv()
        return carry

    for step in (4, 3, 5, 2, 6, 1, 7):
        z_copy(step).start()
    for copy in ft_copies:
        copy.wait_recv()
    for index in range(2):
        cot_arrive[index].wait_recv()
        cot_copies[8 + index].start()
    fill_reversed(ft, north, south, rt)
    fill_adjoint(rt, wedge)
    for copy in cot_arrive[2:]:
        copy.wait_recv()
    fill_basis_grad(cw, weight_ref, bg)
    adjoint(wedge, bg, grad_ref)
    lax.fori_loop(1, ZFAR, z_wait, 0)
    chunk = zbuf[0].astype(F32)
    for source in range(1, ZFAR):
        chunk = chunk + zbuf[source].astype(F32)
    sum_ref[core, spot] = chunk.astype(BF16)

    slots = {offset: step for step, offset in enumerate(offsets)}
    feeders = {(3, 0, 0): [(2, dy, 0) for dy in (2, 1, 3, 0)], (0, 3, 0): [(dx, 2, 0) for dx in (1, 3, 0)]}
    handed = feeders[3, 0, 0] + feeders[0, 3, 0]
    direct = [o for o in offsets[: GROUP - 1] if o not in feeders and o not in handed]

    def all_copy(piece, offset, device):
        return remote(
            sum_ref.at[core, piece], sum_ref.at[core, piece], many_sem.at[2],
            all_recv.at[slots[offset]], device,
        )

    def near_copy(index):
        return remote(
            sum_ref.at[core, index], sum_ref.at[core, index], many_sem.at[3], many_sem.at[4], partner
        )

    for offset in list(feeders) + direct:
        all_copy(spot, offset, across(*offset)[0]).start()
    near_copy(spot).start()
    for offset in list(feeders) + direct + handed:
        dx, dy, dz = offset
        source = across(4 - dx, 4 - dy, dz)[1]
        all_copy(source, offset, partner).wait_recv()
        for goal in feeders.get(offset, []):
            device = across((goal[0] - dx) % 4, (goal[1] - dy) % 4, 0)[0]
            all_copy(source, goal, device).start()
        near_copy(source).start()
    for copy in feat_copies + cot_copies + ft_copies:
        copy.wait_send()
    for index in range(2):
        pair_copy(index).wait_send()
    remote(
        half.at[0 : GROUP - 1], group_in.at[0 : GROUP - 1], many_sem.at[0], group_recv.at[0], partner
    ).wait_send()
    remote(
        zbuf.at[0 : ZFAR - 1], zbuf.at[0 : ZFAR - 1], many_sem.at[1], z_recv.at[0], partner
    ).wait_send()
    remote(
        sum_ref.at[core, 0 : GROUP - 1], sum_ref.at[core, 0 : GROUP - 1], many_sem.at[2],
        all_recv.at[0], partner,
    ).wait_send()
    near_all = remote(
        sum_ref.at[core], sum_ref.at[1 - core], many_sem.at[3], many_sem.at[4], partner
    )
    near_all.wait_send()
    near_all.wait_recv()


def layer(features, cotangent, weight, filter_taps, lat_ext, lon_count):
    dma = pltpu.SemaphoreType.DMA
    vmem = pl.BlockSpec(memory_space=pltpu.VMEM)
    anywhere = pl.BlockSpec(memory_space=pl.ANY)
    return pl.pallas_call(
        layer_kernel,
        out_shape=[
            pltpu.VMEM((ROWS, WIDE, CH), BF16),
            pltpu.VMEM((ROWS, WIDE, CH), BF16),
            pltpu.VMEM((2, GROUP, CHUNK, CH), BF16),
        ],
        in_specs=[anywhere] * 6,
        out_specs=[vmem, vmem, vmem],
        scratch_shapes=[
            pltpu.VMEM((SPAN, LANES, CH), BF16),
            pltpu.VMEM((SPAN, LANES, CH), BF16),
            pltpu.VMEM((BASES, CH, CH), BF16),
            pltpu.VMEM((ROWS, TAPS, BASES, 2 * HALF), BF16),
            pltpu.SMEM((ROWS,), jnp.int32),
            pltpu.SMEM((ROWS,), jnp.int32),
            pltpu.VMEM((SPAN, TAPS, 8, LANES), F32),
            pltpu.VMEM((SPAN, TAPS, 8, LANES), F32),
            pltpu.VMEM((ROWS, BASES * WIDE, TAPS * LANES), BF16),
            pltpu.VMEM((BASES, ROWS * WIDE, CH), BF16),
            pltpu.VMEM((SPAN, BASES * LANES, CH), BF16),
            pltpu.VMEM((ROWS * WIDE, SPAN * BASES * LANES), BF16),
            pltpu.VMEM((2 * CH, CH), F32),
            pltpu.VMEM((2 * CH, CH), BF16),
            pltpu.VMEM((2 * CH, CH), BF16),
            pltpu.VMEM((GROUP, CHUNK, CH), BF16),
            pltpu.VMEM((GROUP, CHUNK, CH), BF16),
            pltpu.VMEM((ZFAR, CHUNK, CH), BF16),
            dma((6,)),
            dma((10,)), dma((10,)), dma((10,)), dma((10,)), dma((2,)), dma((2,)), dma((2,)), dma((2,)),
            dma((GROUP,)), dma((ZFAR,)), dma((GROUP,)), dma((5,)),
            *[pltpu.SemaphoreType.REGULAR] * 5,
        ],
        compiler_params=pltpu.CompilerParams(collective_id=0, has_side_effects=True),
    )(features, cotangent, weight, filter_taps, lat_ext, lon_count)


PIECES = 8


def write_kernel(scale, out_ref, grad_ref, sum_ref, out_any, grad_any, total_any, wide, sem):
    copies = [
        pltpu.make_async_copy(out_ref, out_any, sem.at[PIECES]),
        pltpu.make_async_copy(grad_ref, grad_any, sem.at[PIECES + 1]),
    ]
    for copy in copies:
        copy.start()
    per = 2 * GROUP // PIECES
    for index in range(PIECES):
        side, first = (index * per) // GROUP, (index * per) % GROUP
        wide[side, first : first + per] = sum_ref[side, first : first + per].astype(F32) * scale
        copy = pltpu.make_async_copy(
            wide.at[side, first : first + per], total_any.at[side, first : first + per], sem.at[index]
        )
        copy.start()
        copies.append(copy)
    for copy in copies:
        copy.wait()


def write(scale, output, grad, total):
    vmem = pl.BlockSpec(memory_space=pltpu.VMEM)
    anywhere = pl.BlockSpec(memory_space=pl.ANY)
    return pl.pallas_call(
        lambda *refs: write_kernel(scale, *refs),
        out_shape=[
            jax.ShapeDtypeStruct(output.shape, BF16),
            jax.ShapeDtypeStruct(grad.shape, BF16),
            jax.ShapeDtypeStruct(total.shape, F32),
        ],
        in_specs=[vmem, vmem, vmem],
        out_specs=[anywhere, anywhere, anywhere],
        scratch_shapes=[pltpu.VMEM(total.shape, F32), pltpu.SemaphoreType.DMA((PIECES + 2,))],
        name="write",
    )(*(pltpu.with_memory_space_constraint(held, pltpu.VMEM) for held in (output, grad, total)))


def per_device(features, cotangent, weight, filter_taps, lat_ext, lon_count):
    taps = jnp.transpose(filter_taps, (0, 2, 1, 3))
    output, field_grad, total = layer(features, cotangent, weight, taps, lat_ext, lon_count)
    cells = LATS * ROWS * LONS * WIDE
    output, field_grad, total = write(1.0 / math.sqrt(cells), output, field_grad, total)
    return (output, field_grad, total.reshape(BASES, CH, CH))


def solution(mesh):
    in_specs = (
        P("lat", "lon", None),
        P("lat", "lon", None),
        P(),
        P("lat", None, None, None),
        P("lat"),
        P("lat"),
    )
    out_specs = (P("lat", "lon", None), P("lat", "lon", None), P())
    return jax.shard_map(
        per_device, mesh=mesh, in_specs=in_specs, out_specs=out_specs, check_vma=False
    )
```

```python
import math

import jax
import jax.numpy as jnp
from jax import lax
from jax.experimental import pallas as pl
from jax.experimental.pallas import tpu as pltpu
from jax.sharding import PartitionSpec as P

MESH = pl.DeviceIdType.MESH
GROUP = 32
ZLEN = 16
ZFAR = 8
CHUNK = 16
LATS = 16
LONS = 32
ROWS = 4
REACH = 2
TAPS = 5
WIDE = 32
HALF = 32
BASES = 4
CH = 256
SPAN = ROWS + 2 * REACH
LANES = 128
BF16 = jnp.bfloat16
F32 = jnp.float32


def fill_filters(taps_ref, lat_ref, lon_ref, ft):
    lon_dist = jnp.abs(lax.broadcasted_iota(jnp.int32, (BASES, 2 * HALF), 1) - HALF)
    ft[REACH : REACH + ROWS] = jnp.zeros((ROWS, TAPS, 8, LANES), F32)
    for row in range(ROWS):
        ext, count = lat_ref[row], lon_ref[row]
        size = jnp.full((BASES, 2 * HALF), (2 * ext - 1) * (2 * count - 1), jnp.int32).astype(F32)
        guess = lax.rsqrt(size)
        scale = guess * (1.5 - 0.5 * size * guess * guess)
        scale = jnp.where(lon_dist < count, scale, 0.0)
        for tap in range(TAPS):
            held = jnp.where(abs(tap - REACH) < ext, scale, 0.0)
            taps = taps_ref[row, tap].astype(F32) * held
            ft[REACH + row, tap, 0:BASES, 0 : 2 * HALF] = taps.astype(BF16).astype(F32)


def slanted(base):
    return pltpu.roll(jnp.broadcast_to(base, (WIDE, LANES)), 0, 1, stride=1, stride_axis=0)


def fill_forward(ft, north, south, bands):
    def one(basis, carry):
        start = pl.multiple_of(basis * WIDE, WIDE)
        for row in range(ROWS):
            for tap in range(TAPS):
                line = row + tap
                base = ft[REACH + row, tap, pl.ds(basis, 1), :]
                if line < REACH:
                    base = base * north
                if line >= REACH + ROWS:
                    base = base * south
                bands[row, pl.ds(start, WIDE), tap * LANES : (tap + 1) * LANES] = slanted(
                    base
                ).astype(BF16)
        return carry

    lax.fori_loop(0, BASES, one, 0)


def convolve(bands, fw, bo, first):
    span = pl.ds(pl.multiple_of(first * WIDE, 2 * WIDE), 2 * WIDE)
    for row in range(ROWS):
        patch = fw[row : row + TAPS].reshape(TAPS * LANES, CH)
        sums = jnp.dot(bands[row, span, :], patch, preferred_element_type=F32).astype(BF16)
        bo[pl.ds(first, 2), row * WIDE : (row + 1) * WIDE, :] = sums.reshape(2, WIDE, CH)


def mix(bo, weight_ref, out_ref):
    total = jnp.dot(bo[0], weight_ref[0], preferred_element_type=F32)
    for basis in range(1, BASES):
        total = total + jnp.dot(bo[basis], weight_ref[basis], preferred_element_type=F32)
    out_ref[...] = total.astype(BF16).reshape(ROWS, WIDE, CH)


def fill_basis_grad(cw, weight_ref, bg):
    cells = cw[...].reshape(SPAN * LANES, CH)

    def one(basis, carry):
        grad = lax.dot_general(
            cells, weight_ref[basis], (((1,), (1,)), ((), ())), preferred_element_type=F32
        )
        start = pl.multiple_of(basis * LANES, LANES)
        bg[:, pl.ds(start, LANES), :] = grad.astype(BF16).reshape(SPAN, LANES, CH)
        return carry

    lax.fori_loop(0, BASES, one, 0)


def fill_reversed(ft, north, south, rt):
    first = lax.broadcasted_iota(jnp.int32, (LANES, LANES), 0)
    second = lax.broadcasted_iota(jnp.int32, (LANES, LANES), 1)
    flip = jnp.where(first + second == 2 * HALF, 1.0, 0.0).astype(BF16)
    flat = ft[...].reshape(SPAN * TAPS * 8, LANES).astype(BF16)
    turned = jnp.dot(flat, flip, preferred_element_type=F32)
    rt[...] = turned.reshape(SPAN, TAPS, 8, LANES)
    rt[0:REACH] = rt[0:REACH] * north
    rt[REACH + ROWS :] = rt[REACH + ROWS :] * south


def fill_adjoint(rt, wedge):
    def one(basis, carry):
        for row in range(ROWS):
            for tap in range(TAPS):
                line = row + TAPS - 1 - tap
                base = rt[line, tap, pl.ds(basis, 1), :]
                start = pl.multiple_of((line * BASES + basis) * LANES, LANES)
                wedge[row * WIDE : (row + 1) * WIDE, pl.ds(start, LANES)] = slanted(base).astype(BF16)
        return carry

    lax.fori_loop(0, BASES, one, 0)


def adjoint(wedge, bg, grad_ref):
    flat = bg[...].reshape(SPAN * BASES * LANES, CH)
    total = jnp.dot(wedge[...], flat, preferred_element_type=F32)
    grad_ref[...] = total.astype(BF16).reshape(ROWS, WIDE, CH)


def layer_kernel(
    feat_any, cot_any, weight_any, taps_any, lat_any, lon_any,
    out_ref, grad_ref, sum_ref,
    fw, cw, weight_ref, taps_ref, lat_ref, lon_ref, ft, rt, bands, bo, bg, wedge, part, pair_out, pair_in, half, group_in, zbuf,
    own_sem, feat_send, feat_recv, cot_send, cot_recv, ft_send, ft_recv, pair_send, pair_recv,
    group_recv, z_recv, all_recv, many_sem,
    hop_sem, leap_sem, step_sem, cross_sem, twin_sem,
):
    lat = lax.axis_index("lat")
    lon = lax.axis_index("lon")
    core = lat % 2
    y_lo = (lat // 2) % 2
    x = lat // 4
    z = lon % ZLEN
    z_lo = z % 2
    z_hi = z // 2
    y_hi = lon // ZLEN
    spot = z_lo * 16 + x * 4 + y_hi * 2 + y_lo
    partner = (lat + 1 - 2 * core, lon)

    def across(dx, dy, dz):
        far_x, far_y, far_z = (x + dx) % 4, (y_hi * 2 + y_lo + dy) % 4, (z_lo + dz) % 2
        device = (far_x * 4 + (far_y % 2) * 2 + core, (far_y // 2) * ZLEN + z_hi * 2 + far_z)
        return device, far_z * 16 + far_x * 4 + far_y

    def z_device(index):
        return (lat, y_hi * ZLEN + index)

    def far_device(index):
        return z_device(index * 2 + z_lo)

    def beside(up, right):
        return ((lat + LATS + up) % LATS, (lon + LONS + right) % LONS)

    away = 2 * core - 1
    ways = [(away, 1), (away, -1), (0, 1), (0, -1), (1, 0), (-1, 0)]

    def remote(src, dst, send, recv, device):
        return pltpu.make_async_remote_copy(
            src_ref=src, dst_ref=dst, send_sem=send, recv_sem=recv,
            device_id=device, device_id_type=MESH,
        )

    def signal(sem, device):
        pl.semaphore_signal(sem, inc=1, device_id=device, device_id_type=MESH)

    steps = [(1, 0), (3, 0), (0, 1), (0, 3)]
    barrier = pltpu.get_barrier_semaphore()
    for way in ways:
        signal(barrier, beside(*way))
    for dx, dy in steps:
        signal(barrier, across(dx, dy, 0)[0])
    signal(barrier, z_device((z + 2) % ZLEN))
    signal(barrier, z_device((z + ZLEN - 2) % ZLEN))

    north = jnp.where(lat > 0, 1.0, 0.0)
    south = jnp.where(lat < LATS - 1, 1.0, 0.0)
    inner = slice(REACH, REACH + ROWS)
    middle = slice(WIDE, 2 * WIDE)
    own_copies = [
        pltpu.make_async_copy(feat_any, fw.at[inner, middle], own_sem.at[0]),
        pltpu.make_async_copy(cot_any, cw.at[inner, middle], own_sem.at[1]),
        pltpu.make_async_copy(weight_any, weight_ref, own_sem.at[2]),
        pltpu.make_async_copy(taps_any, taps_ref, own_sem.at[3]),
        pltpu.make_async_copy(lat_any, lat_ref, own_sem.at[4]),
        pltpu.make_async_copy(lon_any, lon_ref, own_sem.at[5]),
    ]
    for copy in own_copies:
        copy.start()
    pl.semaphore_wait(barrier, len(ways) + len(steps) + 2)

    def rows(window, start, left):
        return window.at[pl.ds(start, REACH), left : left + WIDE]

    common, single = REACH * (1 - core), REACH * core
    far = REACH + ROWS

    def halo(source, window, send, recv):
        out, arrive = [], []

        def add(src, start, landing, left, device):
            index = len(out)
            out.append(remote(src, rows(window, start, left), send.at[index], recv.at[index], device))
            place = rows(window, landing, left)
            arrive.append(remote(place, place, send.at[index], recv.at[index], partner))

        for right in (1, -1):
            start = REACH + common
            add(source.at[pl.ds(common, REACH)], start, start, WIDE * (1 - right), beside(0, right))
        for right in (1, -1):
            add(
                source.at[pl.ds(single, REACH)], far * (1 - core), far * core, WIDE * (1 - right),
                beside(away, right),
            )
        for right in (1, -1):
            start = REACH + single
            add(source.at[pl.ds(single, REACH)], start, start, WIDE * (1 - right), beside(0, right))
        add(source.at[ROWS - REACH :], 0, 0, WIDE, beside(1, 0))
        add(source.at[0:REACH], far, far, WIDE, beside(-1, 0))
        for right in (1, -1):
            left = WIDE * (1 - right)
            add(rows(window, REACH + common, left), far * core, far * (1 - core), left, partner)
        return out, arrive

    feat_copies, feat_arrive = halo(feat_any, fw, feat_send, feat_recv)
    cot_copies, cot_arrive = halo(cot_any, cw, cot_send, cot_recv)
    ft_copies = [
        remote(ft.at[ROWS : ROWS + REACH], ft.at[0:REACH], ft_send.at[0], ft_recv.at[0], beside(1, 0)),
        remote(ft.at[REACH : 2 * REACH], ft.at[REACH + ROWS :], ft_send.at[1], ft_recv.at[1], beside(-1, 0)),
    ]
    for copy in feat_copies[:8]:
        copy.start()
    for dx, dy in steps:
        signal(step_sem, across(dx, dy, 0)[0])
    signal(hop_sem, z_device((z + 2) % ZLEN))
    signal(hop_sem, z_device((z + ZLEN - 2) % ZLEN))
    blank = jnp.zeros((SPAN, LANES - 3 * WIDE, CH), BF16)
    fw[:, 3 * WIDE :, :] = blank
    cw[:, 3 * WIDE :, :] = blank
    for copy in own_copies[3:]:
        copy.wait()
    fill_filters(taps_ref, lat_ref, lon_ref, ft)
    fill_forward(ft, north, south, bands)
    wedge[...] = jnp.zeros(wedge.shape, BF16)
    pl.semaphore_wait(step_sem, len(steps))
    signal(cross_sem, across(2, 0, 0)[0])
    signal(cross_sem, across(0, 2, 0)[0])
    pl.semaphore_wait(hop_sem, 2)
    signal(leap_sem, z_device((z + 4) % ZLEN))
    signal(leap_sem, z_device((z + ZLEN - 4) % ZLEN))
    for index in range(2):
        feat_arrive[index].wait_recv()
        feat_copies[8 + index].start()
    pl.semaphore_wait(cross_sem, 2)
    signal(twin_sem, across(0, 0, 1)[0])
    for copy in feat_arrive[2:]:
        copy.wait_recv()
    own_copies[0].wait()
    own_copies[1].wait()
    convolve(bands, fw, bo, (1 - core) * 2)

    cells = cw[inner, middle, :].reshape(ROWS * WIDE, CH)

    def share(basis):
        return lax.dot_general(bo[basis], cells, (((0,), (0,)), ((), ())), preferred_element_type=F32)

    def pair_copy(index):
        span = pl.ds(pl.multiple_of(index * CH, CH), CH)
        return remote(pair_out.at[span], pair_in.at[span], pair_send.at[index], pair_recv.at[index], partner)

    for index in range(2):
        pair_out[index * CH : (index + 1) * CH, :] = share((1 - core) * 2 + index).astype(BF16)
        pair_copy(index).start()
    convolve(bands, fw, bo, core * 2)
    for index in range(2):
        part[index * CH : (index + 1) * CH, :] = share(core * 2 + index)
    per = GROUP // 2
    places = [(dx, dy) for dx in (0, 1, 2, 3) for dy in (0, 1, 2, 3)]
    places.sort(key=lambda p: -(min(p[0], 4 - p[0]) + min(p[1], 4 - p[1])))
    offsets = [(dx, dy, dz) for dx, dy in places for dz in (0, 1)]
    offsets.sort(key=lambda o: -(min(o[0], 4 - o[0]) + min(o[1], 4 - o[1]) + o[2]))

    def group_copy(index, dz):
        device, piece = across(*places[index], dz)
        slot = dz * per + index
        return remote(half.at[piece], group_in.at[slot], many_sem.at[0], group_recv.at[slot], device)

    def group_arrive(slot):
        return remote(
            group_in.at[slot], group_in.at[slot], many_sem.at[0], group_recv.at[slot], partner
        )

    def group_add(slot, carry):
        group_arrive(slot).wait_recv()
        return carry + group_in[slot].astype(F32)

    for index in range(2):
        pair_copy(index).wait_recv()
        span = slice(index * CH, (index + 1) * CH)
        total = part[span, :] + pair_in[span, :].astype(F32)
        half[index * per : (index + 1) * per] = total.astype(BF16).reshape(per, CHUNK, CH)
        if index == 0:
            pl.semaphore_wait(twin_sem, 1)
        turn = (z_lo + index) % 2
        for place in range(per - 1):
            group_copy(place, turn).start()

        @pl.when(turn == 1)
        def _():
            group_copy(per - 1, 1).start()

    for copy in cot_copies[:8] + ft_copies:
        copy.start()
    own_copies[2].wait()
    mix(bo, weight_ref, out_ref)
    chunk = lax.fori_loop(0, per - 1, group_add, half[spot].astype(F32))
    chunk = lax.fori_loop(per, GROUP, group_add, chunk)
    zbuf[z_hi] = chunk.astype(BF16)
    pl.semaphore_wait(leap_sem, 2)

    def z_copy(step):
        return remote(
            zbuf.at[z_hi], zbuf.at[z_hi], many_sem.at[1], z_recv.at[z_hi],
            far_device((z_hi + step) % ZFAR),
        )

    def z_wait(step, carry):
        source = (z_hi + step) % ZFAR
        remote(
            zbuf.at[source], zbuf.at[source], many_sem.at[1], z_recv.at[source], far_device(source)
        ).wait_recv()
        return carry

    for step in (4, 3, 5, 2, 6, 1, 7):
        z_copy(step).start()
    for copy in ft_copies:
        copy.wait_recv()
    for index in range(2):
        cot_arrive[index].wait_recv()
        cot_copies[8 + index].start()
    fill_reversed(ft, north, south, rt)
    fill_adjoint(rt, wedge)
    for copy in cot_arrive[2:]:
        copy.wait_recv()
    fill_basis_grad(cw, weight_ref, bg)
    adjoint(wedge, bg, grad_ref)
    lax.fori_loop(1, ZFAR, z_wait, 0)
    chunk = zbuf[0].astype(F32)
    for source in range(1, ZFAR):
        chunk = chunk + zbuf[source].astype(F32)
    sum_ref[core, spot] = chunk.astype(BF16)

    def all_copy(step):
        return remote(
            sum_ref.at[core, spot], sum_ref.at[core, spot], many_sem.at[2], all_recv.at[step],
            across(*offsets[step])[0],
        )

    def near_copy(index):
        return remote(
            sum_ref.at[core, index], sum_ref.at[core, index], many_sem.at[3], many_sem.at[4], partner
        )

    for step in range(GROUP - 1):
        all_copy(step).start()
    near_copy(spot).start()
    for copy in feat_copies + cot_copies + ft_copies:
        copy.wait_send()
    for index in range(2):
        pair_copy(index).wait_send()
    remote(
        half.at[0 : GROUP - 1], group_in.at[0 : GROUP - 1], many_sem.at[0], group_recv.at[0], partner
    ).wait_send()
    remote(
        zbuf.at[0 : ZFAR - 1], zbuf.at[0 : ZFAR - 1], many_sem.at[1], z_recv.at[0], partner
    ).wait_send()
    for step in range(GROUP - 1):
        dx, dy, dz = offsets[step]
        source = across(4 - dx, 4 - dy, dz)[1]
        remote(
            sum_ref.at[core, source], sum_ref.at[core, source], many_sem.at[2], all_recv.at[step],
            partner,
        ).wait_recv()
        near_copy(source).start()
    remote(
        sum_ref.at[core, 0 : GROUP - 1], sum_ref.at[core, 0 : GROUP - 1], many_sem.at[2],
        all_recv.at[0], partner,
    ).wait_send()
    near_all = remote(
        sum_ref.at[core], sum_ref.at[1 - core], many_sem.at[3], many_sem.at[4], partner
    )
    near_all.wait_send()
    near_all.wait_recv()


def layer(features, cotangent, weight, filter_taps, lat_ext, lon_count):
    dma = pltpu.SemaphoreType.DMA
    vmem = pl.BlockSpec(memory_space=pltpu.VMEM)
    anywhere = pl.BlockSpec(memory_space=pl.ANY)
    return pl.pallas_call(
        layer_kernel,
        out_shape=[
            pltpu.VMEM((ROWS, WIDE, CH), BF16),
            pltpu.VMEM((ROWS, WIDE, CH), BF16),
            pltpu.VMEM((2, GROUP, CHUNK, CH), BF16),
        ],
        in_specs=[anywhere] * 6,
        out_specs=[vmem, vmem, vmem],
        scratch_shapes=[
            pltpu.VMEM((SPAN, LANES, CH), BF16),
            pltpu.VMEM((SPAN, LANES, CH), BF16),
            pltpu.VMEM((BASES, CH, CH), BF16),
            pltpu.VMEM((ROWS, TAPS, BASES, 2 * HALF), BF16),
            pltpu.SMEM((ROWS,), jnp.int32),
            pltpu.SMEM((ROWS,), jnp.int32),
            pltpu.VMEM((SPAN, TAPS, 8, LANES), F32),
            pltpu.VMEM((SPAN, TAPS, 8, LANES), F32),
            pltpu.VMEM((ROWS, BASES * WIDE, TAPS * LANES), BF16),
            pltpu.VMEM((BASES, ROWS * WIDE, CH), BF16),
            pltpu.VMEM((SPAN, BASES * LANES, CH), BF16),
            pltpu.VMEM((ROWS * WIDE, SPAN * BASES * LANES), BF16),
            pltpu.VMEM((2 * CH, CH), F32),
            pltpu.VMEM((2 * CH, CH), BF16),
            pltpu.VMEM((2 * CH, CH), BF16),
            pltpu.VMEM((GROUP, CHUNK, CH), BF16),
            pltpu.VMEM((GROUP, CHUNK, CH), BF16),
            pltpu.VMEM((ZFAR, CHUNK, CH), BF16),
            dma((6,)),
            dma((10,)), dma((10,)), dma((10,)), dma((10,)), dma((2,)), dma((2,)), dma((2,)), dma((2,)),
            dma((GROUP,)), dma((ZFAR,)), dma((GROUP,)), dma((5,)),
            *[pltpu.SemaphoreType.REGULAR] * 5,
        ],
        compiler_params=pltpu.CompilerParams(collective_id=0, has_side_effects=True),
    )(features, cotangent, weight, filter_taps, lat_ext, lon_count)


PIECES = 8


def write_kernel(scale, out_ref, grad_ref, sum_ref, out_any, grad_any, total_any, wide, sem):
    copies = [
        pltpu.make_async_copy(out_ref, out_any, sem.at[PIECES]),
        pltpu.make_async_copy(grad_ref, grad_any, sem.at[PIECES + 1]),
    ]
    for copy in copies:
        copy.start()
    per = 2 * GROUP // PIECES
    for index in range(PIECES):
        side, first = (index * per) // GROUP, (index * per) % GROUP
        wide[side, first : first + per] = sum_ref[side, first : first + per].astype(F32) * scale
        copy = pltpu.make_async_copy(
            wide.at[side, first : first + per], total_any.at[side, first : first + per], sem.at[index]
        )
        copy.start()
        copies.append(copy)
    for copy in copies:
        copy.wait()


def write(scale, output, grad, total):
    vmem = pl.BlockSpec(memory_space=pltpu.VMEM)
    anywhere = pl.BlockSpec(memory_space=pl.ANY)
    return pl.pallas_call(
        lambda *refs: write_kernel(scale, *refs),
        out_shape=[
            jax.ShapeDtypeStruct(output.shape, BF16),
            jax.ShapeDtypeStruct(grad.shape, BF16),
            jax.ShapeDtypeStruct(total.shape, F32),
        ],
        in_specs=[vmem, vmem, vmem],
        out_specs=[anywhere, anywhere, anywhere],
        scratch_shapes=[pltpu.VMEM(total.shape, F32), pltpu.SemaphoreType.DMA((PIECES + 2,))],
        name="write",
    )(*(pltpu.with_memory_space_constraint(held, pltpu.VMEM) for held in (output, grad, total)))


def per_device(features, cotangent, weight, filter_taps, lat_ext, lon_count):
    taps = jnp.transpose(filter_taps, (0, 2, 1, 3))
    output, field_grad, total = layer(features, cotangent, weight, taps, lat_ext, lon_count)
    cells = LATS * ROWS * LONS * WIDE
    output, field_grad, total = write(1.0 / math.sqrt(cells), output, field_grad, total)
    return (output, field_grad, total.reshape(BASES, CH, CH))


def solution(mesh):
    in_specs = (
        P("lat", "lon", None),
        P("lat", "lon", None),
        P(),
        P("lat", None, None, None),
        P("lat"),
        P("lat"),
    )
    out_specs = (P("lat", "lon", None), P("lat", "lon", None), P())
    return jax.shard_map(
        per_device, mesh=mesh, in_specs=in_specs, out_specs=out_specs, check_vma=False
    )
```

```python
import math

import jax
import jax.numpy as jnp
from jax import lax
from jax.experimental import pallas as pl
from jax.experimental.pallas import tpu as pltpu
from jax.sharding import PartitionSpec as P

MESH = pl.DeviceIdType.MESH
GROUP = 32
ZLEN = 16
ZFAR = 8
CHUNK = 16
LATS = 16
LONS = 32
ROWS = 4
REACH = 2
TAPS = 5
WIDE = 32
HALF = 32
BASES = 4
CH = 256
SPAN = ROWS + 2 * REACH
LANES = 128
BF16 = jnp.bfloat16
F32 = jnp.float32


def fill_filters(taps_ref, lat_ref, lon_ref, ft):
    lon_dist = jnp.abs(lax.broadcasted_iota(jnp.int32, (BASES, 2 * HALF), 1) - HALF)
    ft[REACH : REACH + ROWS] = jnp.zeros((ROWS, TAPS, 8, LANES), F32)
    for row in range(ROWS):
        ext, count = lat_ref[row], lon_ref[row]
        size = jnp.full((BASES, 2 * HALF), (2 * ext - 1) * (2 * count - 1), jnp.int32).astype(F32)
        guess = lax.rsqrt(size)
        scale = guess * (1.5 - 0.5 * size * guess * guess)
        scale = jnp.where(lon_dist < count, scale, 0.0)
        for tap in range(TAPS):
            held = jnp.where(abs(tap - REACH) < ext, scale, 0.0)
            taps = taps_ref[row, tap].astype(F32) * held
            ft[REACH + row, tap, 0:BASES, 0 : 2 * HALF] = taps.astype(BF16).astype(F32)


def slanted(base):
    return pltpu.roll(jnp.broadcast_to(base, (WIDE, LANES)), 0, 1, stride=1, stride_axis=0)


def fill_forward(ft, north, south, bands):
    def one(basis, carry):
        start = pl.multiple_of(basis * WIDE, WIDE)
        for row in range(ROWS):
            for tap in range(TAPS):
                line = row + tap
                base = ft[REACH + row, tap, pl.ds(basis, 1), :]
                if line < REACH:
                    base = base * north
                if line >= REACH + ROWS:
                    base = base * south
                bands[row, pl.ds(start, WIDE), tap * LANES : (tap + 1) * LANES] = slanted(
                    base
                ).astype(BF16)
        return carry

    lax.fori_loop(0, BASES, one, 0)


def convolve(bands, fw, bo, first):
    span = pl.ds(pl.multiple_of(first * WIDE, 2 * WIDE), 2 * WIDE)
    for row in range(ROWS):
        patch = fw[row : row + TAPS].reshape(TAPS * LANES, CH)
        sums = jnp.dot(bands[row, span, :], patch, preferred_element_type=F32).astype(BF16)
        bo[pl.ds(first, 2), row * WIDE : (row + 1) * WIDE, :] = sums.reshape(2, WIDE, CH)


def mix(bo, weight_ref, out_ref):
    total = jnp.dot(bo[0], weight_ref[0], preferred_element_type=F32)
    for basis in range(1, BASES):
        total = total + jnp.dot(bo[basis], weight_ref[basis], preferred_element_type=F32)
    out_ref[...] = total.astype(BF16).reshape(ROWS, WIDE, CH)


def fill_basis_grad(cw, weight_ref, bg):
    cells = cw[...].reshape(SPAN * LANES, CH)

    def one(basis, carry):
        grad = lax.dot_general(
            cells, weight_ref[basis], (((1,), (1,)), ((), ())), preferred_element_type=F32
        )
        start = pl.multiple_of(basis * LANES, LANES)
        bg[:, pl.ds(start, LANES), :] = grad.astype(BF16).reshape(SPAN, LANES, CH)
        return carry

    lax.fori_loop(0, BASES, one, 0)


def fill_reversed(ft, north, south, rt):
    first = lax.broadcasted_iota(jnp.int32, (LANES, LANES), 0)
    second = lax.broadcasted_iota(jnp.int32, (LANES, LANES), 1)
    flip = jnp.where(first + second == 2 * HALF, 1.0, 0.0).astype(BF16)
    flat = ft[...].reshape(SPAN * TAPS * 8, LANES).astype(BF16)
    turned = jnp.dot(flat, flip, preferred_element_type=F32)
    rt[...] = turned.reshape(SPAN, TAPS, 8, LANES)
    rt[0:REACH] = rt[0:REACH] * north
    rt[REACH + ROWS :] = rt[REACH + ROWS :] * south


def fill_adjoint(rt, wedge):
    def one(basis, carry):
        for row in range(ROWS):
            for tap in range(TAPS):
                line = row + TAPS - 1 - tap
                base = rt[line, tap, pl.ds(basis, 1), :]
                start = pl.multiple_of((line * BASES + basis) * LANES, LANES)
                wedge[row * WIDE : (row + 1) * WIDE, pl.ds(start, LANES)] = slanted(base).astype(BF16)
        return carry

    lax.fori_loop(0, BASES, one, 0)


def adjoint(wedge, bg, grad_ref):
    flat = bg[...].reshape(SPAN * BASES * LANES, CH)
    total = jnp.dot(wedge[...], flat, preferred_element_type=F32)
    grad_ref[...] = total.astype(BF16).reshape(ROWS, WIDE, CH)


def layer_kernel(
    feat_any, cot_any, weight_any, taps_any, lat_any, lon_any,
    out_ref, grad_ref, sum_ref,
    fw, cw, weight_ref, taps_ref, lat_ref, lon_ref, ft, rt, bands, bo, bg, wedge, part, pair_out, pair_in, half, group_in, zbuf,
    own_sem, feat_send, feat_recv, cot_send, cot_recv, ft_send, ft_recv, pair_send, pair_recv,
    group_recv, z_recv, all_recv, many_sem,
    hop_sem, leap_sem, step_sem, cross_sem, twin_sem,
):
    lat = lax.axis_index("lat")
    lon = lax.axis_index("lon")
    core = lat % 2
    y_lo = (lat // 2) % 2
    x = lat // 4
    z = lon % ZLEN
    z_lo = z % 2
    z_hi = z // 2
    y_hi = lon // ZLEN
    spot = z_lo * 16 + x * 4 + y_hi * 2 + y_lo
    partner = (lat + 1 - 2 * core, lon)

    def across(dx, dy, dz):
        far_x, far_y, far_z = (x + dx) % 4, (y_hi * 2 + y_lo + dy) % 4, (z_lo + dz) % 2
        device = (far_x * 4 + (far_y % 2) * 2 + core, (far_y // 2) * ZLEN + z_hi * 2 + far_z)
        return device, far_z * 16 + far_x * 4 + far_y

    def z_device(index):
        return (lat, y_hi * ZLEN + index)

    def far_device(index):
        return z_device(index * 2 + z_lo)

    def beside(up, right):
        return ((lat + LATS + up) % LATS, (lon + LONS + right) % LONS)

    away = 2 * core - 1
    ways = [(away, 1), (away, -1), (0, 1), (0, -1), (1, 0), (-1, 0)]

    def remote(src, dst, send, recv, device):
        return pltpu.make_async_remote_copy(
            src_ref=src, dst_ref=dst, send_sem=send, recv_sem=recv,
            device_id=device, device_id_type=MESH,
        )

    def signal(sem, device):
        pl.semaphore_signal(sem, inc=1, device_id=device, device_id_type=MESH)

    steps = [(1, 0), (3, 0), (0, 1), (0, 3)]
    barrier = pltpu.get_barrier_semaphore()
    for way in ways:
        signal(barrier, beside(*way))
    for dx, dy in steps:
        signal(barrier, across(dx, dy, 0)[0])
    signal(barrier, z_device((z + 2) % ZLEN))
    signal(barrier, z_device((z + ZLEN - 2) % ZLEN))

    north = jnp.where(lat > 0, 1.0, 0.0)
    south = jnp.where(lat < LATS - 1, 1.0, 0.0)
    inner = slice(REACH, REACH + ROWS)
    middle = slice(WIDE, 2 * WIDE)
    own_copies = [
        pltpu.make_async_copy(feat_any, fw.at[inner, middle], own_sem.at[0]),
        pltpu.make_async_copy(cot_any, cw.at[inner, middle], own_sem.at[1]),
        pltpu.make_async_copy(weight_any, weight_ref, own_sem.at[2]),
        pltpu.make_async_copy(taps_any, taps_ref, own_sem.at[3]),
        pltpu.make_async_copy(lat_any, lat_ref, own_sem.at[4]),
        pltpu.make_async_copy(lon_any, lon_ref, own_sem.at[5]),
    ]
    for copy in own_copies:
        copy.start()
    pl.semaphore_wait(barrier, len(ways) + len(steps) + 2)

    def rows(window, start, left):
        return window.at[pl.ds(start, REACH), left : left + WIDE]

    common, single = REACH * (1 - core), REACH * core
    far = REACH + ROWS

    def halo(source, window, send, recv):
        out, arrive = [], []

        def add(src, start, landing, left, device):
            index = len(out)
            out.append(remote(src, rows(window, start, left), send.at[index], recv.at[index], device))
            place = rows(window, landing, left)
            arrive.append(remote(place, place, send.at[index], recv.at[index], partner))

        for right in (1, -1):
            start = REACH + common
            add(source.at[pl.ds(common, REACH)], start, start, WIDE * (1 - right), beside(0, right))
        for right in (1, -1):
            add(
                source.at[pl.ds(single, REACH)], far * (1 - core), far * core, WIDE * (1 - right),
                beside(away, right),
            )
        for right in (1, -1):
            start = REACH + single
            add(source.at[pl.ds(single, REACH)], start, start, WIDE * (1 - right), beside(0, right))
        add(source.at[ROWS - REACH :], 0, 0, WIDE, beside(1, 0))
        add(source.at[0:REACH], far, far, WIDE, beside(-1, 0))
        for right in (1, -1):
            left = WIDE * (1 - right)
            add(rows(window, REACH + common, left), far * core, far * (1 - core), left, partner)
        return out, arrive

    feat_copies, feat_arrive = halo(feat_any, fw, feat_send, feat_recv)
    cot_copies, cot_arrive = halo(cot_any, cw, cot_send, cot_recv)
    ft_copies = [
        remote(ft.at[ROWS : ROWS + REACH], ft.at[0:REACH], ft_send.at[0], ft_recv.at[0], beside(1, 0)),
        remote(ft.at[REACH : 2 * REACH], ft.at[REACH + ROWS :], ft_send.at[1], ft_recv.at[1], beside(-1, 0)),
    ]
    for copy in feat_copies[:8]:
        copy.start()
    for dx, dy in steps:
        signal(step_sem, across(dx, dy, 0)[0])
    signal(hop_sem, z_device((z + 2) % ZLEN))
    signal(hop_sem, z_device((z + ZLEN - 2) % ZLEN))
    blank = jnp.zeros((SPAN, LANES - 3 * WIDE, CH), BF16)
    fw[:, 3 * WIDE :, :] = blank
    cw[:, 3 * WIDE :, :] = blank
    for copy in own_copies[3:]:
        copy.wait()
    fill_filters(taps_ref, lat_ref, lon_ref, ft)
    pl.semaphore_wait(step_sem, len(steps))
    signal(cross_sem, across(2, 0, 0)[0])
    signal(cross_sem, across(0, 2, 0)[0])
    pl.semaphore_wait(hop_sem, 2)
    signal(leap_sem, z_device((z + 4) % ZLEN))
    signal(leap_sem, z_device((z + ZLEN - 4) % ZLEN))
    fill_forward(ft, north, south, bands)
    wedge[...] = jnp.zeros(wedge.shape, BF16)
    for index in range(2):
        feat_arrive[index].wait_recv()
        feat_copies[8 + index].start()
    pl.semaphore_wait(cross_sem, 2)
    signal(twin_sem, across(0, 0, 1)[0])
    for copy in feat_arrive[2:]:
        copy.wait_recv()
    own_copies[0].wait()
    own_copies[1].wait()
    convolve(bands, fw, bo, (1 - core) * 2)

    cells = cw[inner, middle, :].reshape(ROWS * WIDE, CH)

    def share(basis):
        return lax.dot_general(bo[basis], cells, (((0,), (0,)), ((), ())), preferred_element_type=F32)

    def pair_copy(index):
        span = pl.ds(pl.multiple_of(index * CH, CH), CH)
        return remote(pair_out.at[span], pair_in.at[span], pair_send.at[index], pair_recv.at[index], partner)

    for index in range(2):
        pair_out[index * CH : (index + 1) * CH, :] = share((1 - core) * 2 + index).astype(BF16)
        pair_copy(index).start()
    convolve(bands, fw, bo, core * 2)
    for index in range(2):
        part[index * CH : (index + 1) * CH, :] = share(core * 2 + index)
    per = GROUP // 2
    places = [(dx, dy) for dx in (0, 1, 2, 3) for dy in (0, 1, 2, 3)]
    places.sort(key=lambda p: -(min(p[0], 4 - p[0]) + min(p[1], 4 - p[1])))
    offsets = [(dx, dy, dz) for dx, dy in places for dz in (0, 1)]
    offsets.sort(key=lambda o: -(min(o[0], 4 - o[0]) + min(o[1], 4 - o[1]) + o[2]))

    def group_copy(index, dz):
        device, piece = across(*places[index], dz)
        slot = dz * per + index
        return remote(half.at[piece], group_in.at[slot], many_sem.at[0], group_recv.at[slot], device)

    def group_arrive(slot):
        return remote(
            group_in.at[slot], group_in.at[slot], many_sem.at[0], group_recv.at[slot], partner
        )

    def group_add(slot, carry):
        group_arrive(slot).wait_recv()
        return carry + group_in[slot].astype(F32)

    for index in range(2):
        pair_copy(index).wait_recv()
        span = slice(index * CH, (index + 1) * CH)
        total = part[span, :] + pair_in[span, :].astype(F32)
        half[index * per : (index + 1) * per] = total.astype(BF16).reshape(per, CHUNK, CH)
        if index == 0:
            pl.semaphore_wait(twin_sem, 1)
        turn = (z_lo + index) % 2
        for place in range(per - 1):
            group_copy(place, turn).start()

        @pl.when(turn == 1)
        def _():
            group_copy(per - 1, 1).start()

    for copy in cot_copies[:8] + ft_copies:
        copy.start()
    own_copies[2].wait()
    mix(bo, weight_ref, out_ref)
    chunk = lax.fori_loop(0, per - 1, group_add, half[spot].astype(F32))
    chunk = lax.fori_loop(per, GROUP, group_add, chunk)
    zbuf[z_hi] = chunk.astype(BF16)
    pl.semaphore_wait(leap_sem, 2)

    def z_copy(step):
        return remote(
            zbuf.at[z_hi], zbuf.at[z_hi], many_sem.at[1], z_recv.at[z_hi],
            far_device((z_hi + step) % ZFAR),
        )

    def z_wait(step, carry):
        source = (z_hi + step) % ZFAR
        remote(
            zbuf.at[source], zbuf.at[source], many_sem.at[1], z_recv.at[source], far_device(source)
        ).wait_recv()
        return carry

    for step in (4, 3, 5, 2, 6, 1, 7):
        z_copy(step).start()
    for copy in ft_copies:
        copy.wait_recv()
    for index in range(2):
        cot_arrive[index].wait_recv()
        cot_copies[8 + index].start()
    fill_reversed(ft, north, south, rt)
    fill_adjoint(rt, wedge)
    for copy in cot_arrive[2:]:
        copy.wait_recv()
    fill_basis_grad(cw, weight_ref, bg)
    adjoint(wedge, bg, grad_ref)
    lax.fori_loop(1, ZFAR, z_wait, 0)
    chunk = zbuf[0].astype(F32)
    for source in range(1, ZFAR):
        chunk = chunk + zbuf[source].astype(F32)
    sum_ref[core, spot] = chunk.astype(BF16)

    def all_copy(step):
        return remote(
            sum_ref.at[core, spot], sum_ref.at[core, spot], many_sem.at[2], all_recv.at[step],
            across(*offsets[step])[0],
        )

    def near_copy(index):
        return remote(
            sum_ref.at[core, index], sum_ref.at[core, index], many_sem.at[3], many_sem.at[4], partner
        )

    for step in range(GROUP - 1):
        all_copy(step).start()
    near_copy(spot).start()
    for copy in feat_copies + cot_copies + ft_copies:
        copy.wait_send()
    for index in range(2):
        pair_copy(index).wait_send()
    remote(
        half.at[0 : GROUP - 1], group_in.at[0 : GROUP - 1], many_sem.at[0], group_recv.at[0], partner
    ).wait_send()
    remote(
        zbuf.at[0 : ZFAR - 1], zbuf.at[0 : ZFAR - 1], many_sem.at[1], z_recv.at[0], partner
    ).wait_send()
    for step in range(GROUP - 1):
        dx, dy, dz = offsets[step]
        source = across(4 - dx, 4 - dy, dz)[1]
        remote(
            sum_ref.at[core, source], sum_ref.at[core, source], many_sem.at[2], all_recv.at[step],
            partner,
        ).wait_recv()
        near_copy(source).start()
    remote(
        sum_ref.at[core, 0 : GROUP - 1], sum_ref.at[core, 0 : GROUP - 1], many_sem.at[2],
        all_recv.at[0], partner,
    ).wait_send()
    near_all = remote(
        sum_ref.at[core], sum_ref.at[1 - core], many_sem.at[3], many_sem.at[4], partner
    )
    near_all.wait_send()
    near_all.wait_recv()


def layer(features, cotangent, weight, filter_taps, lat_ext, lon_count):
    dma = pltpu.SemaphoreType.DMA
    vmem = pl.BlockSpec(memory_space=pltpu.VMEM)
    anywhere = pl.BlockSpec(memory_space=pl.ANY)
    return pl.pallas_call(
        layer_kernel,
        out_shape=[
            pltpu.VMEM((ROWS, WIDE, CH), BF16),
            pltpu.VMEM((ROWS, WIDE, CH), BF16),
            pltpu.VMEM((2, GROUP, CHUNK, CH), BF16),
        ],
        in_specs=[anywhere] * 6,
        out_specs=[vmem, vmem, vmem],
        scratch_shapes=[
            pltpu.VMEM((SPAN, LANES, CH), BF16),
            pltpu.VMEM((SPAN, LANES, CH), BF16),
            pltpu.VMEM((BASES, CH, CH), BF16),
            pltpu.VMEM((ROWS, TAPS, BASES, 2 * HALF), BF16),
            pltpu.SMEM((ROWS,), jnp.int32),
            pltpu.SMEM((ROWS,), jnp.int32),
            pltpu.VMEM((SPAN, TAPS, 8, LANES), F32),
            pltpu.VMEM((SPAN, TAPS, 8, LANES), F32),
            pltpu.VMEM((ROWS, BASES * WIDE, TAPS * LANES), BF16),
            pltpu.VMEM((BASES, ROWS * WIDE, CH), BF16),
            pltpu.VMEM((SPAN, BASES * LANES, CH), BF16),
            pltpu.VMEM((ROWS * WIDE, SPAN * BASES * LANES), BF16),
            pltpu.VMEM((2 * CH, CH), F32),
            pltpu.VMEM((2 * CH, CH), BF16),
            pltpu.VMEM((2 * CH, CH), BF16),
            pltpu.VMEM((GROUP, CHUNK, CH), BF16),
            pltpu.VMEM((GROUP, CHUNK, CH), BF16),
            pltpu.VMEM((ZFAR, CHUNK, CH), BF16),
            dma((6,)),
            dma((10,)), dma((10,)), dma((10,)), dma((10,)), dma((2,)), dma((2,)), dma((2,)), dma((2,)),
            dma((GROUP,)), dma((ZFAR,)), dma((GROUP,)), dma((5,)),
            *[pltpu.SemaphoreType.REGULAR] * 5,
        ],
        compiler_params=pltpu.CompilerParams(collective_id=0, has_side_effects=True),
    )(features, cotangent, weight, filter_taps, lat_ext, lon_count)


PIECES = 8


def write_kernel(scale, out_ref, grad_ref, sum_ref, out_any, grad_any, total_any, wide, sem):
    copies = [
        pltpu.make_async_copy(out_ref, out_any, sem.at[PIECES]),
        pltpu.make_async_copy(grad_ref, grad_any, sem.at[PIECES + 1]),
    ]
    for copy in copies:
        copy.start()
    per = 2 * GROUP // PIECES
    for index in range(PIECES):
        side, first = (index * per) // GROUP, (index * per) % GROUP
        wide[side, first : first + per] = sum_ref[side, first : first + per].astype(F32) * scale
        copy = pltpu.make_async_copy(
            wide.at[side, first : first + per], total_any.at[side, first : first + per], sem.at[index]
        )
        copy.start()
        copies.append(copy)
    for copy in copies:
        copy.wait()


def write(scale, output, grad, total):
    vmem = pl.BlockSpec(memory_space=pltpu.VMEM)
    anywhere = pl.BlockSpec(memory_space=pl.ANY)
    return pl.pallas_call(
        lambda *refs: write_kernel(scale, *refs),
        out_shape=[
            jax.ShapeDtypeStruct(output.shape, BF16),
            jax.ShapeDtypeStruct(grad.shape, BF16),
            jax.ShapeDtypeStruct(total.shape, F32),
        ],
        in_specs=[vmem, vmem, vmem],
        out_specs=[anywhere, anywhere, anywhere],
        scratch_shapes=[pltpu.VMEM(total.shape, F32), pltpu.SemaphoreType.DMA((PIECES + 2,))],
        name="write",
    )(*(pltpu.with_memory_space_constraint(held, pltpu.VMEM) for held in (output, grad, total)))


def per_device(features, cotangent, weight, filter_taps, lat_ext, lon_count):
    taps = jnp.transpose(filter_taps, (0, 2, 1, 3))
    output, field_grad, total = layer(features, cotangent, weight, taps, lat_ext, lon_count)
    cells = LATS * ROWS * LONS * WIDE
    output, field_grad, total = write(1.0 / math.sqrt(cells), output, field_grad, total)
    return (output, field_grad, total.reshape(BASES, CH, CH))


def solution(mesh):
    in_specs = (
        P("lat", "lon", None),
        P("lat", "lon", None),
        P(),
        P("lat", None, None, None),
        P("lat"),
        P("lat"),
    )
    out_specs = (P("lat", "lon", None), P("lat", "lon", None), P())
    return jax.shard_map(
        per_device, mesh=mesh, in_specs=in_specs, out_specs=out_specs, check_vma=False
    )
```

```python
import math

import jax
import jax.numpy as jnp
from jax import lax
from jax.experimental import pallas as pl
from jax.experimental.pallas import tpu as pltpu
from jax.sharding import PartitionSpec as P

MESH = pl.DeviceIdType.MESH
GROUP = 32
ZLEN = 16
ZFAR = 8
CHUNK = 16
LATS = 16
LONS = 32
ROWS = 4
REACH = 2
TAPS = 5
WIDE = 32
HALF = 32
BASES = 4
CH = 256
SPAN = ROWS + 2 * REACH
LANES = 128
BF16 = jnp.bfloat16
F32 = jnp.float32


def fill_filters(taps_ref, lat_ref, lon_ref, ft):
    lon_dist = jnp.abs(lax.broadcasted_iota(jnp.int32, (BASES, 2 * HALF), 1) - HALF)
    ft[REACH : REACH + ROWS] = jnp.zeros((ROWS, TAPS, 8, LANES), F32)
    for row in range(ROWS):
        ext, count = lat_ref[row], lon_ref[row]
        size = jnp.full((BASES, 2 * HALF), (2 * ext - 1) * (2 * count - 1), jnp.int32).astype(F32)
        guess = lax.rsqrt(size)
        scale = guess * (1.5 - 0.5 * size * guess * guess)
        scale = jnp.where(lon_dist < count, scale, 0.0)
        for tap in range(TAPS):
            held = jnp.where(abs(tap - REACH) < ext, scale, 0.0)
            taps = taps_ref[row, tap].astype(F32) * held
            ft[REACH + row, tap, 0:BASES, 0 : 2 * HALF] = taps.astype(BF16).astype(F32)


def slanted(base):
    return pltpu.roll(jnp.broadcast_to(base, (WIDE, LANES)), 0, 1, stride=1, stride_axis=0)


def fill_forward(ft, north, south, bands):
    def one(basis, carry):
        start = pl.multiple_of(basis * WIDE, WIDE)
        for row in range(ROWS):
            for tap in range(TAPS):
                line = row + tap
                base = ft[REACH + row, tap, pl.ds(basis, 1), :]
                if line < REACH:
                    base = base * north
                if line >= REACH + ROWS:
                    base = base * south
                bands[row, pl.ds(start, WIDE), tap * LANES : (tap + 1) * LANES] = slanted(
                    base
                ).astype(BF16)
        return carry

    lax.fori_loop(0, BASES, one, 0)


def convolve(bands, fw, bo, first):
    span = pl.ds(pl.multiple_of(first * WIDE, 2 * WIDE), 2 * WIDE)
    for row in range(ROWS):
        patch = fw[row : row + TAPS].reshape(TAPS * LANES, CH)
        sums = jnp.dot(bands[row, span, :], patch, preferred_element_type=F32).astype(BF16)
        bo[pl.ds(first, 2), row * WIDE : (row + 1) * WIDE, :] = sums.reshape(2, WIDE, CH)


def mix(bo, weight_ref, out_ref):
    total = jnp.dot(bo[0], weight_ref[0], preferred_element_type=F32)
    for basis in range(1, BASES):
        total = total + jnp.dot(bo[basis], weight_ref[basis], preferred_element_type=F32)
    out_ref[...] = total.astype(BF16).reshape(ROWS, WIDE, CH)


def fill_basis_grad(cw, weight_ref, bg):
    cells = cw[...].reshape(SPAN * LANES, CH)

    def one(basis, carry):
        grad = lax.dot_general(
            cells, weight_ref[basis], (((1,), (1,)), ((), ())), preferred_element_type=F32
        )
        start = pl.multiple_of(basis * LANES, LANES)
        bg[:, pl.ds(start, LANES), :] = grad.astype(BF16).reshape(SPAN, LANES, CH)
        return carry

    lax.fori_loop(0, BASES, one, 0)


def fill_reversed(ft, north, south, rt):
    first = lax.broadcasted_iota(jnp.int32, (LANES, LANES), 0)
    second = lax.broadcasted_iota(jnp.int32, (LANES, LANES), 1)
    flip = jnp.where(first + second == 2 * HALF, 1.0, 0.0).astype(BF16)
    flat = ft[...].reshape(SPAN * TAPS * 8, LANES).astype(BF16)
    turned = jnp.dot(flat, flip, preferred_element_type=F32)
    rt[...] = turned.reshape(SPAN, TAPS, 8, LANES)
    rt[0:REACH] = rt[0:REACH] * north
    rt[REACH + ROWS :] = rt[REACH + ROWS :] * south


def fill_adjoint(rt, wedge):
    def one(basis, carry):
        for row in range(ROWS):
            for tap in range(TAPS):
                line = row + TAPS - 1 - tap
                base = rt[line, tap, pl.ds(basis, 1), :]
                start = pl.multiple_of((line * BASES + basis) * LANES, LANES)
                wedge[row * WIDE : (row + 1) * WIDE, pl.ds(start, LANES)] = slanted(base).astype(BF16)
        return carry

    lax.fori_loop(0, BASES, one, 0)


def adjoint(wedge, bg, grad_ref):
    flat = bg[...].reshape(SPAN * BASES * LANES, CH)
    total = jnp.dot(wedge[...], flat, preferred_element_type=F32)
    grad_ref[...] = total.astype(BF16).reshape(ROWS, WIDE, CH)


def layer_kernel(
    feat_any, cot_any, weight_any, taps_any, lat_any, lon_any,
    out_ref, grad_ref, sum_ref,
    fw, cw, weight_ref, taps_ref, lat_ref, lon_ref, ft, rt, bands, bo, bg, wedge, part, pair_out, pair_in, half, group_in, zbuf,
    own_sem, feat_send, feat_recv, cot_send, cot_recv, ft_send, ft_recv, pair_send, pair_recv,
    group_recv, z_recv, all_recv, many_sem,
    hop_sem, leap_sem, step_sem, cross_sem, twin_sem,
):
    lat = lax.axis_index("lat")
    lon = lax.axis_index("lon")
    core = lat % 2
    y_lo = (lat // 2) % 2
    x = lat // 4
    z = lon % ZLEN
    z_lo = z % 2
    z_hi = z // 2
    y_hi = lon // ZLEN
    spot = z_lo * 16 + x * 4 + y_hi * 2 + y_lo
    partner = (lat + 1 - 2 * core, lon)

    def across(dx, dy, dz):
        far_x, far_y, far_z = (x + dx) % 4, (y_hi * 2 + y_lo + dy) % 4, (z_lo + dz) % 2
        device = (far_x * 4 + (far_y % 2) * 2 + core, (far_y // 2) * ZLEN + z_hi * 2 + far_z)
        return device, far_z * 16 + far_x * 4 + far_y

    def z_device(index):
        return (lat, y_hi * ZLEN + index)

    def far_device(index):
        return z_device(index * 2 + z_lo)

    def beside(up, right):
        return ((lat + LATS + up) % LATS, (lon + LONS + right) % LONS)

    away = 2 * core - 1
    ways = [(away, 1), (away, -1), (0, 1), (0, -1), (1, 0), (-1, 0)]

    def remote(src, dst, send, recv, device):
        return pltpu.make_async_remote_copy(
            src_ref=src, dst_ref=dst, send_sem=send, recv_sem=recv,
            device_id=device, device_id_type=MESH,
        )

    def signal(sem, device):
        pl.semaphore_signal(sem, inc=1, device_id=device, device_id_type=MESH)

    steps = [(1, 0), (3, 0), (0, 1), (0, 3)]
    barrier = pltpu.get_barrier_semaphore()
    for way in ways:
        signal(barrier, beside(*way))
    for dx, dy in steps:
        signal(barrier, across(dx, dy, 0)[0])
    signal(barrier, z_device((z + 2) % ZLEN))
    signal(barrier, z_device((z + ZLEN - 2) % ZLEN))

    north = jnp.where(lat > 0, 1.0, 0.0)
    south = jnp.where(lat < LATS - 1, 1.0, 0.0)
    inner = slice(REACH, REACH + ROWS)
    middle = slice(WIDE, 2 * WIDE)
    own_copies = [
        pltpu.make_async_copy(feat_any, fw.at[inner, middle], own_sem.at[0]),
        pltpu.make_async_copy(cot_any, cw.at[inner, middle], own_sem.at[1]),
        pltpu.make_async_copy(weight_any, weight_ref, own_sem.at[2]),
        pltpu.make_async_copy(taps_any, taps_ref, own_sem.at[3]),
        pltpu.make_async_copy(lat_any, lat_ref, own_sem.at[4]),
        pltpu.make_async_copy(lon_any, lon_ref, own_sem.at[5]),
    ]
    for copy in own_copies:
        copy.start()
    pl.semaphore_wait(barrier, len(ways) + len(steps) + 2)

    def rows(window, start, left):
        return window.at[pl.ds(start, REACH), left : left + WIDE]

    common, single = REACH * (1 - core), REACH * core
    far = REACH + ROWS

    def halo(source, window, send, recv):
        out, arrive = [], []

        def add(src, start, landing, left, device):
            index = len(out)
            out.append(remote(src, rows(window, start, left), send.at[index], recv.at[index], device))
            place = rows(window, landing, left)
            arrive.append(remote(place, place, send.at[index], recv.at[index], partner))

        for right in (1, -1):
            start = REACH + common
            add(source.at[pl.ds(common, REACH)], start, start, WIDE * (1 - right), beside(0, right))
        for right in (1, -1):
            add(
                source.at[pl.ds(single, REACH)], far * (1 - core), far * core, WIDE * (1 - right),
                beside(away, right),
            )
        for right in (1, -1):
            start = REACH + single
            add(source.at[pl.ds(single, REACH)], start, start, WIDE * (1 - right), beside(0, right))
        add(source.at[ROWS - REACH :], 0, 0, WIDE, beside(1, 0))
        add(source.at[0:REACH], far, far, WIDE, beside(-1, 0))
        for right in (1, -1):
            left = WIDE * (1 - right)
            add(rows(window, REACH + common, left), far * core, far * (1 - core), left, partner)
        return out, arrive

    feat_copies, feat_arrive = halo(feat_any, fw, feat_send, feat_recv)
    cot_copies, cot_arrive = halo(cot_any, cw, cot_send, cot_recv)
    ft_copies = [
        remote(ft.at[ROWS : ROWS + REACH], ft.at[0:REACH], ft_send.at[0], ft_recv.at[0], beside(1, 0)),
        remote(ft.at[REACH : 2 * REACH], ft.at[REACH + ROWS :], ft_send.at[1], ft_recv.at[1], beside(-1, 0)),
    ]
    for copy in feat_copies[:8]:
        copy.start()
    for dx, dy in steps:
        signal(step_sem, across(dx, dy, 0)[0])
    signal(hop_sem, z_device((z + 2) % ZLEN))
    signal(hop_sem, z_device((z + ZLEN - 2) % ZLEN))
    blank = jnp.zeros((SPAN, LANES - 3 * WIDE, CH), BF16)
    fw[:, 3 * WIDE :, :] = blank
    cw[:, 3 * WIDE :, :] = blank
    for copy in own_copies[3:]:
        copy.wait()
    fill_filters(taps_ref, lat_ref, lon_ref, ft)
    pl.semaphore_wait(step_sem, len(steps))
    signal(cross_sem, across(2, 0, 0)[0])
    signal(cross_sem, across(0, 2, 0)[0])
    pl.semaphore_wait(hop_sem, 2)
    signal(leap_sem, z_device((z + 4) % ZLEN))
    signal(leap_sem, z_device((z + ZLEN - 4) % ZLEN))
    fill_forward(ft, north, south, bands)
    wedge[...] = jnp.zeros(wedge.shape, BF16)
    for index in range(2):
        feat_arrive[index].wait_recv()
        feat_copies[8 + index].start()
    pl.semaphore_wait(cross_sem, 2)
    signal(twin_sem, across(0, 0, 1)[0])
    for copy in feat_arrive[2:]:
        copy.wait_recv()
    own_copies[0].wait()
    own_copies[1].wait()
    convolve(bands, fw, bo, (1 - core) * 2)

    cells = cw[inner, middle, :].reshape(ROWS * WIDE, CH)

    def share(basis):
        return lax.dot_general(bo[basis], cells, (((0,), (0,)), ((), ())), preferred_element_type=F32)

    def pair_copy(index):
        span = pl.ds(pl.multiple_of(index * CH, CH), CH)
        return remote(pair_out.at[span], pair_in.at[span], pair_send.at[index], pair_recv.at[index], partner)

    for index in range(2):
        pair_out[index * CH : (index + 1) * CH, :] = share((1 - core) * 2 + index).astype(BF16)
        pair_copy(index).start()
    convolve(bands, fw, bo, core * 2)
    for index in range(2):
        part[index * CH : (index + 1) * CH, :] = share(core * 2 + index)
    per = GROUP // 2
    places = [(dx, dy) for dx in (0, 1, 2, 3) for dy in (0, 1, 2, 3)]
    places.sort(key=lambda p: -(min(p[0], 4 - p[0]) + min(p[1], 4 - p[1])))
    offsets = [(dx, dy, dz) for dx, dy in places for dz in (0, 1)]
    offsets.sort(key=lambda o: -(min(o[0], 4 - o[0]) + min(o[1], 4 - o[1]) + o[2]))

    def group_copy(index, dz):
        device, piece = across(*places[index], dz)
        slot = dz * per + index
        return remote(half.at[piece], group_in.at[slot], many_sem.at[0], group_recv.at[slot], device)

    def group_arrive(slot):
        return remote(
            group_in.at[slot], group_in.at[slot], many_sem.at[0], group_recv.at[slot], partner
        )

    def group_add(slot, carry):
        group_arrive(slot).wait_recv()
        return carry + group_in[slot].astype(F32)

    for index in range(2):
        pair_copy(index).wait_recv()
        span = slice(index * CH, (index + 1) * CH)
        total = part[span, :] + pair_in[span, :].astype(F32)
        half[index * per : (index + 1) * per] = total.astype(BF16).reshape(per, CHUNK, CH)
        if index == 0:
            pl.semaphore_wait(twin_sem, 1)
        turn = (z_lo + index) % 2
        for place in range(per - 1):
            group_copy(place, turn).start()

        @pl.when(turn == 1)
        def _():
            group_copy(per - 1, 1).start()

    for copy in cot_copies[:8] + ft_copies:
        copy.start()
    chunk = lax.fori_loop(0, per - 1, group_add, half[spot].astype(F32))
    chunk = lax.fori_loop(per, GROUP, group_add, chunk)
    zbuf[z_hi] = chunk.astype(BF16)
    pl.semaphore_wait(leap_sem, 2)

    def z_copy(step):
        return remote(
            zbuf.at[z_hi], zbuf.at[z_hi], many_sem.at[1], z_recv.at[z_hi],
            far_device((z_hi + step) % ZFAR),
        )

    def z_wait(step, carry):
        source = (z_hi + step) % ZFAR
        remote(
            zbuf.at[source], zbuf.at[source], many_sem.at[1], z_recv.at[source], far_device(source)
        ).wait_recv()
        return carry

    for step in (4, 3, 5, 2, 6, 1, 7):
        z_copy(step).start()
    own_copies[2].wait()
    mix(bo, weight_ref, out_ref)
    for copy in ft_copies:
        copy.wait_recv()
    for index in range(2):
        cot_arrive[index].wait_recv()
        cot_copies[8 + index].start()
    fill_reversed(ft, north, south, rt)
    fill_adjoint(rt, wedge)
    for copy in cot_arrive[2:]:
        copy.wait_recv()
    fill_basis_grad(cw, weight_ref, bg)
    adjoint(wedge, bg, grad_ref)
    lax.fori_loop(1, ZFAR, z_wait, 0)
    chunk = zbuf[0].astype(F32)
    for source in range(1, ZFAR):
        chunk = chunk + zbuf[source].astype(F32)
    sum_ref[core, spot] = chunk.astype(BF16)

    def all_copy(step):
        return remote(
            sum_ref.at[core, spot], sum_ref.at[core, spot], many_sem.at[2], all_recv.at[step],
            across(*offsets[step])[0],
        )

    def near_copy(index):
        return remote(
            sum_ref.at[core, index], sum_ref.at[core, index], many_sem.at[3], many_sem.at[4], partner
        )

    for step in range(GROUP - 1):
        all_copy(step).start()
    near_copy(spot).start()
    for copy in feat_copies + cot_copies + ft_copies:
        copy.wait_send()
    for index in range(2):
        pair_copy(index).wait_send()
    remote(
        half.at[0 : GROUP - 1], group_in.at[0 : GROUP - 1], many_sem.at[0], group_recv.at[0], partner
    ).wait_send()
    remote(
        zbuf.at[0 : ZFAR - 1], zbuf.at[0 : ZFAR - 1], many_sem.at[1], z_recv.at[0], partner
    ).wait_send()
    for step in range(GROUP - 1):
        dx, dy, dz = offsets[step]
        source = across(4 - dx, 4 - dy, dz)[1]
        remote(
            sum_ref.at[core, source], sum_ref.at[core, source], many_sem.at[2], all_recv.at[step],
            partner,
        ).wait_recv()
        near_copy(source).start()
    remote(
        sum_ref.at[core, 0 : GROUP - 1], sum_ref.at[core, 0 : GROUP - 1], many_sem.at[2],
        all_recv.at[0], partner,
    ).wait_send()
    near_all = remote(
        sum_ref.at[core], sum_ref.at[1 - core], many_sem.at[3], many_sem.at[4], partner
    )
    near_all.wait_send()
    near_all.wait_recv()


def layer(features, cotangent, weight, filter_taps, lat_ext, lon_count):
    dma = pltpu.SemaphoreType.DMA
    vmem = pl.BlockSpec(memory_space=pltpu.VMEM)
    anywhere = pl.BlockSpec(memory_space=pl.ANY)
    return pl.pallas_call(
        layer_kernel,
        out_shape=[
            pltpu.VMEM((ROWS, WIDE, CH), BF16),
            pltpu.VMEM((ROWS, WIDE, CH), BF16),
            pltpu.VMEM((2, GROUP, CHUNK, CH), BF16),
        ],
        in_specs=[anywhere] * 6,
        out_specs=[vmem, vmem, vmem],
        scratch_shapes=[
            pltpu.VMEM((SPAN, LANES, CH), BF16),
            pltpu.VMEM((SPAN, LANES, CH), BF16),
            pltpu.VMEM((BASES, CH, CH), BF16),
            pltpu.VMEM((ROWS, TAPS, BASES, 2 * HALF), BF16),
            pltpu.SMEM((ROWS,), jnp.int32),
            pltpu.SMEM((ROWS,), jnp.int32),
            pltpu.VMEM((SPAN, TAPS, 8, LANES), F32),
            pltpu.VMEM((SPAN, TAPS, 8, LANES), F32),
            pltpu.VMEM((ROWS, BASES * WIDE, TAPS * LANES), BF16),
            pltpu.VMEM((BASES, ROWS * WIDE, CH), BF16),
            pltpu.VMEM((SPAN, BASES * LANES, CH), BF16),
            pltpu.VMEM((ROWS * WIDE, SPAN * BASES * LANES), BF16),
            pltpu.VMEM((2 * CH, CH), F32),
            pltpu.VMEM((2 * CH, CH), BF16),
            pltpu.VMEM((2 * CH, CH), BF16),
            pltpu.VMEM((GROUP, CHUNK, CH), BF16),
            pltpu.VMEM((GROUP, CHUNK, CH), BF16),
            pltpu.VMEM((ZFAR, CHUNK, CH), BF16),
            dma((6,)),
            dma((10,)), dma((10,)), dma((10,)), dma((10,)), dma((2,)), dma((2,)), dma((2,)), dma((2,)),
            dma((GROUP,)), dma((ZFAR,)), dma((GROUP,)), dma((5,)),
            *[pltpu.SemaphoreType.REGULAR] * 5,
        ],
        compiler_params=pltpu.CompilerParams(collective_id=0, has_side_effects=True),
    )(features, cotangent, weight, filter_taps, lat_ext, lon_count)


PIECES = 8


def write_kernel(scale, out_ref, grad_ref, sum_ref, out_any, grad_any, total_any, wide, sem):
    copies = [
        pltpu.make_async_copy(out_ref, out_any, sem.at[PIECES]),
        pltpu.make_async_copy(grad_ref, grad_any, sem.at[PIECES + 1]),
    ]
    for copy in copies:
        copy.start()
    per = 2 * GROUP // PIECES
    for index in range(PIECES):
        side, first = (index * per) // GROUP, (index * per) % GROUP
        wide[side, first : first + per] = sum_ref[side, first : first + per].astype(F32) * scale
        copy = pltpu.make_async_copy(
            wide.at[side, first : first + per], total_any.at[side, first : first + per], sem.at[index]
        )
        copy.start()
        copies.append(copy)
    for copy in copies:
        copy.wait()


def write(scale, output, grad, total):
    vmem = pl.BlockSpec(memory_space=pltpu.VMEM)
    anywhere = pl.BlockSpec(memory_space=pl.ANY)
    return pl.pallas_call(
        lambda *refs: write_kernel(scale, *refs),
        out_shape=[
            jax.ShapeDtypeStruct(output.shape, BF16),
            jax.ShapeDtypeStruct(grad.shape, BF16),
            jax.ShapeDtypeStruct(total.shape, F32),
        ],
        in_specs=[vmem, vmem, vmem],
        out_specs=[anywhere, anywhere, anywhere],
        scratch_shapes=[pltpu.VMEM(total.shape, F32), pltpu.SemaphoreType.DMA((PIECES + 2,))],
        name="write",
    )(*(pltpu.with_memory_space_constraint(held, pltpu.VMEM) for held in (output, grad, total)))


def per_device(features, cotangent, weight, filter_taps, lat_ext, lon_count):
    taps = jnp.transpose(filter_taps, (0, 2, 1, 3))
    output, field_grad, total = layer(features, cotangent, weight, taps, lat_ext, lon_count)
    cells = LATS * ROWS * LONS * WIDE
    output, field_grad, total = write(1.0 / math.sqrt(cells), output, field_grad, total)
    return (output, field_grad, total.reshape(BASES, CH, CH))


def solution(mesh):
    in_specs = (
        P("lat", "lon", None),
        P("lat", "lon", None),
        P(),
        P("lat", None, None, None),
        P("lat"),
        P("lat"),
    )
    out_specs = (P("lat", "lon", None), P("lat", "lon", None), P())
    return jax.shard_map(
        per_device, mesh=mesh, in_specs=in_specs, out_specs=out_specs, check_vma=False
    )
```
